128 devices in a mesh: seq: 16 (over z_lo, x, core), fsdp: 8 (over z_hi, y).
Axes of the slice: x: 4, y: 4, z: 4 (z_hi: 2, z_lo: 2; z = z_hi * 2 + z_lo), core: 2. Of those that a mesh axis runs over, the one named last changes fastest.
Arguments:
- real_tokens: bfloat16 [8, 1024, 3072], P('fsdp', 'seq'), may hold values from -6 to 6
- gen_hidden: bfloat16 [8, 1024, 3072], P('fsdp', 'seq'), may hold values from -6 to 6
- modulation: float32 [8, 2, 3072], P('fsdp'), may hold values from -3 to 3
- norm_gain: float32 [3072], replicated, may hold values from 0.5 to 1.5
- proj_weight: bfloat16 [3, 3072, 2048], P(None, None, 'fsdp'), may hold values from -4 to 4
Outputs:
- grad_hidden: bfloat16 [8, 1024, 3072], P('fsdp', 'seq')
The draws below stay inside these ranges and needn't reach their ends.
All inputs are finite; a program needn't handle non-finite values.
Results may differ from the reference program's by a relative error of at most 0.012.
The reference program's roundings to bfloat16 on the way (of `fake_tokens`, `normed` and `grad_out`) count: a program that leaves them out, or rounds other values in their place, can miss the bound.
Values may be sent and summed in bfloat16 or wider, within the bound.
No kernel may reach another device: no remote copies, remote signals or barrier semaphores. Data moves between devices by JAX's collectives and lax.ppermute only.
A program may use at most 128 MiB of HBM per device.

```python
import jax
import jax.numpy as jnp
from jax import lax

D = 3072
HEADS = 16
HEAD_DIM = 128
LENGTH = 1024
BATCH = 8


def draw_proj_weight(key, part):
    columns = HEADS * HEAD_DIM
    drawn = jax.random.normal(jax.random.fold_in(key, 11), (3, D, columns), jnp.float32) * D ** (-0.5)
    return jnp.clip(drawn, -4.0, 4.0).astype(jnp.bfloat16)


def levels(stream_key, dims, split, smallest, largest):
    loudness = 1.0
    for dim, blocks in split:
        heights = jax.random.uniform(jax.random.fold_in(jax.random.fold_in(stream_key, 6), dim), (blocks,), jnp.float32, smallest / len(split), largest / len(split))
        loudness = loudness * jnp.repeat(jnp.exp(heights), dims[dim] // blocks).reshape((-1,) + (1,) * (len(dims) - 1 - dim))
    return loudness


def bell_draw(key, extent, deviation, bound, cuts=(), kind=jnp.bfloat16):
    result = jax.random.normal(key, extent, jnp.float32) * deviation
    if len(cuts) > 0:
        result = levels(key, extent, cuts, -0.22, 0.18) * result
    return jnp.clip(result, min=-bound, max=bound).astype(kind)


def setup_inputs(seed: int = 0) -> dict:
    arg_keys = jax.random.split(jax.random.key(seed), 6)
    real_tokens = bell_draw(arg_keys[0], (BATCH, LENGTH, D), 1.0, 6.0, ((0, 8), (1, 16)))
    gen_hidden = bell_draw(arg_keys[1], (BATCH, LENGTH, D), 1.0, 6.0, ((0, 8), (1, 16)))
    modulation = bell_draw(arg_keys[2], (BATCH, 2, D), 0.5, 3.0, ((0, 8),), jnp.float32)
    norm_gain = jnp.clip(1.0 + 0.1 * jax.random.normal(arg_keys[3], (D,), jnp.float32), 0.5, 1.5)
    proj_weight = draw_proj_weight(jax.random.fold_in(arg_keys[5], 71), 0)
    return dict(real_tokens=real_tokens, gen_hidden=gen_hidden, modulation=modulation, norm_gain=norm_gain, proj_weight=proj_weight)


norm_eps = 1e-06
match_eps = 0.05
loss_weight = 4.0

def to_wide(values):
    return lax.optimization_barrier(values).astype(jnp.float32)

def normalize(tokens, norm_gain):
    values = to_wide(tokens)
    inverse = lax.rsqrt(lax.optimization_barrier(jnp.mean(values * values, axis=-1, keepdims=True)) + norm_eps)
    return ((values * inverse * norm_gain).astype(jnp.bfloat16), inverse)

def attend(queries, key_rows, value_rows):
    scores = jnp.einsum('qhd,khd->hqk', to_wide(queries), to_wide(key_rows)) * HEAD_DIM ** (-0.5)
    highest = lax.optimization_barrier(jnp.max(scores, axis=-1, keepdims=True))
    weights = jnp.exp(scores - highest)
    totals = lax.optimization_barrier(jnp.sum(weights, axis=-1, keepdims=True))
    mixed_values = jnp.einsum('hqk,khd->qhd', to_wide(weights.astype(jnp.bfloat16)), to_wide(value_rows))
    outputs = mixed_values / jnp.transpose(totals, (1, 0, 2))
    return (outputs, highest + jnp.log(totals))

def match_grad(fake_out, real_out):
    differ = fake_out - real_out
    return (loss_weight * differ / jnp.sqrt(differ * differ + match_eps * match_eps)).astype(jnp.bfloat16)

def row_delta(grad_out, fake_out):
    return lax.optimization_barrier(jnp.sum(to_wide(grad_out) * fake_out, axis=-1))

def backward_scores(queries, key_rows, value_rows, log_total, deltas, grad_out):
    scores = jnp.einsum('qhd,khd->hqk', to_wide(queries), to_wide(key_rows)) * HEAD_DIM ** (-0.5)
    probs = jnp.exp(scores - log_total)
    dprobs = jnp.einsum('qhd,khd->hqk', to_wide(grad_out), to_wide(value_rows))
    dscores = (probs * (dprobs - jnp.transpose(deltas)[:, :, None]) * HEAD_DIM ** (-0.5)).astype(jnp.bfloat16)
    return (probs.astype(jnp.bfloat16), dscores)

def one_sequence(real_row, hidden_row, modulation_row, norm_gain, proj_weight):
    seq_rows = real_row.shape[0]
    weight_wide = proj_weight.astype(jnp.float32)
    fake_tokens = (hidden_row.astype(jnp.float32) * (1.0 + modulation_row[0]) + modulation_row[1]).astype(jnp.bfloat16)
    real_normed, real_inverse = normalize(real_row, norm_gain)
    fake_normed, fake_inverse = normalize(fake_tokens, norm_gain)

    def project(normed):
        mapped = jnp.einsum('td,kdc->ktc', to_wide(normed), weight_wide).astype(jnp.bfloat16)
        return mapped.reshape(3, seq_rows, HEADS, HEAD_DIM)
    real_map = project(real_normed)
    fake_map = project(fake_normed)
    real_out, real_total = attend(real_map[0], real_map[1], real_map[2])
    fake_out, fake_total = attend(fake_map[0], fake_map[1], fake_map[2])
    grad_out = match_grad(fake_out, real_out)
    deltas = row_delta(grad_out, fake_out)
    prob_low, dscores = backward_scores(fake_map[0], fake_map[1], fake_map[2], fake_total, deltas, grad_out)
    grad_query = jnp.einsum('hqk,khd->qhd', to_wide(dscores), to_wide(fake_map[1]))
    grad_key = jnp.einsum('hqk,qhd->khd', to_wide(dscores), to_wide(fake_map[0]))
    grad_value = jnp.einsum('hqk,qhd->khd', to_wide(prob_low), to_wide(grad_out))
    all_grads = jnp.stack([grad_query, grad_key, grad_value]).astype(jnp.bfloat16)
    all_grads = all_grads.reshape(3, seq_rows, HEADS * HEAD_DIM)
    grad_normed = jnp.einsum('ktc,kdc->td', to_wide(all_grads), weight_wide)
    scaled = to_wide(fake_tokens) * fake_inverse
    grad_scaled = grad_normed * norm_gain
    grad_fake = fake_inverse * (grad_scaled - scaled * lax.optimization_barrier(jnp.mean(grad_scaled * scaled, axis=-1, keepdims=True)))
    return (grad_fake * (1.0 + modulation_row[0])).astype(jnp.bfloat16)

def reference(real_tokens, gen_hidden, modulation, norm_gain, proj_weight):

    def per_sequence(packed):
        return one_sequence(packed[0], packed[1], packed[2], norm_gain, proj_weight)
    return lax.map(per_sequence, (real_tokens, gen_hidden, modulation))
```

```python
import jax
import jax.numpy as jnp
from jax import lax
from jax.experimental import pallas as pl
from jax.experimental.pallas import tpu as pltpu
from jax.sharding import Mesh
from jax.sharding import PartitionSpec as P

HEADS = 16
HEAD_DIM = 128
WIDTH = 3072
BLOCK = 64
PIECE = WIDTH // 8

norm_eps = 1e-06
match_eps = 0.05
loss_weight = 4.0


SEQ = ("zl", "x", "core")
ACROSS = [(0, 3), (3, 0), (1, 2), (2, 1)]


def ring(step):
    return [(i, (i + step) % 4) for i in range(4)]


def swap():
    return [(0, 1), (1, 0)]


def normalize(tokens, norm_gain):
    values = tokens.astype(jnp.float32)
    inverse = lax.rsqrt(jnp.mean(values * values, axis=-1, keepdims=True) + norm_eps)
    return (values * inverse * norm_gain).astype(jnp.bfloat16), inverse


def attention_kernel(x_ref, o_ref, dk_ref, dv_ref):
    bf = jnp.bfloat16
    f32 = jnp.float32
    length = 16 * BLOCK
    tile = 256
    per = tile // BLOCK
    scale = HEAD_DIM ** (-0.5)
    to_two = scale * 1.4426950408889634

    def whole(stream, part):
        return x_ref[:, stream, part].reshape(length, HEAD_DIM)

    def dot(a, b):
        return jnp.dot(a, b, preferred_element_type=f32)

    keys = [whole(s, 1) for s in range(2)]
    values = [whole(s, 2) for s in range(2)]
    values_t = [v.T for v in values]
    fake_key_t = keys[1].T

    for i in range(length // tile):
        blocks = slice(per * i, per * (i + 1))

        def mix(stream):
            query = x_ref[blocks, stream, 0].reshape(tile, HEAD_DIM)
            scores = dot(keys[stream], query.T)
            highest = jnp.max(scores, axis=0, keepdims=True)
            weights = jnp.exp2((scores - highest) * to_two)
            total = jnp.sum(weights, axis=0, keepdims=True)
            mixed = dot(values_t[stream], weights.astype(bf)) / total
            return mixed, weights, total, query

        real_out = mix(0)[0]
        fake_out, weights, total, query = mix(1)
        differ = fake_out - real_out
        grad_out_t = (loss_weight * differ * lax.rsqrt(differ * differ + match_eps * match_eps)).astype(bf)
        grad_out = grad_out_t.T
        deltas = jnp.sum(grad_out_t.astype(f32) * fake_out, axis=0, keepdims=True)
        probs = weights * (1.0 / total)
        dprobs = dot(values[1], grad_out_t)
        dscores = (probs * (dprobs - deltas) * scale).astype(bf)
        prob_low = probs.astype(bf)
        dq = dot(fake_key_t, dscores).astype(bf).T
        o_ref[blocks, 0] = dq.reshape(per, BLOCK, HEAD_DIM)
        dk = dot(dscores, query)
        dv = dot(prob_low, grad_out)
        if i == 0:
            dk_ref[...] = dk
            dv_ref[...] = dv
        else:
            dk_ref[...] += dk
            dv_ref[...] += dv
    o_ref[:, 1] = dk_ref[...].astype(bf).reshape(16, BLOCK, HEAD_DIM)
    o_ref[:, 2] = dv_ref[...].astype(bf).reshape(16, BLOCK, HEAD_DIM)


def attention(received):
    vmem = pl.BlockSpec(memory_space=pltpu.VMEM)
    return pl.pallas_call(
        attention_kernel,
        out_shape=jax.ShapeDtypeStruct((16, 3, BLOCK, HEAD_DIM), jnp.bfloat16),
        in_specs=[vmem],
        out_specs=vmem,
        scratch_shapes=[pltpu.VMEM((16 * BLOCK, HEAD_DIM), jnp.float32)] * 2,
        compiler_params=pltpu.CompilerParams(vmem_limit_bytes=40 * 1024 * 1024),
        name="attention",
    )(received)


def fetch_weights(weight):
    colour = (lax.axis_index("x") + 2 * lax.axis_index("zl")) % 4
    core = lax.axis_index("core")

    def start_of(c, k):
        return ((c % 4) * 2 + k) * PIECE

    sent = lax.dynamic_slice(weight, (0, start_of(colour + 2, core), 0), (3, PIECE, weight.shape[2]))
    mine = lax.ppermute(sent, ("zl", "zh"), ACROSS)
    pieces = [
        (colour, mine),
        (colour + 3, lax.ppermute(mine, "x", ring(1))),
        (colour + 1, lax.ppermute(mine, "x", ring(-1))),
        (colour + 2, lax.ppermute(mine, "zl", swap())),
    ]
    whole = jnp.zeros_like(weight)
    for c, piece in pieces:
        whole = lax.dynamic_update_slice(whole, piece, (0, start_of(c, core), 0))
        other = lax.ppermute(piece, "core", swap())
        whole = lax.dynamic_update_slice(whole, other, (0, start_of(c, 1 - core), 0))
    return whole


def on_device(real_tokens, gen_hidden, modulation, norm_gain, weight):
    bf = jnp.bfloat16
    f32 = jnp.float32
    other_weight = fetch_weights(weight)
    fake_tokens = (gen_hidden[0].astype(f32) * (1.0 + modulation[0, 0]) + modulation[0, 1]).astype(bf)
    real_normed, _ = normalize(real_tokens[0], norm_gain)
    fake_tokens = lax.optimization_barrier(fake_tokens)
    fake_normed, fake_inverse = normalize(fake_tokens, norm_gain)
    both = jnp.stack([real_normed, fake_normed])
    below = lax.ppermute(both, "y", ring(1))
    above = lax.ppermute(both, "y", ring(-1))
    far = jnp.stack([lax.ppermute(below[0], "y", ring(1)), lax.ppermute(above[1], "y", ring(-1))])
    slots = [both, below, above, far]

    def project(rows, columns):
        out = jnp.einsum("srd,qdc->srqc", rows, columns, preferred_element_type=f32).astype(bf)
        out = out.reshape(2, BLOCK, 3, 2, HEAD_DIM)
        return jnp.transpose(out, (3, 0, 2, 1, 4))

    sends = []
    for rows in slots:
        sends.append(project(rows, weight))
        sends.append(project(rows, other_weight))
    send = jnp.concatenate(sends, axis=0).reshape(16, 6 * BLOCK, HEAD_DIM)
    received = lax.all_to_all(send, SEQ, split_axis=0, concat_axis=0, tiled=True)
    grads = attention(received.reshape(16, 2, 3, BLOCK, HEAD_DIM))
    back = lax.all_to_all(grads.reshape(16, 3 * BLOCK, HEAD_DIM), SEQ, split_axis=0, concat_axis=0, tiled=True)
    back = back.reshape(4, 2, 2, 3, BLOCK, HEAD_DIM)

    def partial(j):
        total = 0.0
        for p, columns in enumerate((weight, other_weight)):
            block = jnp.transpose(back[j, p], (1, 2, 0, 3)).reshape(3, BLOCK, 2 * HEAD_DIM)
            total = total + jnp.einsum("qrc,qdc->rd", block, columns, preferred_element_type=f32)
        return total

    from_far = lax.ppermute(partial(3).astype(bf), "y", ring(2))
    from_above = lax.ppermute(partial(1).astype(bf), "y", ring(-1))
    from_below = lax.ppermute(partial(2).astype(bf), "y", ring(1))
    grad_normed = partial(0) + from_far.astype(f32) + from_above.astype(f32) + from_below.astype(f32)
    scaled = fake_tokens.astype(f32) * fake_inverse
    grad_scaled = grad_normed * norm_gain
    grad_fake = fake_inverse * (grad_scaled - scaled * jnp.mean(grad_scaled * scaled, axis=-1, keepdims=True))
    grad_hidden = (grad_fake * (1.0 + modulation[0, 0])).astype(bf)
    return grad_hidden[None]


def solution(mesh):
    torus = Mesh(mesh.devices.reshape(2, 4, 2, 2, 4), ("zl", "x", "core", "zh", "y"))
    fsdp = ("zh", "y")
    in_specs = (
        P(fsdp, SEQ, None),
        P(fsdp, SEQ, None),
        P(fsdp, None, None),
        P(),
        P(None, None, fsdp),
    )
    return jax.shard_map(on_device, mesh=torus, in_specs=in_specs, out_specs=P(fsdp, SEQ, None), check_vma=False)
```

```python
import jax
import jax.numpy as jnp
from jax import lax
from jax.experimental import pallas as pl
from jax.experimental.pallas import tpu as pltpu
from jax.sharding import Mesh
from jax.sharding import PartitionSpec as P

HEADS = 16
HEAD_DIM = 128
WIDTH = 3072
BLOCK = 64
PIECE = WIDTH // 8

norm_eps = 1e-06
match_eps = 0.05
loss_weight = 4.0


SEQ = ("zl", "x", "core")
ACROSS = [(0, 3), (3, 0), (1, 2), (2, 1)]


VMEM = pl.BlockSpec(memory_space=pltpu.VMEM)


def cost(flops, touched):
    return pl.CostEstimate(flops=flops, bytes_accessed=touched, transcendentals=0)


def limit(mib=40):
    return pltpu.CompilerParams(vmem_limit_bytes=mib * 1024 * 1024)


def ring(step):
    return [(i, (i + step) % 4) for i in range(4)]


def swap():
    return [(0, 1), (1, 0)]


def attention_kernel(x_ref, o_ref, dk_ref, dv_ref):
    bf = jnp.bfloat16
    f32 = jnp.float32
    length = 16 * BLOCK
    tile = 256
    per = tile // BLOCK
    scale = HEAD_DIM ** (-0.5)
    to_two = scale * 1.4426950408889634

    def whole(stream, part):
        return x_ref[:, stream, part].reshape(length, HEAD_DIM)

    def dot(a, b):
        return jnp.dot(a, b, preferred_element_type=f32)

    keys = [whole(s, 1) for s in range(2)]
    values = [whole(s, 2) for s in range(2)]
    values_t = [v.T for v in values]
    fake_key_t = keys[1].T

    for i in range(length // tile):
        blocks = slice(per * i, per * (i + 1))

        def mix(stream):
            query = x_ref[blocks, stream, 0].reshape(tile, HEAD_DIM)
            scores = dot(keys[stream], query.T)
            highest = jnp.max(scores, axis=0, keepdims=True)
            weights = jnp.exp2((scores - highest) * to_two)
            total = jnp.sum(weights, axis=0, keepdims=True)
            mixed = dot(values_t[stream], weights.astype(bf)) / total
            return mixed, weights, total, query

        real_out = mix(0)[0]
        fake_out, weights, total, query = mix(1)
        differ = fake_out - real_out
        grad_out_t = (loss_weight * differ * lax.rsqrt(differ * differ + match_eps * match_eps)).astype(bf)
        grad_out = grad_out_t.T
        deltas = jnp.sum(grad_out_t.astype(f32) * fake_out, axis=0, keepdims=True)
        probs = weights * (1.0 / total)
        dprobs = dot(values[1], grad_out_t)
        dscores = (probs * (dprobs - deltas) * scale).astype(bf)
        prob_low = probs.astype(bf)
        dq = dot(fake_key_t, dscores).astype(bf).T
        o_ref[blocks, 0] = dq.reshape(per, BLOCK, HEAD_DIM)
        dk = dot(dscores, query)
        dv = dot(prob_low, grad_out)
        if i == 0:
            dk_ref[...] = dk
            dv_ref[...] = dv
        else:
            dk_ref[...] += dk
            dv_ref[...] += dv
    o_ref[:, 1] = dk_ref[...].astype(bf).reshape(16, BLOCK, HEAD_DIM)
    o_ref[:, 2] = dv_ref[...].astype(bf).reshape(16, BLOCK, HEAD_DIM)


def attention(received):
    return pl.pallas_call(
        attention_kernel,
        out_shape=jax.ShapeDtypeStruct((16, 3, BLOCK, HEAD_DIM), jnp.bfloat16),
        in_specs=[VMEM],
        out_specs=VMEM,
        scratch_shapes=[pltpu.VMEM((16 * BLOCK, HEAD_DIM), jnp.float32)] * 2,
        cost_estimate=cost(11 * 1024 * 1024 * 256, 4 << 20),
        compiler_params=limit(),
        name="attention",
    )(received)


def pick_kernel(index_ref, w_ref, o_ref):
    o_ref[...] = w_ref[...]


def pick(weight, index):
    return pl.pallas_call(
        pick_kernel,
        out_shape=jax.ShapeDtypeStruct((3, PIECE, 2 * HEAD_DIM), jnp.bfloat16),
        grid_spec=pltpu.PrefetchScalarGridSpec(
            num_scalar_prefetch=1,
            grid=(3,),
            in_specs=[pl.BlockSpec((1, PIECE, 2 * HEAD_DIM), lambda q, i: (q, i[0], 0))],
            out_specs=pl.BlockSpec((1, PIECE, 2 * HEAD_DIM), lambda q, i: (q, 0, 0)),
        ),
        cost_estimate=cost(0, 1 << 20),
        name="pick",
    )(index, weight)


def prepare_kernel(real_ref, gen_ref, mod_ref, gain_ref, o_ref):
    f32, bf = jnp.float32, jnp.bfloat16
    gain = gain_ref[...]
    scale = 1.0 + mod_ref[0:1]
    shift = mod_ref[1:2]
    for r in range(0, BLOCK, 16):
        rows = slice(r, r + 16)
        fake = (gen_ref[rows].astype(f32) * scale + shift).astype(bf).astype(f32)
        for stream, values in ((0, real_ref[rows].astype(f32)), (1, fake)):
            inverse = lax.rsqrt(jnp.mean(values * values, axis=-1, keepdims=True) + norm_eps)
            o_ref[stream, rows] = (values * inverse * gain).astype(bf)


def prepare(real, gen, modulation, gain):
    return pl.pallas_call(
        prepare_kernel,
        out_shape=jax.ShapeDtypeStruct((2, BLOCK, WIDTH), jnp.bfloat16),
        in_specs=[VMEM] * 4,
        out_specs=VMEM,
        cost_estimate=cost(4 << 20, 2 << 20),
        compiler_params=limit(),
        name="prepare",
    )(real, gen, modulation, gain)


def gather_rows(step, own_ref, below_ref, above_ref, far0_ref, far1_ref, rows_ref):
    @pl.when(step == 0)
    def _():
        for j, ref in enumerate((own_ref, below_ref, above_ref)):
            rows_ref[128 * j : 128 * (j + 1)] = ref[...].reshape(128, WIDTH)
        rows_ref[384:448] = far0_ref[...]
        rows_ref[448:512] = far1_ref[...]


def store_heads(out, o_ref):
    for k in range(2):
        for j in range(4):
            for s in range(2):
                r = (2 * j + s) * BLOCK
                o_ref[4 * k + j, s, 0] = out[r : r + BLOCK, HEAD_DIM * k : HEAD_DIM * (k + 1)]


def project_own_kernel(own_ref, below_ref, above_ref, far0_ref, far1_ref, w_ref, o_ref, rows_ref):
    gather_rows(pl.program_id(0), own_ref, below_ref, above_ref, far0_ref, far1_ref, rows_ref)
    out = jnp.dot(rows_ref[...], w_ref[0], preferred_element_type=jnp.float32).astype(jnp.bfloat16)
    store_heads(out, o_ref)


def project_other_kernel(
    place_ref, own_ref, below_ref, above_ref, far0_ref, far1_ref, held_ref, *refs
):
    pieces, (o_ref, w_ref, rows_ref) = refs[:8], refs[8:]
    gather_rows(pl.program_id(0), own_ref, below_ref, above_ref, far0_ref, far1_ref, rows_ref)
    for i, piece in enumerate(pieces):
        w_ref[0, pl.ds(pl.multiple_of(place_ref[i], PIECE), PIECE)] = piece[0]
    out = jnp.dot(rows_ref[...], w_ref[0], preferred_element_type=jnp.float32).astype(jnp.bfloat16)
    store_heads(out, o_ref)


SEND = (16, 2, 3, BLOCK, HEAD_DIM)
HALF = (8, 2, 1, BLOCK, HEAD_DIM)
ROWS = pltpu.VMEM((8 * BLOCK, WIDTH), jnp.bfloat16)


def row_specs(whole):
    return [
        pl.BlockSpec((2, BLOCK, WIDTH), whole(3)),
        pl.BlockSpec((2, BLOCK, WIDTH), whole(3)),
        pl.BlockSpec((2, BLOCK, WIDTH), whole(3)),
        pl.BlockSpec((BLOCK, WIDTH), whole(2)),
        pl.BlockSpec((BLOCK, WIDTH), whole(2)),
    ]


def project_own(slots, weight):
    return pl.pallas_call(
        project_own_kernel,
        out_shape=jax.ShapeDtypeStruct(SEND, jnp.bfloat16),
        grid=(3,),
        in_specs=row_specs(lambda n: lambda q: (0,) * n)
        + [pl.BlockSpec((1, WIDTH, 2 * HEAD_DIM), lambda q: (q, 0, 0))],
        out_specs=pl.BlockSpec(HALF, lambda q: (0, 0, q, 0, 0)),
        scratch_shapes=[ROWS],
        cost_estimate=cost(2 * 512 * 3072 * 768, 9 << 20),
        compiler_params=limit(),
        name="project_own",
    )(*slots, weight)


def project_other(slots, held, pieces, places):
    piece_spec = pl.BlockSpec((1, PIECE, 2 * HEAD_DIM), lambda q, i: (q, 0, 0))
    return pl.pallas_call(
        project_other_kernel,
        out_shape=[
            jax.ShapeDtypeStruct(SEND, jnp.bfloat16),
            jax.ShapeDtypeStruct((3, WIDTH, 2 * HEAD_DIM), jnp.bfloat16),
        ],
        grid_spec=pltpu.PrefetchScalarGridSpec(
            num_scalar_prefetch=1,
            grid=(3,),
            in_specs=row_specs(lambda n: lambda q, i: (0,) * n)
            + [pl.BlockSpec(memory_space=pl.ANY)]
            + [piece_spec] * 8,
            out_specs=[
                pl.BlockSpec(HALF, lambda q, i: (1, 0, q, 0, 0)),
                pl.BlockSpec((1, WIDTH, 2 * HEAD_DIM), lambda q, i: (q, 0, 0)),
            ],
            scratch_shapes=[ROWS],
        ),
        input_output_aliases={6: 0},
        cost_estimate=cost(2 * 512 * 3072 * 768, 12 << 20),
        compiler_params=limit(),
        name="project_other",
    )(places, *slots, held, *pieces)


CHUNK = 768


def unproject_kernel(back_ref, own_ref, other_ref, o0_ref, o1_ref, o2_ref, o3_ref, grads_ref):
    bf, f32 = jnp.bfloat16, jnp.float32

    @pl.when(pl.program_id(0) == 0)
    def _():
        for p in range(2):
            for q in range(3):
                for k in range(2):
                    d = 4 * (2 * p + k)
                    c = ((3 * p + q) * 2 + k) * HEAD_DIM
                    grads_ref[:, c : c + HEAD_DIM] = back_ref[d : d + 4, q].reshape(4 * BLOCK, HEAD_DIM)

    total = None
    for p, ref in enumerate((own_ref, other_ref)):
        for q in range(3):
            c = (3 * p + q) * 2 * HEAD_DIM
            term = lax.dot_general(
                grads_ref[:, c : c + 2 * HEAD_DIM], ref[q], (((1,), (1,)), ((), ())), preferred_element_type=f32
            )
            total = term if total is None else total + term
    o0_ref[...] = total[:BLOCK]
    for j, ref in ((1, o1_ref), (2, o2_ref), (3, o3_ref)):
        ref[...] = total[BLOCK * j : BLOCK * (j + 1)].astype(bf)


def unproject(back, weight, other):
    w_spec = pl.BlockSpec((3, CHUNK, 2 * HEAD_DIM), lambda n: (0, n, 0))
    o_spec = pl.BlockSpec((BLOCK, CHUNK), lambda n: (0, n))
    return pl.pallas_call(
        unproject_kernel,
        out_shape=[jax.ShapeDtypeStruct((BLOCK, WIDTH), jnp.float32)]
        + [jax.ShapeDtypeStruct((BLOCK, WIDTH), jnp.bfloat16)] * 3,
        grid=(WIDTH // CHUNK,),
        in_specs=[pl.BlockSpec((16, 3, BLOCK, HEAD_DIM), lambda n: (0, 0, 0, 0)), w_spec, w_spec],
        out_specs=[o_spec] * 4,
        scratch_shapes=[pltpu.VMEM((4 * BLOCK, 12 * HEAD_DIM), jnp.bfloat16)],
        cost_estimate=cost(2 * 256 * 3072 * 1536, 12 << 20),
        compiler_params=limit(),
        name="unproject",
    )(back, weight, other)


def finish_kernel(own_ref, a_ref, b_ref, c_ref, gen_ref, mod_ref, gain_ref, o_ref):
    f32, bf = jnp.float32, jnp.bfloat16
    gain = gain_ref[...]
    scale = 1.0 + mod_ref[0:1]
    shift = mod_ref[1:2]
    for r in range(0, BLOCK, 16):
        rows = slice(r, r + 16)
        fake = (gen_ref[rows].astype(f32) * scale + shift).astype(bf).astype(f32)
        inverse = lax.rsqrt(jnp.mean(fake * fake, axis=-1, keepdims=True) + norm_eps)
        scaled = fake * inverse
        grad = own_ref[rows] + a_ref[rows].astype(f32) + b_ref[rows].astype(f32) + c_ref[rows].astype(f32)
        grad = grad * gain
        grad = inverse * (grad - scaled * jnp.mean(grad * scaled, axis=-1, keepdims=True))
        o_ref[rows] = (grad * scale).astype(bf)


def finish(own, a, b, c, gen, modulation, gain):
    return pl.pallas_call(
        finish_kernel,
        out_shape=jax.ShapeDtypeStruct((BLOCK, WIDTH), jnp.bfloat16),
        in_specs=[VMEM] * 7,
        out_specs=VMEM,
        cost_estimate=cost(4 << 20, 3 << 20),
        compiler_params=limit(),
        name="finish",
    )(own, a, b, c, gen, modulation, gain)


def on_device(real_tokens, gen_hidden, modulation, norm_gain, weight):
    colour = (lax.axis_index("x") + 2 * lax.axis_index("zl")) % 4
    core = lax.axis_index("core")

    sent = pick(weight, (((colour + 2) % 4) * 2 + core).astype(jnp.int32)[None])
    mine = lax.ppermute(sent, ("zl", "zh"), ACROSS)
    gain = norm_gain[None]
    both = prepare(real_tokens[0], gen_hidden[0], modulation[0], gain)
    below = lax.ppermute(both, "y", ring(1))
    above = lax.ppermute(both, "y", ring(-1))
    pieces = [
        mine,
        lax.ppermute(mine, "x", ring(1)),
        lax.ppermute(mine, "x", ring(-1)),
        lax.ppermute(mine, "zl", swap()),
    ]
    pieces = pieces + [lax.ppermute(p, "core", swap()) for p in pieces]
    places = jnp.stack(
        [(((colour + c) % 4) * 2 + k) * PIECE for k in (core, 1 - core) for c in (0, 3, 1, 2)]
    ).astype(jnp.int32)
    far = [lax.ppermute(below[0], "y", ring(1)), lax.ppermute(above[1], "y", ring(-1))]
    slots = [both, below, above, *far]

    held = project_own(slots, weight)
    send, other = project_other(slots, held, pieces, places)
    received = lax.all_to_all(send.reshape(16, 6 * BLOCK, HEAD_DIM), SEQ, split_axis=0, concat_axis=0, tiled=True)
    grads = attention(received.reshape(SEND))
    back = lax.all_to_all(grads.reshape(16, 3 * BLOCK, HEAD_DIM), SEQ, split_axis=0, concat_axis=0, tiled=True)
    part = unproject(back.reshape(16, 3, BLOCK, HEAD_DIM), weight, other)
    from_far = lax.ppermute(part[3], "y", ring(2))
    from_above = lax.ppermute(part[1], "y", ring(-1))
    from_below = lax.ppermute(part[2], "y", ring(1))
    out = finish(part[0], from_far, from_above, from_below, gen_hidden[0], modulation[0], gain)
    return out[None]


def solution(mesh):
    torus = Mesh(mesh.devices.reshape(2, 4, 2, 2, 4), ("zl", "x", "core", "zh", "y"))
    fsdp = ("zh", "y")
    in_specs = (
        P(fsdp, SEQ, None),
        P(fsdp, SEQ, None),
        P(fsdp, None, None),
        P(),
        P(None, None, fsdp),
    )
    return jax.shard_map(on_device, mesh=torus, in_specs=in_specs, out_specs=P(fsdp, SEQ, None), check_vma=False)
```

```python
import jax
import jax.numpy as jnp
from jax import lax
from jax.experimental import pallas as pl
from jax.experimental.pallas import tpu as pltpu
from jax.sharding import Mesh
from jax.sharding import PartitionSpec as P


HEAD_DIM = 128
WIDTH = 3072
BLOCK = 64
PIECE = WIDTH // 8

norm_eps = 1e-06
match_eps = 0.05
loss_weight = 4.0


SEQ = ("zl", "x", "core")
ACROSS = [(0, 3), (3, 0), (1, 2), (2, 1)]


VMEM = pl.BlockSpec(memory_space=pltpu.VMEM)


def cost(flops, touched):
    return pl.CostEstimate(flops=flops, bytes_accessed=touched, transcendentals=0)


def limit(mib=40):
    return pltpu.CompilerParams(vmem_limit_bytes=mib * 1024 * 1024)


def ring(step):
    return [(i, (i + step) % 4) for i in range(4)]


def swap():
    return [(0, 1), (1, 0)]


def attention_kernel(x_ref, o_ref, dk_ref, dv_ref):
    bf = jnp.bfloat16
    f32 = jnp.float32
    length = 16 * BLOCK
    tile = 256
    per = tile // BLOCK
    scale = HEAD_DIM ** (-0.5)
    to_two = scale * 1.4426950408889634

    def whole(stream, part):
        return x_ref[:, stream, part].reshape(length, HEAD_DIM)

    def dot(a, b):
        return jnp.dot(a, b, preferred_element_type=f32)

    keys = [whole(s, 1) for s in range(2)]
    values = [whole(s, 2) for s in range(2)]
    values_t = [v.T for v in values]
    fake_key_t = keys[1].T

    for i in range(length // tile):
        blocks = slice(per * i, per * (i + 1))

        def mix(stream):
            query = x_ref[blocks, stream, 0].reshape(tile, HEAD_DIM)
            scores = dot(keys[stream], query.T)
            highest = jnp.max(scores, axis=0, keepdims=True)
            weights = jnp.exp2((scores - highest) * to_two)
            total = jnp.sum(weights, axis=0, keepdims=True)
            mixed = dot(values_t[stream], weights.astype(bf)) / total
            return mixed, weights, total, query

        real_out = mix(0)[0]
        fake_out, weights, total, query = mix(1)
        differ = fake_out - real_out
        grad_out_t = (loss_weight * differ * lax.rsqrt(differ * differ + match_eps * match_eps)).astype(bf)
        grad_out = grad_out_t.T
        deltas = jnp.sum(grad_out_t.astype(f32) * fake_out, axis=0, keepdims=True)
        probs = weights * (1.0 / total)
        dprobs = dot(values[1], grad_out_t)
        dscores = (probs * (dprobs - deltas) * scale).astype(bf)
        prob_low = probs.astype(bf)
        dq = dot(fake_key_t, dscores).astype(bf).T
        o_ref[blocks, 0] = dq.reshape(per, BLOCK, HEAD_DIM)
        dk = dot(dscores, query)
        dv = dot(prob_low, grad_out)
        if i == 0:
            dk_ref[...] = dk
            dv_ref[...] = dv
        else:
            dk_ref[...] += dk
            dv_ref[...] += dv
    o_ref[:, 1] = dk_ref[...].astype(bf).reshape(16, BLOCK, HEAD_DIM)
    o_ref[:, 2] = dv_ref[...].astype(bf).reshape(16, BLOCK, HEAD_DIM)


def attention(received):
    return pl.pallas_call(
        attention_kernel,
        out_shape=jax.ShapeDtypeStruct((16, 3, BLOCK, HEAD_DIM), jnp.bfloat16),
        in_specs=[VMEM],
        out_specs=VMEM,
        scratch_shapes=[pltpu.VMEM((16 * BLOCK, HEAD_DIM), jnp.float32)] * 2,
        cost_estimate=cost(11 * 1024 * 1024 * 256, 4 << 20),
        compiler_params=limit(),
        name="attention",
    )(received)


HBM = pl.BlockSpec(memory_space=pltpu.HBM)
ANY = pl.BlockSpec(memory_space=pl.ANY)
SMEM = pl.BlockSpec(memory_space=pltpu.SMEM)
DMA = pltpu.SemaphoreType.DMA
COLUMNS = 2 * HEAD_DIM


def prepare_kernel(
    place_ref, real_ref, gen_ref, mod_ref, gain_ref, w_ref, sent_ref, oreal_ref, ofake_ref,
    real_buf, gen_buf, mod_buf, gain_buf, sems,
):
    f32, bf = jnp.float32, jnp.bfloat16
    place = pl.multiple_of(place_ref[0], PIECE)
    copies = [
        pltpu.make_async_copy(gen_ref, gen_buf, sems.at[0]),
        pltpu.make_async_copy(real_ref, real_buf, sems.at[1]),
        pltpu.make_async_copy(mod_ref, mod_buf, sems.at[2]),
        pltpu.make_async_copy(gain_ref, gain_buf, sems.at[3]),
        pltpu.make_async_copy(w_ref.at[:, pl.ds(place, PIECE)], sent_ref, sems.at[4]),
    ]
    for copy in copies:
        copy.start()
    for copy in copies[:4]:
        copy.wait()
    gain = gain_buf[...]
    scale = 1.0 + mod_buf[0:1]
    shift = mod_buf[1:2]
    for r in range(0, BLOCK, 16):
        rows = slice(r, r + 16)
        fake = (gen_buf[rows].astype(f32) * scale + shift).astype(bf).astype(f32)
        for ref, values in ((oreal_ref, real_buf[rows].astype(f32)), (ofake_ref, fake)):
            inverse = lax.rsqrt(jnp.mean(values * values, axis=-1, keepdims=True) + norm_eps)
            ref[rows] = (values * inverse * gain).astype(bf)
    copies[4].wait()


def prepare(place, real, gen, modulation, gain, weight):
    bf, f32 = jnp.bfloat16, jnp.float32
    rows = jax.ShapeDtypeStruct((BLOCK, WIDTH), bf)
    return pl.pallas_call(
        prepare_kernel,
        out_shape=[jax.ShapeDtypeStruct((3, PIECE, COLUMNS), bf), rows, rows],
        in_specs=[SMEM] + [HBM] * 5,
        out_specs=[VMEM] * 3,
        scratch_shapes=[
            pltpu.VMEM((BLOCK, WIDTH), bf),
            pltpu.VMEM((BLOCK, WIDTH), bf),
            pltpu.VMEM((2, WIDTH), f32),
            pltpu.VMEM((1, WIDTH), f32),
            DMA((5,)),
        ],
        cost_estimate=cost(4 << 20, 3 << 20),
        compiler_params=limit(16),
        name="prepare",
    )(place, real, gen, modulation, gain, weight)


NEAR = (2, 3, 2, 3, BLOCK, HEAD_DIM)
SEND = (16, 2, 3, BLOCK, HEAD_DIM)


def near_kernel(*refs):
    row_refs, (w_ref, o_ref, rows_ref, w_buf, sems) = refs[:6], refs[6:]
    copies = [pltpu.make_async_copy(w_ref.at[q], w_buf.at[q], sems.at[q]) for q in range(3)]
    for copy in copies:
        copy.start()
    for i, ref in enumerate(row_refs):
        rows_ref[BLOCK * i : BLOCK * (i + 1)] = ref[...]
    for q in range(3):
        copies[q].wait()
        out = jnp.dot(rows_ref[...], w_buf[q], preferred_element_type=jnp.float32).astype(jnp.bfloat16)
        for k in range(2):
            for j in range(3):
                for s in range(2):
                    r = (2 * j + s) * BLOCK
                    o_ref[k, j, s, q] = out[r : r + BLOCK, HEAD_DIM * k : HEAD_DIM * (k + 1)]


def project_near(rows, weight):
    return pl.pallas_call(
        near_kernel,
        out_shape=jax.ShapeDtypeStruct(NEAR, jnp.bfloat16),
        in_specs=[VMEM] * 6 + [HBM],
        out_specs=VMEM,
        scratch_shapes=[
            pltpu.VMEM((6 * BLOCK, WIDTH), jnp.bfloat16),
            pltpu.VMEM((3, WIDTH, COLUMNS), jnp.bfloat16),
            DMA((3,)),
        ],
        cost_estimate=cost(2 * 384 * 3072 * 768, 7 << 20),
        compiler_params=limit(20),
        name="project_near",
    )(*rows, weight)


def rest_kernel(*refs):
    place_ref, row_refs, near_ref, pieces, w_ref = refs[0], refs[1:9], refs[9], refs[10:18], refs[18]
    o_ref, other_ref, rows_ref, w_buf, other_buf, w_sems, piece_sems, out_sems = refs[19:]
    bf, f32 = jnp.bfloat16, jnp.float32
    own, other = [], []
    for q in range(3):
        own.append(pltpu.make_async_copy(w_ref.at[q], w_buf.at[q], w_sems.at[q]))
        other.append([])
        for i, piece in enumerate(pieces):
            place = pl.multiple_of(place_ref[i], PIECE)
            other[q].append(
                pltpu.make_async_copy(piece.at[q], other_buf.at[q, pl.ds(place, PIECE)], piece_sems.at[q, i])
            )
        for copy in other[q]:
            copy.start()
        own[q].start()
    for i, ref in enumerate(row_refs):
        rows_ref[BLOCK * i : BLOCK * (i + 1)] = ref[...]
    for k in range(2):
        for j in range(3):
            o_ref[4 * k + j] = near_ref[k, j]
    outs = []
    for q in range(3):
        for copy in other[q]:
            copy.wait()
        outs.append(pltpu.make_async_copy(other_buf.at[q], other_ref.at[q], out_sems.at[q]))
        outs[q].start()
        out = jnp.dot(rows_ref[...], other_buf[q], preferred_element_type=f32).astype(bf)
        for k in range(2):
            for j in range(4):
                for s in range(2):
                    r = (2 * j + s) * BLOCK
                    o_ref[4 * (2 + k) + j, s, q] = out[r : r + BLOCK, HEAD_DIM * k : HEAD_DIM * (k + 1)]
        own[q].wait()
        out = jnp.dot(rows_ref[6 * BLOCK :], w_buf[q], preferred_element_type=f32).astype(bf)
        for k in range(2):
            for s in range(2):
                o_ref[4 * k + 3, s, q] = out[BLOCK * s : BLOCK * (s + 1), HEAD_DIM * k : HEAD_DIM * (k + 1)]
    for copy in outs:
        copy.wait()


def project_rest(places, rows, near, pieces, weight):
    bf = jnp.bfloat16
    return pl.pallas_call(
        rest_kernel,
        out_shape=[jax.ShapeDtypeStruct(SEND, bf), jax.ShapeDtypeStruct((3, WIDTH, COLUMNS), bf)],
        in_specs=[SMEM] + [VMEM] * 9 + [ANY] * 8 + [HBM],
        out_specs=[VMEM, HBM],
        scratch_shapes=[
            pltpu.VMEM((8 * BLOCK, WIDTH), bf),
            pltpu.VMEM((3, WIDTH, COLUMNS), bf),
            pltpu.VMEM((3, WIDTH, COLUMNS), bf),
            DMA((3,)),
            DMA((3, 8)),
            DMA((3,)),
        ],
        cost_estimate=cost(2 * 640 * 3072 * 768, 14 << 20),
        compiler_params=limit(28),
        name="project_rest",
    )(places, *rows, near, *pieces, weight)


CHUNK = 768


def unproject_kernel(back_ref, own_ref, other_ref, o0_ref, o1_ref, o2_ref, o3_ref, grads_ref):
    bf, f32 = jnp.bfloat16, jnp.float32

    @pl.when(pl.program_id(0) == 0)
    def _():
        for p in range(2):
            for q in range(3):
                for k in range(2):
                    d = 4 * (2 * p + k)
                    c = ((3 * p + q) * 2 + k) * HEAD_DIM
                    grads_ref[:, c : c + HEAD_DIM] = back_ref[d : d + 4, q].reshape(4 * BLOCK, HEAD_DIM)

    total = None
    for p, ref in enumerate((own_ref, other_ref)):
        for q in range(3):
            c = (3 * p + q) * 2 * HEAD_DIM
            term = lax.dot_general(
                grads_ref[:, c : c + 2 * HEAD_DIM], ref[q], (((1,), (1,)), ((), ())), preferred_element_type=f32
            )
            total = term if total is None else total + term
    o0_ref[...] = total[:BLOCK]
    for j, ref in ((1, o1_ref), (2, o2_ref), (3, o3_ref)):
        ref[...] = total[BLOCK * j : BLOCK * (j + 1)].astype(bf)


def unproject(back, weight, other):
    w_spec = pl.BlockSpec((3, CHUNK, 2 * HEAD_DIM), lambda n: (0, n, 0))
    o_spec = pl.BlockSpec((BLOCK, CHUNK), lambda n: (0, n))
    return pl.pallas_call(
        unproject_kernel,
        out_shape=[jax.ShapeDtypeStruct((BLOCK, WIDTH), jnp.float32)]
        + [jax.ShapeDtypeStruct((BLOCK, WIDTH), jnp.bfloat16)] * 3,
        grid=(WIDTH // CHUNK,),
        in_specs=[pl.BlockSpec((16, 3, BLOCK, HEAD_DIM), lambda n: (0, 0, 0, 0)), w_spec, w_spec],
        out_specs=[o_spec] * 4,
        scratch_shapes=[pltpu.VMEM((4 * BLOCK, 12 * HEAD_DIM), jnp.bfloat16)],
        cost_estimate=cost(2 * 256 * 3072 * 1536, 12 << 20),
        compiler_params=limit(),
        name="unproject",
    )(back, weight, other)


def finish_kernel(own_ref, a_ref, b_ref, c_ref, gen_ref, mod_ref, gain_ref, o_ref):
    f32, bf = jnp.float32, jnp.bfloat16
    gain = gain_ref[...]
    scale = 1.0 + mod_ref[0:1]
    shift = mod_ref[1:2]
    for r in range(0, BLOCK, 16):
        rows = slice(r, r + 16)
        fake = (gen_ref[rows].astype(f32) * scale + shift).astype(bf).astype(f32)
        inverse = lax.rsqrt(jnp.mean(fake * fake, axis=-1, keepdims=True) + norm_eps)
        scaled = fake * inverse
        grad = own_ref[rows] + a_ref[rows].astype(f32) + b_ref[rows].astype(f32) + c_ref[rows].astype(f32)
        grad = grad * gain
        grad = inverse * (grad - scaled * jnp.mean(grad * scaled, axis=-1, keepdims=True))
        o_ref[rows] = (grad * scale).astype(bf)


def finish(own, a, b, c, gen, modulation, gain):
    return pl.pallas_call(
        finish_kernel,
        out_shape=jax.ShapeDtypeStruct((BLOCK, WIDTH), jnp.bfloat16),
        in_specs=[VMEM] * 7,
        out_specs=VMEM,
        cost_estimate=cost(4 << 20, 3 << 20),
        compiler_params=limit(),
        name="finish",
    )(own, a, b, c, gen, modulation, gain)


def on_device(real_tokens, gen_hidden, modulation, norm_gain, weight):
    return step(real_tokens[0], gen_hidden[0], modulation[0], norm_gain[None], weight)[None]


def in_hbm(x):
    return pltpu.with_memory_space_constraint(x, pltpu.HBM)


def step(real_tokens, gen_hidden, modulation, gain, weight):
    colour = (lax.axis_index("x") + 2 * lax.axis_index("zl")) % 4
    core = lax.axis_index("core")

    place = ((((colour + 2) % 4) * 2 + core) * PIECE).astype(jnp.int32)[None]
    sent, real, fake = prepare(
        place, in_hbm(real_tokens), in_hbm(gen_hidden), in_hbm(modulation), in_hbm(gain), in_hbm(weight)
    )
    mine = lax.ppermute(sent, ("zl", "zh"), ACROSS)
    below_real = lax.ppermute(real, "y", ring(1))
    above_fake = lax.ppermute(fake, "y", ring(-1))
    below_fake = lax.ppermute(fake, "y", ring(1))
    above_real = lax.ppermute(real, "y", ring(-1))
    far_real = lax.ppermute(below_real, "y", ring(1))
    far_fake = lax.ppermute(above_fake, "y", ring(-1))
    pieces = [
        mine, lax.ppermute(mine, "x", ring(1)), lax.ppermute(mine, "x", ring(-1)), lax.ppermute(mine, "zl", swap())
    ]
    pieces = pieces + [lax.ppermute(p, "core", swap()) for p in pieces]
    places = jnp.stack(
        [(((colour + c) % 4) * 2 + k) * PIECE for k in (core, 1 - core) for c in (0, 3, 1, 2)]
    ).astype(jnp.int32)

    near_rows = [real, fake, below_real, below_fake, above_real, above_fake]
    near = project_near(near_rows, in_hbm(weight))
    send, other = project_rest(places, near_rows + [far_real, far_fake], near, pieces, in_hbm(weight))
    received = lax.all_to_all(send.reshape(16, 6 * BLOCK, HEAD_DIM), SEQ, split_axis=0, concat_axis=0, tiled=True)
    grads = attention(received.reshape(SEND))
    back = lax.all_to_all(grads.reshape(16, 3 * BLOCK, HEAD_DIM), SEQ, split_axis=0, concat_axis=0, tiled=True)
    part = unproject(back.reshape(16, 3, BLOCK, HEAD_DIM), weight, other)
    from_far = lax.ppermute(part[3], "y", ring(2))
    from_above = lax.ppermute(part[1], "y", ring(-1))
    from_below = lax.ppermute(part[2], "y", ring(1))
    return finish(part[0], from_far, from_above, from_below, gen_hidden, modulation, gain)


def solution(mesh):
    torus = Mesh(mesh.devices.reshape(2, 4, 2, 2, 4), ("zl", "x", "core", "zh", "y"))
    fsdp = ("zh", "y")
    in_specs = (
        P(fsdp, SEQ, None),
        P(fsdp, SEQ, None),
        P(fsdp, None, None),
        P(),
        P(None, None, fsdp),
    )
    return jax.shard_map(on_device, mesh=torus, in_specs=in_specs, out_specs=P(fsdp, SEQ, None), check_vma=False)
```

```python
import jax
import jax.numpy as jnp
from jax import lax
from jax.experimental import pallas as pl
from jax.experimental.pallas import tpu as pltpu
from jax.sharding import Mesh
from jax.sharding import PartitionSpec as P


HEAD_DIM = 128
WIDTH = 3072
BLOCK = 64
PIECE = WIDTH // 8

norm_eps = 1e-06
match_eps = 0.05
loss_weight = 4.0


SEQ = ("zl", "x", "core")
ACROSS = [(0, 3), (3, 0), (1, 2), (2, 1)]


VMEM = pl.BlockSpec(memory_space=pltpu.VMEM)


def cost(flops, touched):
    return pl.CostEstimate(flops=flops, bytes_accessed=touched, transcendentals=0)


def limit(mib=24):
    return pltpu.CompilerParams(vmem_limit_bytes=mib * 1024 * 1024)


def ring(step):
    return [(i, (i + step) % 4) for i in range(4)]


def swap():
    return [(0, 1), (1, 0)]


def attention_kernel(x_ref, o_ref, dk_ref, dv_ref):
    bf = jnp.bfloat16
    f32 = jnp.float32
    length = 16 * BLOCK
    tile = 256
    per = tile // BLOCK
    scale = HEAD_DIM ** (-0.5)
    to_two = scale * 1.4426950408889634

    def whole(stream, part):
        return x_ref[:, stream, part].reshape(length, HEAD_DIM)

    def dot(a, b):
        return jnp.dot(a, b, preferred_element_type=f32)

    keys = [whole(s, 1) for s in range(2)]
    values = [whole(s, 2) for s in range(2)]
    values_t = [v.T for v in values]
    fake_key_t = keys[1].T

    for i in range(length // tile):
        blocks = slice(per * i, per * (i + 1))

        def mix(stream):
            query = x_ref[blocks, stream, 0].reshape(tile, HEAD_DIM)
            scores = dot(keys[stream], query.T)
            highest = jnp.max(scores, axis=0, keepdims=True)
            weights = jnp.exp2((scores - highest) * to_two)
            total = jnp.sum(weights, axis=0, keepdims=True)
            mixed = dot(values_t[stream], weights.astype(bf)) / total
            return mixed, weights, total, query

        real_out = mix(0)[0]
        fake_out, weights, total, query = mix(1)
        differ = fake_out - real_out
        grad_out_t = (loss_weight * differ * lax.rsqrt(differ * differ + match_eps * match_eps)).astype(bf)
        grad_out = grad_out_t.T
        deltas = jnp.sum(grad_out_t.astype(f32) * fake_out, axis=0, keepdims=True)
        probs = weights * (1.0 / total)
        dprobs = dot(values[1], grad_out_t)
        dscores = (probs * (dprobs - deltas) * scale).astype(bf)
        prob_low = probs.astype(bf)
        dq = dot(fake_key_t, dscores).astype(bf).T
        o_ref[blocks, 0] = dq.reshape(per, BLOCK, HEAD_DIM)
        dk = dot(dscores, query)
        dv = dot(prob_low, grad_out)
        if i == 0:
            dk_ref[...] = dk
            dv_ref[...] = dv
        else:
            dk_ref[...] += dk
            dv_ref[...] += dv
    o_ref[:, 1] = dk_ref[...].astype(bf).reshape(16, BLOCK, HEAD_DIM)
    o_ref[:, 2] = dv_ref[...].astype(bf).reshape(16, BLOCK, HEAD_DIM)


def attention(received):
    return pl.pallas_call(
        attention_kernel,
        out_shape=jax.ShapeDtypeStruct((16, 3, BLOCK, HEAD_DIM), jnp.bfloat16),
        in_specs=[VMEM],
        out_specs=VMEM,
        scratch_shapes=[pltpu.VMEM((16 * BLOCK, HEAD_DIM), jnp.float32)] * 2,
        cost_estimate=cost(11 * 1024 * 1024 * 256, 4 << 20),
        compiler_params=limit(),
        name="attention",
    )(received)


HBM = pl.BlockSpec(memory_space=pltpu.HBM)
ANY = pl.BlockSpec(memory_space=pl.ANY)
SMEM = pl.BlockSpec(memory_space=pltpu.SMEM)
DMA = pltpu.SemaphoreType.DMA
COLUMNS = 2 * HEAD_DIM


def prepare_kernel(
    where_ref, real_ref, gen_ref, mod_ref, gain_ref, w_ref, sent_ref, oreal_ref, ofake_ref,
    real_buf, gen_buf, mod_buf, gain_buf, sems,
):
    f32, bf = jnp.float32, jnp.bfloat16
    place = pl.multiple_of(((where_ref[0] + 4) % 8) * PIECE, PIECE)
    copies = [
        pltpu.make_async_copy(gen_ref, gen_buf, sems.at[0]),
        pltpu.make_async_copy(real_ref, real_buf, sems.at[1]),
        pltpu.make_async_copy(mod_ref, mod_buf, sems.at[2]),
        pltpu.make_async_copy(gain_ref, gain_buf, sems.at[3]),
        pltpu.make_async_copy(w_ref.at[:, pl.ds(place, PIECE)], sent_ref, sems.at[4]),
    ]
    for copy in copies:
        copy.start()
    for copy in copies[:4]:
        copy.wait()
    gain = gain_buf[...]
    scale = 1.0 + mod_buf[0:1]
    shift = mod_buf[1:2]
    for r in range(0, BLOCK, 16):
        rows = slice(r, r + 16)
        fake = (gen_buf[rows].astype(f32) * scale + shift).astype(bf).astype(f32)
        for ref, values in ((oreal_ref, real_buf[rows].astype(f32)), (ofake_ref, fake)):
            inverse = lax.rsqrt(jnp.mean(values * values, axis=-1, keepdims=True) + norm_eps)
            ref[rows] = (values * inverse * gain).astype(bf)
    copies[4].wait()


def prepare(where, real, gen, modulation, gain, weight):
    bf, f32 = jnp.bfloat16, jnp.float32
    rows = jax.ShapeDtypeStruct((BLOCK, WIDTH), bf)
    return pl.pallas_call(
        prepare_kernel,
        out_shape=[jax.ShapeDtypeStruct((3, PIECE, COLUMNS), bf), rows, rows],
        in_specs=[SMEM] + [HBM] * 5,
        out_specs=[VMEM] * 3,
        scratch_shapes=[
            pltpu.VMEM((BLOCK, WIDTH), bf),
            pltpu.VMEM((BLOCK, WIDTH), bf),
            pltpu.VMEM((2, WIDTH), f32),
            pltpu.VMEM((1, WIDTH), f32),
            DMA((5,)),
        ],
        cost_estimate=cost(4 << 20, 3 << 20),
        compiler_params=limit(16),
        name="prepare",
    )(where, real, gen, modulation, gain, weight)


NEAR = (2, 3, 2, 3, BLOCK, HEAD_DIM)
SEND = (16, 2, 3, BLOCK, HEAD_DIM)


def near_kernel(*refs):
    row_refs, (w_ref, o_ref, held_ref, rows_ref, sems) = refs[:6], refs[6:]
    copies = [pltpu.make_async_copy(w_ref.at[q], held_ref.at[q], sems.at[q]) for q in range(3)]
    for copy in copies:
        copy.start()
    for i, ref in enumerate(row_refs):
        rows_ref[BLOCK * i : BLOCK * (i + 1)] = ref[...]
    for q in range(3):
        copies[q].wait()
        out = jnp.dot(rows_ref[...], held_ref[q], preferred_element_type=jnp.float32).astype(jnp.bfloat16)
        for k in range(2):
            for j in range(3):
                for s in range(2):
                    r = (2 * j + s) * BLOCK
                    o_ref[k, j, s, q] = out[r : r + BLOCK, HEAD_DIM * k : HEAD_DIM * (k + 1)]


def project_near(rows, weight):
    return pl.pallas_call(
        near_kernel,
        out_shape=[
            jax.ShapeDtypeStruct(NEAR, jnp.bfloat16),
            jax.ShapeDtypeStruct((3, WIDTH, COLUMNS), jnp.bfloat16),
        ],
        in_specs=[VMEM] * 6 + [HBM],
        out_specs=[VMEM] * 2,
        scratch_shapes=[pltpu.VMEM((6 * BLOCK, WIDTH), jnp.bfloat16), DMA((3,))],
        cost_estimate=cost(2 * 384 * 3072 * 768, 7 << 20),
        compiler_params=limit(16),
        name="project_near",
    )(*rows, weight)


def rest_kernel(*refs):
    where_ref, row_refs, near_ref, pieces, w_ref = refs[0], refs[1:9], refs[9], refs[10:18], refs[18]
    o_ref, other_ref, rows_ref = refs[19:]
    bf, f32 = jnp.bfloat16, jnp.float32
    where = where_ref[0]
    colour, core = where // 2, where % 2
    places = [(((colour + c) % 4) * 2 + k) * PIECE for k in (core, 1 - core) for c in (0, 3, 1, 2)]
    for i, ref in enumerate(row_refs):
        rows_ref[BLOCK * i : BLOCK * (i + 1)] = ref[...]
    for k in range(2):
        for j in range(3):
            o_ref[4 * k + j] = near_ref[k, j]
    for q in range(3):
        out = jnp.dot(rows_ref[6 * BLOCK :], w_ref[q], preferred_element_type=f32).astype(bf)
        for k in range(2):
            for s in range(2):
                o_ref[4 * k + 3, s, q] = out[BLOCK * s : BLOCK * (s + 1), HEAD_DIM * k : HEAD_DIM * (k + 1)]
        for i, piece in enumerate(pieces):
            other_ref[q, pl.ds(pl.multiple_of(places[i], PIECE), PIECE)] = piece[q]
        out = jnp.dot(rows_ref[...], other_ref[q], preferred_element_type=f32).astype(bf)
        for k in range(2):
            for j in range(4):
                for s in range(2):
                    r = (2 * j + s) * BLOCK
                    o_ref[4 * (2 + k) + j, s, q] = out[r : r + BLOCK, HEAD_DIM * k : HEAD_DIM * (k + 1)]


def project_rest(where, rows, near, pieces, weight):
    bf = jnp.bfloat16
    return pl.pallas_call(
        rest_kernel,
        out_shape=[jax.ShapeDtypeStruct(SEND, bf), jax.ShapeDtypeStruct((3, WIDTH, COLUMNS), bf)],
        in_specs=[SMEM] + [VMEM] * 18,
        out_specs=[VMEM] * 2,
        scratch_shapes=[pltpu.VMEM((8 * BLOCK, WIDTH), bf)],
        cost_estimate=cost(2 * 640 * 3072 * 768, 14 << 20),
        compiler_params=limit(16),
        name="project_rest",
    )(where, *rows, near, *pieces, weight)


CHUNK = 768


def unproject_kernel(back_ref, own_ref, other_ref, o0_ref, o1_ref, o2_ref, o3_ref, grads_ref):
    bf, f32 = jnp.bfloat16, jnp.float32
    for p in range(2):
        for q in range(3):
            for k in range(2):
                d = 4 * (2 * p + k)
                c = ((3 * p + q) * 2 + k) * HEAD_DIM
                grads_ref[:, c : c + HEAD_DIM] = back_ref[d : d + 4, q].reshape(4 * BLOCK, HEAD_DIM)
    for n in range(0, WIDTH, CHUNK):
        total = None
        for p, ref in enumerate((own_ref, other_ref)):
            for q in range(3):
                c = (3 * p + q) * COLUMNS
                term = lax.dot_general(
                    grads_ref[:, c : c + COLUMNS],
                    ref[q, n : n + CHUNK],
                    (((1,), (1,)), ((), ())),
                    preferred_element_type=f32,
                )
                total = term if total is None else total + term
        o0_ref[:, n : n + CHUNK] = total[:BLOCK]
        for j, ref in ((1, o1_ref), (2, o2_ref), (3, o3_ref)):
            ref[:, n : n + CHUNK] = total[BLOCK * j : BLOCK * (j + 1)].astype(bf)


def unproject(back, weight, other):
    return pl.pallas_call(
        unproject_kernel,
        out_shape=[jax.ShapeDtypeStruct((BLOCK, WIDTH), jnp.float32)]
        + [jax.ShapeDtypeStruct((BLOCK, WIDTH), jnp.bfloat16)] * 3,
        in_specs=[VMEM] * 3,
        out_specs=[VMEM] * 4,
        scratch_shapes=[pltpu.VMEM((4 * BLOCK, 12 * HEAD_DIM), jnp.bfloat16)],
        cost_estimate=cost(2 * 256 * 3072 * 1536, 12 << 20),
        compiler_params=limit(16),
        name="unproject",
    )(back, weight, other)


def finish_kernel(own_ref, a_ref, b_ref, c_ref, gen_ref, mod_ref, gain_ref, o_ref):
    f32, bf = jnp.float32, jnp.bfloat16
    gain = gain_ref[...]
    scale = 1.0 + mod_ref[0:1]
    shift = mod_ref[1:2]
    for r in range(0, BLOCK, 16):
        rows = slice(r, r + 16)
        fake = (gen_ref[rows].astype(f32) * scale + shift).astype(bf).astype(f32)
        inverse = lax.rsqrt(jnp.mean(fake * fake, axis=-1, keepdims=True) + norm_eps)
        scaled = fake * inverse
        grad = own_ref[rows] + a_ref[rows].astype(f32) + b_ref[rows].astype(f32) + c_ref[rows].astype(f32)
        grad = grad * gain
        grad = inverse * (grad - scaled * jnp.mean(grad * scaled, axis=-1, keepdims=True))
        o_ref[rows] = (grad * scale).astype(bf)


def finish(own, a, b, c, gen, modulation, gain):
    return pl.pallas_call(
        finish_kernel,
        out_shape=jax.ShapeDtypeStruct((BLOCK, WIDTH), jnp.bfloat16),
        in_specs=[VMEM] * 7,
        out_specs=VMEM,
        cost_estimate=cost(4 << 20, 3 << 20),
        compiler_params=limit(),
        name="finish",
    )(own, a, b, c, gen, modulation, gain)


def on_device(real_tokens, gen_hidden, modulation, norm_gain, weight):
    return step(real_tokens[0], gen_hidden[0], modulation[0], norm_gain[None], weight)[None]


def in_hbm(x):
    return pltpu.with_memory_space_constraint(x, pltpu.HBM)


def step(real_tokens, gen_hidden, modulation, gain, weight):
    colour = (lax.axis_index("x") + 2 * lax.axis_index("zl")) % 4
    core = lax.axis_index("core")

    where = (colour * 2 + core).astype(jnp.int32)[None]
    sent, real, fake = prepare(
        where, in_hbm(real_tokens), in_hbm(gen_hidden), in_hbm(modulation), in_hbm(gain), in_hbm(weight)
    )
    mine = lax.ppermute(sent, ("zl", "zh"), ACROSS)
    below_real = lax.ppermute(real, "y", ring(1))
    above_fake = lax.ppermute(fake, "y", ring(-1))
    below_fake = lax.ppermute(fake, "y", ring(1))
    above_real = lax.ppermute(real, "y", ring(-1))
    far_real = lax.ppermute(below_real, "y", ring(1))
    far_fake = lax.ppermute(above_fake, "y", ring(-1))
    pieces = [
        mine, lax.ppermute(mine, "x", ring(1)), lax.ppermute(mine, "x", ring(-1)), lax.ppermute(mine, "zl", swap())
    ]
    pieces = pieces + [lax.ppermute(p, "core", swap()) for p in pieces]

    near_rows = [real, fake, below_real, below_fake, above_real, above_fake]
    near, held = project_near(near_rows, in_hbm(weight))
    pieces = [pltpu.with_memory_space_constraint(p, pltpu.VMEM) for p in pieces]
    send, other = project_rest(where, near_rows + [far_real, far_fake], near, pieces, held)
    received = lax.all_to_all(send.reshape(16, 6 * BLOCK, HEAD_DIM), SEQ, split_axis=0, concat_axis=0, tiled=True)
    grads = attention(received.reshape(SEND))
    back = lax.all_to_all(grads.reshape(16, 3 * BLOCK, HEAD_DIM), SEQ, split_axis=0, concat_axis=0, tiled=True)
    part = unproject(back.reshape(16, 3, BLOCK, HEAD_DIM), held, other)
    from_far = lax.ppermute(part[3], "y", ring(2))
    from_above = lax.ppermute(part[1], "y", ring(-1))
    from_below = lax.ppermute(part[2], "y", ring(1))
    return finish(part[0], from_far, from_above, from_below, gen_hidden, modulation, gain)


def solution(mesh):
    torus = Mesh(mesh.devices.reshape(2, 4, 2, 2, 4), ("zl", "x", "core", "zh", "y"))
    fsdp = ("zh", "y")
    in_specs = (
        P(fsdp, SEQ, None),
        P(fsdp, SEQ, None),
        P(fsdp, None, None),
        P(),
        P(None, None, fsdp),
    )
    return jax.shard_map(on_device, mesh=torus, in_specs=in_specs, out_specs=P(fsdp, SEQ, None), check_vma=False)
```

```python
import jax
import jax.numpy as jnp
from jax import lax
from jax.experimental import pallas as pl
from jax.experimental.pallas import tpu as pltpu
from jax.sharding import Mesh
from jax.sharding import PartitionSpec as P


HEAD_DIM = 128
WIDTH = 3072
BLOCK = 64
PIECE = WIDTH // 8

norm_eps = 1e-06
match_eps = 0.05
loss_weight = 4.0


SEQ = ("zl", "x", "core")
ACROSS = [(0, 3), (3, 0), (1, 2), (2, 1)]


VMEM = pl.BlockSpec(memory_space=pltpu.VMEM)


def cost(flops, touched):
    return pl.CostEstimate(flops=flops, bytes_accessed=touched, transcendentals=0)


def limit(mib=24):
    return pltpu.CompilerParams(vmem_limit_bytes=mib * 1024 * 1024)


def ring(step):
    return [(i, (i + step) % 4) for i in range(4)]


def swap():
    return [(0, 1), (1, 0)]


def attention_kernel(x_ref, o_ref):
    bf = jnp.bfloat16
    f32 = jnp.float32
    length = 16 * BLOCK
    scale = HEAD_DIM ** (-0.5)
    to_two = scale * 1.4426950408889634

    def whole(stream, part):
        return x_ref[:, stream, part].reshape(length, HEAD_DIM)

    def dot(a, b):
        return jnp.dot(a, b, preferred_element_type=f32)

    def mix(stream):
        query, key, value = (whole(stream, part) for part in range(3))
        scores = dot(key, query.T)
        highest = jnp.max(scores, axis=0, keepdims=True)
        weights = jnp.exp2((scores - highest) * to_two)
        inverse = 1.0 / jnp.sum(weights, axis=0, keepdims=True)
        return dot(value.T, weights.astype(bf)) * inverse, weights, inverse

    real_out = mix(0)[0]
    fake_out, weights, inverse = mix(1)
    query, key, value = (whole(1, part) for part in range(3))
    differ = fake_out - real_out
    grad_out = (loss_weight * differ * lax.rsqrt(differ * differ + match_eps * match_eps)).astype(bf)
    deltas = jnp.sum(grad_out.astype(f32) * fake_out, axis=0, keepdims=True)
    probs = weights * inverse
    dscores = (probs * (dot(value, grad_out) - deltas)).astype(bf)

    def store(part, grad):
        o_ref[:, part] = grad.reshape(16, BLOCK, HEAD_DIM)

    store(0, (dot(key.T, dscores) * scale).astype(bf).T)
    store(1, (dot(dscores, query) * scale).astype(bf))
    store(2, dot(probs.astype(bf), grad_out.T).astype(bf))


def attention(received):
    return pl.pallas_call(
        attention_kernel,
        out_shape=jax.ShapeDtypeStruct((16, 3, BLOCK, HEAD_DIM), jnp.bfloat16),
        in_specs=[VMEM],
        out_specs=VMEM,
        cost_estimate=cost(11 * 1024 * 1024 * 256, 4 << 20),
        compiler_params=pltpu.CompilerParams(vmem_limit_bytes=36 << 20),
        name="attention",
    )(received)


HBM = pl.BlockSpec(memory_space=pltpu.HBM)
ANY = pl.BlockSpec(memory_space=pl.ANY)
SMEM = pl.BlockSpec(memory_space=pltpu.SMEM)
DMA = pltpu.SemaphoreType.DMA
COLUMNS = 2 * HEAD_DIM


def prepare_kernel(
    where_ref, real_ref, gen_ref, mod_ref, gain_ref, w_ref, sent_ref, oreal_ref, ofake_ref,
    real_buf, gen_buf, mod_buf, gain_buf, sems,
):
    f32, bf = jnp.float32, jnp.bfloat16
    place = pl.multiple_of(((where_ref[0] + 4) % 8) * PIECE, PIECE)
    copies = [
        pltpu.make_async_copy(gen_ref, gen_buf, sems.at[0]),
        pltpu.make_async_copy(real_ref, real_buf, sems.at[1]),
        pltpu.make_async_copy(mod_ref, mod_buf, sems.at[2]),
        pltpu.make_async_copy(gain_ref, gain_buf, sems.at[3]),
        pltpu.make_async_copy(w_ref.at[:, pl.ds(place, PIECE)], sent_ref, sems.at[4]),
    ]
    for copy in copies:
        copy.start()
    for copy in copies[:4]:
        copy.wait()
    gain = gain_buf[...]
    scale = 1.0 + mod_buf[0:1]
    shift = mod_buf[1:2]
    for r in range(0, BLOCK, 16):
        rows = slice(r, r + 16)
        fake = (gen_buf[rows].astype(f32) * scale + shift).astype(bf).astype(f32)
        for ref, values in ((oreal_ref, real_buf[rows].astype(f32)), (ofake_ref, fake)):
            inverse = lax.rsqrt(jnp.mean(values * values, axis=-1, keepdims=True) + norm_eps)
            ref[rows] = (values * inverse * gain).astype(bf)
    copies[4].wait()


def prepare(where, real, gen, modulation, gain, weight):
    bf, f32 = jnp.bfloat16, jnp.float32
    rows = jax.ShapeDtypeStruct((BLOCK, WIDTH), bf)
    return pl.pallas_call(
        prepare_kernel,
        out_shape=[jax.ShapeDtypeStruct((3, PIECE, COLUMNS), bf), rows, rows],
        in_specs=[SMEM] + [HBM] * 5,
        out_specs=[VMEM] * 3,
        scratch_shapes=[
            pltpu.VMEM((BLOCK, WIDTH), bf),
            pltpu.VMEM((BLOCK, WIDTH), bf),
            pltpu.VMEM((2, WIDTH), f32),
            pltpu.VMEM((1, WIDTH), f32),
            DMA((5,)),
        ],
        cost_estimate=cost(4 << 20, 3 << 20),
        compiler_params=limit(16),
        name="prepare",
    )(where, real, gen, modulation, gain, weight)


NEAR = (2, 3, 2, 3, BLOCK, HEAD_DIM)
SEND = (16, 2, 3, BLOCK, HEAD_DIM)


def near_kernel(*refs):
    row_refs, (w_ref, o_ref, held_ref, rows_ref, sems) = refs[:6], refs[6:]
    copies = [pltpu.make_async_copy(w_ref.at[q], held_ref.at[q], sems.at[q]) for q in range(3)]
    for copy in copies:
        copy.start()
    for i, ref in enumerate(row_refs):
        rows_ref[BLOCK * i : BLOCK * (i + 1)] = ref[...]
    for q in range(3):
        copies[q].wait()
        out = jnp.dot(rows_ref[...], held_ref[q], preferred_element_type=jnp.float32).astype(jnp.bfloat16)
        for k in range(2):
            for j in range(3):
                for s in range(2):
                    r = (2 * j + s) * BLOCK
                    o_ref[k, j, s, q] = out[r : r + BLOCK, HEAD_DIM * k : HEAD_DIM * (k + 1)]


def project_near(rows, weight):
    return pl.pallas_call(
        near_kernel,
        out_shape=[
            jax.ShapeDtypeStruct(NEAR, jnp.bfloat16),
            jax.ShapeDtypeStruct((3, WIDTH, COLUMNS), jnp.bfloat16),
        ],
        in_specs=[VMEM] * 6 + [HBM],
        out_specs=[VMEM] * 2,
        scratch_shapes=[pltpu.VMEM((6 * BLOCK, WIDTH), jnp.bfloat16), DMA((3,))],
        cost_estimate=cost(2 * 384 * 3072 * 768, 7 << 20),
        compiler_params=limit(16),
        name="project_near",
    )(*rows, weight)


def rest_kernel(*refs):
    where_ref, row_refs, near_ref, pieces, w_ref = refs[0], refs[1:9], refs[9], refs[10:18], refs[18]
    o_ref, other_ref, rows_ref = refs[19:]
    bf, f32 = jnp.bfloat16, jnp.float32
    where = where_ref[0]
    colour, core = where // 2, where % 2
    places = [(((colour + c) % 4) * 2 + k) * PIECE for k in (core, 1 - core) for c in (0, 3, 1, 2)]
    for i, ref in enumerate(row_refs):
        rows_ref[BLOCK * i : BLOCK * (i + 1)] = ref[...]
    for k in range(2):
        for j in range(3):
            o_ref[4 * k + j] = near_ref[k, j]
    for q in range(3):
        out = jnp.dot(rows_ref[6 * BLOCK :], w_ref[q], preferred_element_type=f32).astype(bf)
        for k in range(2):
            for s in range(2):
                o_ref[4 * k + 3, s, q] = out[BLOCK * s : BLOCK * (s + 1), HEAD_DIM * k : HEAD_DIM * (k + 1)]
        for i, piece in enumerate(pieces):
            other_ref[q, pl.ds(pl.multiple_of(places[i], PIECE), PIECE)] = piece[q]
        out = jnp.dot(rows_ref[...], other_ref[q], preferred_element_type=f32).astype(bf)
        for k in range(2):
            for j in range(4):
                for s in range(2):
                    r = (2 * j + s) * BLOCK
                    o_ref[4 * (2 + k) + j, s, q] = out[r : r + BLOCK, HEAD_DIM * k : HEAD_DIM * (k + 1)]


def project_rest(where, rows, near, pieces, weight):
    bf = jnp.bfloat16
    return pl.pallas_call(
        rest_kernel,
        out_shape=[jax.ShapeDtypeStruct(SEND, bf), jax.ShapeDtypeStruct((3, WIDTH, COLUMNS), bf)],
        in_specs=[SMEM] + [VMEM] * 18,
        out_specs=[VMEM] * 2,
        scratch_shapes=[pltpu.VMEM((8 * BLOCK, WIDTH), bf)],
        cost_estimate=cost(2 * 640 * 3072 * 768, 14 << 20),
        compiler_params=limit(16),
        name="project_rest",
    )(where, *rows, near, *pieces, weight)


CHUNK = 768


HALF_BLOCK = BLOCK // 2


def unproject_kernel(back_ref, own_ref, other_ref, own_out, below_ref, above_ref, *refs):
    far_up, far_down, near_up, near_down, grads_ref = refs
    bf, f32 = jnp.bfloat16, jnp.float32
    for p in range(2):
        for q in range(3):
            for k in range(2):
                d = 4 * (2 * p + k)
                c = ((3 * p + q) * 2 + k) * HEAD_DIM
                grads_ref[:, c : c + HEAD_DIM] = back_ref[d : d + 4, q].reshape(4 * BLOCK, HEAD_DIM)
    for n in range(0, WIDTH, CHUNK):
        total = None
        for p, ref in enumerate((own_ref, other_ref)):
            for q in range(3):
                c = (3 * p + q) * COLUMNS
                term = lax.dot_general(
                    grads_ref[:, c : c + COLUMNS],
                    ref[q, n : n + CHUNK],
                    (((1,), (1,)), ((), ())),
                    preferred_element_type=f32,
                )
                total = term if total is None else total + term
        columns = slice(n, n + CHUNK)
        parts = [total[HALF_BLOCK * i : HALF_BLOCK * (i + 1)] for i in range(8)]
        own_out[:, columns] = total[:BLOCK]
        near_down[:, columns] = parts[2].astype(bf)
        below_ref[:, columns] = parts[3]
        above_ref[:, columns] = parts[4]
        near_up[:, columns] = parts[5].astype(bf)
        far_up[:, columns] = parts[6].astype(bf)
        far_down[:, columns] = parts[7].astype(bf)


def unproject(back, weight, other):
    f32 = jnp.float32
    half = (HALF_BLOCK, WIDTH)
    return pl.pallas_call(
        unproject_kernel,
        out_shape=[jax.ShapeDtypeStruct((BLOCK, WIDTH), f32)]
        + [jax.ShapeDtypeStruct(half, f32)] * 2
        + [jax.ShapeDtypeStruct(half, jnp.bfloat16)] * 4,
        in_specs=[VMEM] * 3,
        out_specs=[VMEM] * 7,
        scratch_shapes=[pltpu.VMEM((4 * BLOCK, 12 * HEAD_DIM), jnp.bfloat16)],
        cost_estimate=cost(2 * 256 * 3072 * 1536, 12 << 20),
        compiler_params=limit(16),
        name="unproject",
    )(back, weight, other)


def pass_on_kernel(below_ref, above_ref, down_ref, up_ref, odown_ref, oup_ref):
    odown_ref[...] = (below_ref[...] + down_ref[...].astype(jnp.float32)).astype(jnp.bfloat16)
    oup_ref[...] = (above_ref[...] + up_ref[...].astype(jnp.float32)).astype(jnp.bfloat16)


def pass_on(below, above, from_up, from_down):
    return pl.pallas_call(
        pass_on_kernel,
        out_shape=[jax.ShapeDtypeStruct((HALF_BLOCK, WIDTH), jnp.bfloat16)] * 2,
        in_specs=[VMEM] * 4,
        out_specs=[VMEM] * 2,
        cost_estimate=cost(1 << 18, 2 << 20),
        compiler_params=limit(8),
        name="pass_on",
    )(below, above, from_up, from_down)


def finish_kernel(own_ref, a_ref, b_ref, c_ref, d_ref, gen_ref, mod_ref, gain_ref, o_ref):
    f32, bf = jnp.float32, jnp.bfloat16
    gain = gain_ref[...]
    scale = 1.0 + mod_ref[0:1]
    shift = mod_ref[1:2]
    for r in range(0, BLOCK, 16):
        rows = slice(r, r + 16)
        fake = (gen_ref[rows].astype(f32) * scale + shift).astype(bf).astype(f32)
        inverse = lax.rsqrt(jnp.mean(fake * fake, axis=-1, keepdims=True) + norm_eps)
        scaled = fake * inverse
        one, two = (a_ref, b_ref) if r < HALF_BLOCK else (c_ref, d_ref)
        part = slice(r % HALF_BLOCK, r % HALF_BLOCK + 16)
        grad = own_ref[rows] + one[part].astype(f32) + two[part].astype(f32)
        grad = grad * gain
        grad = inverse * (grad - scaled * jnp.mean(grad * scaled, axis=-1, keepdims=True))
        o_ref[rows] = (grad * scale).astype(bf)


def finish(own, parts, gen, modulation, gain):
    return pl.pallas_call(
        finish_kernel,
        out_shape=jax.ShapeDtypeStruct((BLOCK, WIDTH), jnp.bfloat16),
        in_specs=[VMEM] * 8,
        out_specs=VMEM,
        cost_estimate=cost(4 << 20, 3 << 20),
        compiler_params=limit(8),
        name="finish",
    )(own, *parts, gen, modulation, gain)


def on_device(real_tokens, gen_hidden, modulation, norm_gain, weight):
    return step(real_tokens[0], gen_hidden[0], modulation[0], norm_gain[None], weight)[None]


def in_hbm(x):
    return pltpu.with_memory_space_constraint(x, pltpu.HBM)


def step(real_tokens, gen_hidden, modulation, gain, weight):
    colour = (lax.axis_index("x") + 2 * lax.axis_index("zl")) % 4
    core = lax.axis_index("core")

    where = (colour * 2 + core).astype(jnp.int32)[None]
    sent, real, fake = prepare(
        where, in_hbm(real_tokens), in_hbm(gen_hidden), in_hbm(modulation), in_hbm(gain), in_hbm(weight)
    )
    mine = lax.ppermute(sent, ("zl", "zh"), ACROSS)
    below_real = lax.ppermute(real, "y", ring(1))
    above_fake = lax.ppermute(fake, "y", ring(-1))
    below_fake = lax.ppermute(fake, "y", ring(1))
    above_real = lax.ppermute(real, "y", ring(-1))
    far_real = lax.ppermute(below_real, "y", ring(1))
    far_fake = lax.ppermute(above_fake, "y", ring(-1))
    pieces = [
        mine, lax.ppermute(mine, "x", ring(1)), lax.ppermute(mine, "x", ring(-1)), lax.ppermute(mine, "zl", swap())
    ]
    pieces = pieces + [lax.ppermute(p, "core", swap()) for p in pieces]

    near_rows = [real, fake, below_real, below_fake, above_real, above_fake]
    near, held = project_near(near_rows, in_hbm(weight))
    pieces = [pltpu.with_memory_space_constraint(p, pltpu.VMEM) for p in pieces]
    send, other = project_rest(where, near_rows + [far_real, far_fake], near, pieces, held)
    received = lax.all_to_all(send.reshape(16, 6 * BLOCK, HEAD_DIM), SEQ, split_axis=0, concat_axis=0, tiled=True)
    grads = attention(received.reshape(SEND))
    back = lax.all_to_all(grads.reshape(16, 3 * BLOCK, HEAD_DIM), SEQ, split_axis=0, concat_axis=0, tiled=True)
    own, below, above, far_up, far_down, near_up, near_down = unproject(
        back.reshape(16, 3, BLOCK, HEAD_DIM), held, other
    )
    got_up = lax.ppermute(far_up, "y", ring(1))
    got_down = lax.ppermute(far_down, "y", ring(-1))
    low_near = lax.ppermute(near_down, "y", ring(-1))
    high_near = lax.ppermute(near_up, "y", ring(1))
    sum_down, sum_up = pass_on(below, above, got_down, got_up)
    low_sum = lax.ppermute(sum_up, "y", ring(1))
    high_sum = lax.ppermute(sum_down, "y", ring(-1))
    return finish(own, (low_sum, low_near, high_near, high_sum), gen_hidden, modulation, gain)


def solution(mesh):
    torus = Mesh(mesh.devices.reshape(2, 4, 2, 2, 4), ("zl", "x", "core", "zh", "y"))
    fsdp = ("zh", "y")
    in_specs = (
        P(fsdp, SEQ, None),
        P(fsdp, SEQ, None),
        P(fsdp, None, None),
        P(),
        P(None, None, fsdp),
    )
    return jax.shard_map(on_device, mesh=torus, in_specs=in_specs, out_specs=P(fsdp, SEQ, None), check_vma=False)
```

```python
import jax
import jax.numpy as jnp
from jax import lax
from jax.experimental import pallas as pl
from jax.experimental.pallas import tpu as pltpu
from jax.sharding import Mesh
from jax.sharding import PartitionSpec as P


HEAD_DIM = 128
WIDTH = 3072
BLOCK = 64
PIECE = 288
SHARED = 8 * PIECE
TAIL = (WIDTH - SHARED) // 2

norm_eps = 1e-06
match_eps = 0.05
loss_weight = 4.0


SEQ = ("zl", "x", "core")
ACROSS = [(0, 3), (3, 0), (1, 2), (2, 1)]


VMEM = pl.BlockSpec(memory_space=pltpu.VMEM)


def cost(flops, touched):
    return pl.CostEstimate(flops=flops, bytes_accessed=touched, transcendentals=0)


def limit(mib=24):
    return pltpu.CompilerParams(vmem_limit_bytes=mib * 1024 * 1024)


def ring(step):
    return [(i, (i + step) % 4) for i in range(4)]


def swap():
    return [(0, 1), (1, 0)]


def attention_kernel(x_ref, o_ref):
    bf = jnp.bfloat16
    f32 = jnp.float32
    length = 16 * BLOCK
    scale = HEAD_DIM ** (-0.5)
    to_two = scale * 1.4426950408889634

    def whole(stream, part):
        return x_ref[:, stream, part].reshape(length, HEAD_DIM)

    def dot(a, b):
        return jnp.dot(a, b, preferred_element_type=f32)

    def mix(stream):
        query, key, value = (whole(stream, part) for part in range(3))
        scores = dot(key, query.T)
        highest = jnp.max(scores, axis=0, keepdims=True)
        weights = jnp.exp2((scores - highest) * to_two)
        inverse = 1.0 / jnp.sum(weights, axis=0, keepdims=True)
        return dot(value.T, weights.astype(bf)) * inverse, weights, inverse

    real_out = mix(0)[0]
    fake_out, weights, inverse = mix(1)
    query, key, value = (whole(1, part) for part in range(3))
    differ = fake_out - real_out
    grad_out = (loss_weight * differ * lax.rsqrt(differ * differ + match_eps * match_eps)).astype(bf)
    deltas = jnp.sum(grad_out.astype(f32) * fake_out, axis=0, keepdims=True)
    probs = weights * inverse
    dscores = (probs * (dot(value, grad_out) - deltas)).astype(bf)

    def store(part, grad):
        o_ref[:, part] = grad.reshape(16, BLOCK, HEAD_DIM)

    store(0, (dot(key.T, dscores) * scale).astype(bf).T)
    store(1, (dot(dscores, query) * scale).astype(bf))
    store(2, dot(probs.astype(bf), grad_out.T).astype(bf))


def attention(received):
    return pl.pallas_call(
        attention_kernel,
        out_shape=jax.ShapeDtypeStruct((16, 3, BLOCK, HEAD_DIM), jnp.bfloat16),
        in_specs=[VMEM],
        out_specs=VMEM,
        cost_estimate=cost(11 * 1024 * 1024 * 256, 4 << 20),
        compiler_params=pltpu.CompilerParams(vmem_limit_bytes=36 << 20),
        name="attention",
    )(received)


HBM = pl.BlockSpec(memory_space=pltpu.HBM)
ANY = pl.BlockSpec(memory_space=pl.ANY)
SMEM = pl.BlockSpec(memory_space=pltpu.SMEM)
DMA = pltpu.SemaphoreType.DMA
COLUMNS = 2 * HEAD_DIM


def prepare_kernel(
    where_ref, real_ref, gen_ref, mod_ref, gain_ref, w_ref, sent_ref, tail_ref, oreal_ref, ofake_ref,
    real_buf, gen_buf, mod_buf, gain_buf, sems,
):
    f32, bf = jnp.float32, jnp.bfloat16
    place = pl.multiple_of(((where_ref[0] + 4) % 8) * PIECE, PIECE)
    tail = pl.multiple_of(SHARED + (where_ref[0] % 2) * TAIL, TAIL)
    copies = [
        pltpu.make_async_copy(gen_ref, gen_buf, sems.at[0]),
        pltpu.make_async_copy(real_ref, real_buf, sems.at[1]),
        pltpu.make_async_copy(mod_ref, mod_buf, sems.at[2]),
        pltpu.make_async_copy(gain_ref, gain_buf, sems.at[3]),
        pltpu.make_async_copy(w_ref.at[:, pl.ds(place, PIECE)], sent_ref, sems.at[4]),
        pltpu.make_async_copy(w_ref.at[:, pl.ds(tail, TAIL)], tail_ref, sems.at[5]),
    ]
    for copy in copies:
        copy.start()
    for copy in copies[:4]:
        copy.wait()
    gain = gain_buf[...]
    scale = 1.0 + mod_buf[0:1]
    shift = mod_buf[1:2]
    for r in range(0, BLOCK, 16):
        rows = slice(r, r + 16)
        fake = (gen_buf[rows].astype(f32) * scale + shift).astype(bf).astype(f32)
        for ref, values in ((oreal_ref, real_buf[rows].astype(f32)), (ofake_ref, fake)):
            inverse = lax.rsqrt(jnp.mean(values * values, axis=-1, keepdims=True) + norm_eps)
            ref[rows] = (values * inverse * gain).astype(bf)
    copies[4].wait()
    copies[5].wait()


def prepare(where, real, gen, modulation, gain, weight):
    bf, f32 = jnp.bfloat16, jnp.float32
    rows = jax.ShapeDtypeStruct((BLOCK, WIDTH), bf)
    return pl.pallas_call(
        prepare_kernel,
        out_shape=[jax.ShapeDtypeStruct((3, n, COLUMNS), bf) for n in (PIECE, TAIL)] + [rows, rows],
        in_specs=[SMEM] + [HBM] * 5,
        out_specs=[VMEM] * 4,
        scratch_shapes=[
            pltpu.VMEM((BLOCK, WIDTH), bf),
            pltpu.VMEM((BLOCK, WIDTH), bf),
            pltpu.VMEM((2, WIDTH), f32),
            pltpu.VMEM((1, WIDTH), f32),
            DMA((6,)),
        ],
        cost_estimate=cost(4 << 20, 3 << 20),
        compiler_params=limit(16),
        name="prepare",
    )(where, real, gen, modulation, gain, weight)


NEAR = (2, 3, 2, 3, BLOCK, HEAD_DIM)
SEND = (16, 2, 3, BLOCK, HEAD_DIM)


def near_kernel(*refs):
    row_refs, (w_ref, o_ref, held_ref, rows_ref, sems) = refs[:6], refs[6:]
    copies = [pltpu.make_async_copy(w_ref.at[q], held_ref.at[q], sems.at[q]) for q in range(3)]
    for copy in copies:
        copy.start()
    for i, ref in enumerate(row_refs):
        rows_ref[BLOCK * i : BLOCK * (i + 1)] = ref[...]
    for q in range(3):
        copies[q].wait()
        out = jnp.dot(rows_ref[...], held_ref[q], preferred_element_type=jnp.float32).astype(jnp.bfloat16)
        for k in range(2):
            for j in range(3):
                for s in range(2):
                    r = (2 * j + s) * BLOCK
                    o_ref[k, j, s, q] = out[r : r + BLOCK, HEAD_DIM * k : HEAD_DIM * (k + 1)]


def project_near(rows, weight):
    return pl.pallas_call(
        near_kernel,
        out_shape=[
            jax.ShapeDtypeStruct(NEAR, jnp.bfloat16),
            jax.ShapeDtypeStruct((3, WIDTH, COLUMNS), jnp.bfloat16),
        ],
        in_specs=[VMEM] * 6 + [HBM],
        out_specs=[VMEM] * 2,
        scratch_shapes=[pltpu.VMEM((6 * BLOCK, WIDTH), jnp.bfloat16), DMA((3,))],
        cost_estimate=cost(2 * 384 * 3072 * 768, 7 << 20),
        compiler_params=limit(16),
        name="project_near",
    )(*rows, weight)


def rest_kernel(*refs):
    where_ref, row_refs, near_ref, pieces, w_ref = refs[0], refs[1:9], refs[9], refs[10:20], refs[20]
    o_ref, other_ref, rows_ref = refs[21:]
    bf, f32 = jnp.bfloat16, jnp.float32
    where = where_ref[0]
    colour, core = where // 2, where % 2
    places = [
        (pl.multiple_of((((colour + c) % 4) * 2 + k) * PIECE, PIECE), PIECE) for k in (core, 1 - core) for c in (0, 3, 1, 2)
    ] + [(pl.multiple_of(SHARED + k * TAIL, TAIL), TAIL) for k in (core, 1 - core)]
    for i, ref in enumerate(row_refs):
        rows_ref[BLOCK * i : BLOCK * (i + 1)] = ref[...]
    for k in range(2):
        for j in range(3):
            o_ref[4 * k + j] = near_ref[k, j]
    for q in range(3):
        out = jnp.dot(rows_ref[6 * BLOCK :], w_ref[q], preferred_element_type=f32).astype(bf)
        for k in range(2):
            for s in range(2):
                o_ref[4 * k + 3, s, q] = out[BLOCK * s : BLOCK * (s + 1), HEAD_DIM * k : HEAD_DIM * (k + 1)]
        for i, piece in enumerate(pieces):
            other_ref[q, pl.ds(*places[i])] = piece[q]
        out = jnp.dot(rows_ref[...], other_ref[q], preferred_element_type=f32).astype(bf)
        for k in range(2):
            for j in range(4):
                for s in range(2):
                    r = (2 * j + s) * BLOCK
                    o_ref[4 * (2 + k) + j, s, q] = out[r : r + BLOCK, HEAD_DIM * k : HEAD_DIM * (k + 1)]


def project_rest(where, rows, near, pieces, weight):
    bf = jnp.bfloat16
    return pl.pallas_call(
        rest_kernel,
        out_shape=[jax.ShapeDtypeStruct(SEND, bf), jax.ShapeDtypeStruct((3, WIDTH, COLUMNS), bf)],
        in_specs=[SMEM] + [VMEM] * 20,
        out_specs=[VMEM] * 2,
        scratch_shapes=[pltpu.VMEM((8 * BLOCK, WIDTH), bf)],
        cost_estimate=cost(2 * 640 * 3072 * 768, 14 << 20),
        compiler_params=limit(16),
        name="project_rest",
    )(where, *rows, near, *pieces, weight)


CHUNK = 768


HALF_BLOCK = BLOCK // 2


def unproject_kernel(back_ref, own_ref, other_ref, own_out, below_ref, above_ref, *refs):
    far_up, far_down, near_up, near_down, grads_ref = refs
    bf, f32 = jnp.bfloat16, jnp.float32
    for p in range(2):
        for q in range(3):
            for k in range(2):
                d = 4 * (2 * p + k)
                c = ((3 * p + q) * 2 + k) * HEAD_DIM
                grads_ref[:, c : c + HEAD_DIM] = back_ref[d : d + 4, q].reshape(4 * BLOCK, HEAD_DIM)
    for n in range(0, WIDTH, CHUNK):
        total = None
        for p, ref in enumerate((own_ref, other_ref)):
            for q in range(3):
                c = (3 * p + q) * COLUMNS
                term = lax.dot_general(
                    grads_ref[:, c : c + COLUMNS],
                    ref[q, n : n + CHUNK],
                    (((1,), (1,)), ((), ())),
                    preferred_element_type=f32,
                )
                total = term if total is None else total + term
        columns = slice(n, n + CHUNK)
        parts = [total[HALF_BLOCK * i : HALF_BLOCK * (i + 1)] for i in range(8)]
        own_out[:, columns] = total[:BLOCK]
        near_down[:, columns] = parts[2].astype(bf)
        below_ref[:, columns] = parts[3]
        above_ref[:, columns] = parts[4]
        near_up[:, columns] = parts[5].astype(bf)
        far_up[:, columns] = parts[6].astype(bf)
        far_down[:, columns] = parts[7].astype(bf)


def unproject(back, weight, other):
    f32 = jnp.float32
    half = (HALF_BLOCK, WIDTH)
    return pl.pallas_call(
        unproject_kernel,
        out_shape=[jax.ShapeDtypeStruct((BLOCK, WIDTH), f32)]
        + [jax.ShapeDtypeStruct(half, f32)] * 2
        + [jax.ShapeDtypeStruct(half, jnp.bfloat16)] * 4,
        in_specs=[VMEM] * 3,
        out_specs=[VMEM] * 7,
        scratch_shapes=[pltpu.VMEM((4 * BLOCK, 12 * HEAD_DIM), jnp.bfloat16)],
        cost_estimate=cost(2 * 256 * 3072 * 1536, 12 << 20),
        compiler_params=limit(16),
        name="unproject",
    )(back, weight, other)


def pass_on_kernel(below_ref, above_ref, down_ref, up_ref, odown_ref, oup_ref):
    odown_ref[...] = (below_ref[...] + down_ref[...].astype(jnp.float32)).astype(jnp.bfloat16)
    oup_ref[...] = (above_ref[...] + up_ref[...].astype(jnp.float32)).astype(jnp.bfloat16)


def pass_on(below, above, from_up, from_down):
    return pl.pallas_call(
        pass_on_kernel,
        out_shape=[jax.ShapeDtypeStruct((HALF_BLOCK, WIDTH), jnp.bfloat16)] * 2,
        in_specs=[VMEM] * 4,
        out_specs=[VMEM] * 2,
        cost_estimate=cost(1 << 18, 2 << 20),
        compiler_params=limit(8),
        name="pass_on",
    )(below, above, from_up, from_down)


def finish_kernel(own_ref, a_ref, b_ref, c_ref, d_ref, gen_ref, mod_ref, gain_ref, o_ref):
    f32, bf = jnp.float32, jnp.bfloat16
    gain = gain_ref[...]
    scale = 1.0 + mod_ref[0:1]
    shift = mod_ref[1:2]
    for r in range(0, BLOCK, 16):
        rows = slice(r, r + 16)
        fake = (gen_ref[rows].astype(f32) * scale + shift).astype(bf).astype(f32)
        inverse = lax.rsqrt(jnp.mean(fake * fake, axis=-1, keepdims=True) + norm_eps)
        scaled = fake * inverse
        one, two = (a_ref, b_ref) if r < HALF_BLOCK else (c_ref, d_ref)
        part = slice(r % HALF_BLOCK, r % HALF_BLOCK + 16)
        grad = own_ref[rows] + one[part].astype(f32) + two[part].astype(f32)
        grad = grad * gain
        grad = inverse * (grad - scaled * jnp.mean(grad * scaled, axis=-1, keepdims=True))
        o_ref[rows] = (grad * scale).astype(bf)


def finish(own, parts, gen, modulation, gain):
    return pl.pallas_call(
        finish_kernel,
        out_shape=jax.ShapeDtypeStruct((BLOCK, WIDTH), jnp.bfloat16),
        in_specs=[VMEM] * 8,
        out_specs=VMEM,
        cost_estimate=cost(4 << 20, 3 << 20),
        compiler_params=limit(8),
        name="finish",
    )(own, *parts, gen, modulation, gain)


def on_device(real_tokens, gen_hidden, modulation, norm_gain, weight):
    return step(real_tokens[0], gen_hidden[0], modulation[0], norm_gain[None], weight)[None]


def in_hbm(x):
    return pltpu.with_memory_space_constraint(x, pltpu.HBM)


def step(real_tokens, gen_hidden, modulation, gain, weight):
    colour = (lax.axis_index("x") + 2 * lax.axis_index("zl")) % 4
    core = lax.axis_index("core")

    where = (colour * 2 + core).astype(jnp.int32)[None]
    sent, sent_tail, real, fake = prepare(
        where, in_hbm(real_tokens), in_hbm(gen_hidden), in_hbm(modulation), in_hbm(gain), in_hbm(weight)
    )
    mine = lax.ppermute(sent, ("zl", "zh"), ACROSS)
    tail = lax.ppermute(sent_tail, ("zl", "zh"), ACROSS)
    below_real = lax.ppermute(real, "y", ring(1))
    above_fake = lax.ppermute(fake, "y", ring(-1))
    below_fake = lax.ppermute(fake, "y", ring(1))
    above_real = lax.ppermute(real, "y", ring(-1))
    far_real = lax.ppermute(below_real, "y", ring(1))
    far_fake = lax.ppermute(above_fake, "y", ring(-1))
    pieces = [
        mine, lax.ppermute(mine, "x", ring(1)), lax.ppermute(mine, "x", ring(-1)), lax.ppermute(mine, "zl", swap())
    ]
    pieces = pieces + [lax.ppermute(p, "core", swap()) for p in pieces]
    pieces += [tail, lax.ppermute(tail, "core", swap())]

    near_rows = [real, fake, below_real, below_fake, above_real, above_fake]
    near, held = project_near(near_rows, in_hbm(weight))
    pieces = [pltpu.with_memory_space_constraint(p, pltpu.VMEM) for p in pieces]
    send, other = project_rest(where, near_rows + [far_real, far_fake], near, pieces, held)
    received = lax.all_to_all(send.reshape(16, 6 * BLOCK, HEAD_DIM), SEQ, split_axis=0, concat_axis=0, tiled=True)
    grads = attention(received.reshape(SEND))
    back = lax.all_to_all(grads.reshape(16, 3 * BLOCK, HEAD_DIM), SEQ, split_axis=0, concat_axis=0, tiled=True)
    own, below, above, far_up, far_down, near_up, near_down = unproject(
        back.reshape(16, 3, BLOCK, HEAD_DIM), held, other
    )
    got_up = lax.ppermute(far_up, "y", ring(1))
    got_down = lax.ppermute(far_down, "y", ring(-1))
    low_near = lax.ppermute(near_down, "y", ring(-1))
    high_near = lax.ppermute(near_up, "y", ring(1))
    sum_down, sum_up = pass_on(below, above, got_down, got_up)
    low_sum = lax.ppermute(sum_up, "y", ring(1))
    high_sum = lax.ppermute(sum_down, "y", ring(-1))
    return finish(own, (low_sum, low_near, high_near, high_sum), gen_hidden, modulation, gain)


def solution(mesh):
    torus = Mesh(mesh.devices.reshape(2, 4, 2, 2, 4), ("zl", "x", "core", "zh", "y"))
    fsdp = ("zh", "y")
    in_specs = (
        P(fsdp, SEQ, None),
        P(fsdp, SEQ, None),
        P(fsdp, None, None),
        P(),
        P(None, None, fsdp),
    )
    return jax.shard_map(on_device, mesh=torus, in_specs=in_specs, out_specs=P(fsdp, SEQ, None), check_vma=False)
```

```python
import jax
import jax.numpy as jnp
from jax import lax
from jax.experimental import pallas as pl
from jax.experimental.pallas import tpu as pltpu
from jax.sharding import Mesh
from jax.sharding import PartitionSpec as P


HEAD_DIM = 128
WIDTH = 3072
BLOCK = 64
PIECE = 288
SHARED = 8 * PIECE
TAIL = (WIDTH - SHARED) // 2

norm_eps = 1e-06
match_eps = 0.05
loss_weight = 4.0


SEQ = ("zl", "x", "core")
ACROSS = [(0, 3), (3, 0), (1, 2), (2, 1)]


VMEM = pl.BlockSpec(memory_space=pltpu.VMEM)


def cost(flops, touched):
    return pl.CostEstimate(flops=flops, bytes_accessed=touched, transcendentals=0)


def limit(mib=24):
    return pltpu.CompilerParams(vmem_limit_bytes=mib * 1024 * 1024)


def ring(step):
    return [(i, (i + step) % 4) for i in range(4)]


def swap():
    return [(0, 1), (1, 0)]


def attention_kernel(index_ref, *refs):
    blocks, o_ref = refs[:16], refs[16]
    bf = jnp.bfloat16
    f32 = jnp.float32
    scale = HEAD_DIM ** (-0.5)
    to_two = scale * 1.4426950408889634

    def whole(stream, part):
        return jnp.concatenate([block[stream, part] for block in blocks], axis=0)

    def dot(a, b):
        return jnp.dot(a, b, preferred_element_type=f32)

    def mix(stream):
        query, key, value = (whole(stream, part) for part in range(3))
        scores = dot(key, query.T)
        highest = jnp.max(scores, axis=0, keepdims=True)
        weights = jnp.exp2((scores - highest) * to_two)
        inverse = 1.0 / jnp.sum(weights, axis=0, keepdims=True)
        return dot(value.T, weights.astype(bf)) * inverse, weights, inverse

    real_out = mix(0)[0]
    fake_out, weights, inverse = mix(1)
    query, key, value = (whole(1, part) for part in range(3))
    differ = fake_out - real_out
    grad_out = (loss_weight * differ * lax.rsqrt(differ * differ + match_eps * match_eps)).astype(bf)
    deltas = jnp.sum(grad_out.astype(f32) * fake_out, axis=0, keepdims=True)
    probs = weights * inverse
    dscores = (probs * (dot(value, grad_out) - deltas)).astype(bf)

    def store(part, grad):
        for r in range(16):
            o_ref[jnp.bitwise_xor(index_ref[0], r), part] = grad[BLOCK * r : BLOCK * (r + 1)]

    store(0, (dot(key.T, dscores) * scale).astype(bf).T)
    store(1, (dot(dscores, query) * scale).astype(bf))
    store(2, dot(probs.astype(bf), grad_out.T).astype(bf))


def attention(index, blocks):
    return pl.pallas_call(
        attention_kernel,
        out_shape=jax.ShapeDtypeStruct((16, 3, BLOCK, HEAD_DIM), jnp.bfloat16),
        in_specs=[SMEM] + [VMEM] * 16,
        out_specs=VMEM,
        cost_estimate=cost(11 * 1024 * 1024 * 256, 4 << 20),
        compiler_params=pltpu.CompilerParams(vmem_limit_bytes=36 << 20),
        name="attention",
    )(index, *blocks)


HBM = pl.BlockSpec(memory_space=pltpu.HBM)
ANY = pl.BlockSpec(memory_space=pl.ANY)
SMEM = pl.BlockSpec(memory_space=pltpu.SMEM)
DMA = pltpu.SemaphoreType.DMA
COLUMNS = 2 * HEAD_DIM


def colour_and_core(index):
    return ((index // 2) % 4 + 2 * (index // 8)) % 4, index % 2


def prepare_kernel(
    index_ref, real_ref, gen_ref, mod_ref, gain_ref, w_ref, sent_ref, tail_ref, oreal_ref, ofake_ref,
    real_buf, gen_buf, mod_buf, gain_buf, sems,
):
    f32, bf = jnp.float32, jnp.bfloat16
    colour, core = colour_and_core(index_ref[0])
    place = pl.multiple_of((((colour + 2) % 4) * 2 + core) * PIECE, PIECE)
    tail = pl.multiple_of(SHARED + core * TAIL, TAIL)
    copies = [
        pltpu.make_async_copy(gen_ref, gen_buf, sems.at[0]),
        pltpu.make_async_copy(real_ref, real_buf, sems.at[1]),
        pltpu.make_async_copy(mod_ref, mod_buf, sems.at[2]),
        pltpu.make_async_copy(gain_ref, gain_buf, sems.at[3]),
        pltpu.make_async_copy(w_ref.at[:, pl.ds(place, PIECE)], sent_ref, sems.at[4]),
        pltpu.make_async_copy(w_ref.at[:, pl.ds(tail, TAIL)], tail_ref, sems.at[5]),
    ]
    for copy in copies:
        copy.start()
    for copy in copies[:4]:
        copy.wait()
    gain = gain_buf[...]
    scale = 1.0 + mod_buf[0:1]
    shift = mod_buf[1:2]
    for r in range(0, BLOCK, 16):
        rows = slice(r, r + 16)
        fake = (gen_buf[rows].astype(f32) * scale + shift).astype(bf).astype(f32)
        for ref, values in ((oreal_ref, real_buf[rows].astype(f32)), (ofake_ref, fake)):
            inverse = lax.rsqrt(jnp.mean(values * values, axis=-1, keepdims=True) + norm_eps)
            ref[rows] = (values * inverse * gain).astype(bf)
    copies[4].wait()
    copies[5].wait()


def prepare(index, real, gen, modulation, gain, weight):
    bf, f32 = jnp.bfloat16, jnp.float32
    rows = jax.ShapeDtypeStruct((BLOCK, WIDTH), bf)
    return pl.pallas_call(
        prepare_kernel,
        out_shape=[jax.ShapeDtypeStruct((3, n, COLUMNS), bf) for n in (PIECE, TAIL)] + [rows, rows],
        in_specs=[SMEM] + [HBM] * 5,
        out_specs=[VMEM] * 4,
        scratch_shapes=[
            pltpu.VMEM((BLOCK, WIDTH), bf),
            pltpu.VMEM((BLOCK, WIDTH), bf),
            pltpu.VMEM((2, WIDTH), f32),
            pltpu.VMEM((1, WIDTH), f32),
            DMA((6,)),
        ],
        cost_estimate=cost(4 << 20, 3 << 20),
        compiler_params=limit(16),
        name="prepare",
    )(index, real, gen, modulation, gain, weight)


NEAR = (2, 3, 2, 3, BLOCK, HEAD_DIM)
SEND = (16, 2, 3, BLOCK, HEAD_DIM)


def near_kernel(*refs):
    row_refs, (w_ref, o_ref, held_ref, rows_ref, sems) = refs[:6], refs[6:]
    copies = [pltpu.make_async_copy(w_ref.at[q], held_ref.at[q], sems.at[q]) for q in range(3)]
    for copy in copies:
        copy.start()
    for i, ref in enumerate(row_refs):
        rows_ref[BLOCK * i : BLOCK * (i + 1)] = ref[...]
    for q in range(3):
        copies[q].wait()
        out = jnp.dot(rows_ref[...], held_ref[q], preferred_element_type=jnp.float32).astype(jnp.bfloat16)
        for k in range(2):
            for j in range(3):
                for s in range(2):
                    r = (2 * j + s) * BLOCK
                    o_ref[k, j, s, q] = out[r : r + BLOCK, HEAD_DIM * k : HEAD_DIM * (k + 1)]


def project_near(rows, weight):
    return pl.pallas_call(
        near_kernel,
        out_shape=[
            jax.ShapeDtypeStruct(NEAR, jnp.bfloat16),
            jax.ShapeDtypeStruct((3, WIDTH, COLUMNS), jnp.bfloat16),
        ],
        in_specs=[VMEM] * 6 + [HBM],
        out_specs=[VMEM] * 2,
        scratch_shapes=[pltpu.VMEM((6 * BLOCK, WIDTH), jnp.bfloat16), DMA((3,))],
        cost_estimate=cost(2 * 384 * 3072 * 768, 7 << 20),
        compiler_params=limit(16),
        name="project_near",
    )(*rows, weight)


def rest_kernel(*refs):
    index_ref, row_refs, near_ref, pieces, w_ref = refs[0], refs[1:9], refs[9], refs[10:20], refs[20]
    blocks, other_ref, rows_ref, o_ref = refs[21:37], refs[37], refs[38], refs[39]
    bf, f32 = jnp.bfloat16, jnp.float32
    index = index_ref[0]
    colour, core = colour_and_core(index)
    places = [
        (pl.multiple_of((((colour + c) % 4) * 2 + k) * PIECE, PIECE), PIECE) for k in (core, 1 - core) for c in (0, 3, 1, 2)
    ] + [(pl.multiple_of(SHARED + k * TAIL, TAIL), TAIL) for k in (core, 1 - core)]
    for i, ref in enumerate(row_refs):
        rows_ref[BLOCK * i : BLOCK * (i + 1)] = ref[...]
    for k in range(2):
        for j in range(3):
            o_ref[4 * k + j] = near_ref[k, j]
    for q in range(3):
        out = jnp.dot(rows_ref[6 * BLOCK :], w_ref[q], preferred_element_type=f32).astype(bf)
        for k in range(2):
            for s in range(2):
                o_ref[4 * k + 3, s, q] = out[BLOCK * s : BLOCK * (s + 1), HEAD_DIM * k : HEAD_DIM * (k + 1)]
        for i, piece in enumerate(pieces):
            other_ref[q, pl.ds(*places[i])] = piece[q]
        out = jnp.dot(rows_ref[...], other_ref[q], preferred_element_type=f32).astype(bf)
        for k in range(2):
            for j in range(4):
                for s in range(2):
                    r = (2 * j + s) * BLOCK
                    o_ref[4 * (2 + k) + j, s, q] = out[r : r + BLOCK, HEAD_DIM * k : HEAD_DIM * (k + 1)]
    for r, block in enumerate(blocks):
        block[...] = o_ref[jnp.bitwise_xor(index, r)]


def project_rest(index, rows, near, pieces, weight):
    bf = jnp.bfloat16
    return pl.pallas_call(
        rest_kernel,
        out_shape=[jax.ShapeDtypeStruct(SEND[1:], bf)] * 16 + [jax.ShapeDtypeStruct((3, WIDTH, COLUMNS), bf)],
        in_specs=[SMEM] + [VMEM] * 20,
        out_specs=[VMEM] * 17,
        scratch_shapes=[pltpu.VMEM((8 * BLOCK, WIDTH), bf), pltpu.VMEM(SEND, bf)],
        cost_estimate=cost(2 * 640 * 3072 * 768, 14 << 20),
        compiler_params=limit(16),
        name="project_rest",
    )(index, *rows, near, *pieces, weight)


CHUNK = 768


HALF_BLOCK = BLOCK // 2


def unproject_kernel(back_ref, own_ref, other_ref, own_out, below_ref, above_ref, *refs):
    far_up, far_down, near_up, near_down, grads_ref = refs
    bf, f32 = jnp.bfloat16, jnp.float32
    for p in range(2):
        for q in range(3):
            for k in range(2):
                d = 4 * (2 * p + k)
                c = ((3 * p + q) * 2 + k) * HEAD_DIM
                grads_ref[:, c : c + HEAD_DIM] = back_ref[d : d + 4, q].reshape(4 * BLOCK, HEAD_DIM)
    for n in range(0, WIDTH, CHUNK):
        total = None
        for p, ref in enumerate((own_ref, other_ref)):
            for q in range(3):
                c = (3 * p + q) * COLUMNS
                term = lax.dot_general(
                    grads_ref[:, c : c + COLUMNS],
                    ref[q, n : n + CHUNK],
                    (((1,), (1,)), ((), ())),
                    preferred_element_type=f32,
                )
                total = term if total is None else total + term
        columns = slice(n, n + CHUNK)
        parts = [total[HALF_BLOCK * i : HALF_BLOCK * (i + 1)] for i in range(8)]
        own_out[:, columns] = total[:BLOCK]
        near_down[:, columns] = parts[2].astype(bf)
        below_ref[:, columns] = parts[3]
        above_ref[:, columns] = parts[4]
        near_up[:, columns] = parts[5].astype(bf)
        far_up[:, columns] = parts[6].astype(bf)
        far_down[:, columns] = parts[7].astype(bf)


def unproject(back, weight, other):
    f32 = jnp.float32
    half = (HALF_BLOCK, WIDTH)
    return pl.pallas_call(
        unproject_kernel,
        out_shape=[jax.ShapeDtypeStruct((BLOCK, WIDTH), f32)]
        + [jax.ShapeDtypeStruct(half, f32)] * 2
        + [jax.ShapeDtypeStruct(half, jnp.bfloat16)] * 4,
        in_specs=[VMEM] * 3,
        out_specs=[VMEM] * 7,
        scratch_shapes=[pltpu.VMEM((4 * BLOCK, 12 * HEAD_DIM), jnp.bfloat16)],
        cost_estimate=cost(2 * 256 * 3072 * 1536, 12 << 20),
        compiler_params=limit(16),
        name="unproject",
    )(back, weight, other)


def pass_on_kernel(below_ref, above_ref, down_ref, up_ref, odown_ref, oup_ref):
    odown_ref[...] = (below_ref[...] + down_ref[...].astype(jnp.float32)).astype(jnp.bfloat16)
    oup_ref[...] = (above_ref[...] + up_ref[...].astype(jnp.float32)).astype(jnp.bfloat16)


def pass_on(below, above, from_up, from_down):
    return pl.pallas_call(
        pass_on_kernel,
        out_shape=[jax.ShapeDtypeStruct((HALF_BLOCK, WIDTH), jnp.bfloat16)] * 2,
        in_specs=[VMEM] * 4,
        out_specs=[VMEM] * 2,
        cost_estimate=cost(1 << 18, 2 << 20),
        compiler_params=limit(8),
        name="pass_on",
    )(below, above, from_up, from_down)


def finish_kernel(own_ref, a_ref, b_ref, c_ref, d_ref, gen_ref, mod_ref, gain_ref, o_ref):
    f32, bf = jnp.float32, jnp.bfloat16
    gain = gain_ref[...]
    scale = 1.0 + mod_ref[0:1]
    shift = mod_ref[1:2]
    for r in range(0, BLOCK, 16):
        rows = slice(r, r + 16)
        fake = (gen_ref[rows].astype(f32) * scale + shift).astype(bf).astype(f32)
        inverse = lax.rsqrt(jnp.mean(fake * fake, axis=-1, keepdims=True) + norm_eps)
        scaled = fake * inverse
        one, two = (a_ref, b_ref) if r < HALF_BLOCK else (c_ref, d_ref)
        part = slice(r % HALF_BLOCK, r % HALF_BLOCK + 16)
        grad = own_ref[rows] + one[part].astype(f32) + two[part].astype(f32)
        grad = grad * gain
        grad = inverse * (grad - scaled * jnp.mean(grad * scaled, axis=-1, keepdims=True))
        o_ref[rows] = (grad * scale).astype(bf)


def finish(own, parts, gen, modulation, gain):
    return pl.pallas_call(
        finish_kernel,
        out_shape=jax.ShapeDtypeStruct((BLOCK, WIDTH), jnp.bfloat16),
        in_specs=[VMEM] * 8,
        out_specs=VMEM,
        cost_estimate=cost(4 << 20, 3 << 20),
        compiler_params=limit(8),
        name="finish",
    )(own, *parts, gen, modulation, gain)


def on_device(real_tokens, gen_hidden, modulation, norm_gain, weight):
    return step(real_tokens[0], gen_hidden[0], modulation[0], norm_gain[None], weight)[None]


def in_hbm(x):
    return pltpu.with_memory_space_constraint(x, pltpu.HBM)


def step(real_tokens, gen_hidden, modulation, gain, weight):
    index = lax.axis_index(SEQ).astype(jnp.int32)[None]

    sent, sent_tail, real, fake = prepare(
        index, in_hbm(real_tokens), in_hbm(gen_hidden), in_hbm(modulation), in_hbm(gain), in_hbm(weight)
    )
    mine = lax.ppermute(sent, ("zl", "zh"), ACROSS)
    tail = lax.ppermute(sent_tail, ("zl", "zh"), ACROSS)
    below_real = lax.ppermute(real, "y", ring(1))
    above_fake = lax.ppermute(fake, "y", ring(-1))
    below_fake = lax.ppermute(fake, "y", ring(1))
    above_real = lax.ppermute(real, "y", ring(-1))
    far_real = lax.ppermute(below_real, "y", ring(1))
    far_fake = lax.ppermute(above_fake, "y", ring(-1))
    pieces = [
        mine, lax.ppermute(mine, "x", ring(1)), lax.ppermute(mine, "x", ring(-1)), lax.ppermute(mine, "zl", swap())
    ]
    pieces = pieces + [lax.ppermute(p, "core", swap()) for p in pieces]
    pieces += [tail, lax.ppermute(tail, "core", swap())]

    near_rows = [real, fake, below_real, below_fake, above_real, above_fake]
    near, held = project_near(near_rows, in_hbm(weight))
    pieces = [pltpu.with_memory_space_constraint(p, pltpu.VMEM) for p in pieces]
    *blocks, other = project_rest(index, near_rows + [far_real, far_fake], near, pieces, held)
    for r in range(1, 16):
        blocks[r] = lax.ppermute(blocks[r], SEQ, [(i, i ^ r) for i in range(16)])
    grads = attention(index, blocks)
    back = lax.all_to_all(grads.reshape(16, 3 * BLOCK, HEAD_DIM), SEQ, split_axis=0, concat_axis=0, tiled=True)
    own, below, above, far_up, far_down, near_up, near_down = unproject(
        back.reshape(16, 3, BLOCK, HEAD_DIM), held, other
    )
    got_up = lax.ppermute(far_up, "y", ring(1))
    got_down = lax.ppermute(far_down, "y", ring(-1))
    low_near = lax.ppermute(near_down, "y", ring(-1))
    high_near = lax.ppermute(near_up, "y", ring(1))
    sum_down, sum_up = pass_on(below, above, got_down, got_up)
    low_sum = lax.ppermute(sum_up, "y", ring(1))
    high_sum = lax.ppermute(sum_down, "y", ring(-1))
    return finish(own, (low_sum, low_near, high_near, high_sum), gen_hidden, modulation, gain)


def solution(mesh):
    torus = Mesh(mesh.devices.reshape(2, 4, 2, 2, 4), ("zl", "x", "core", "zh", "y"))
    fsdp = ("zh", "y")
    in_specs = (
        P(fsdp, SEQ, None),
        P(fsdp, SEQ, None),
        P(fsdp, None, None),
        P(),
        P(None, None, fsdp),
    )
    return jax.shard_map(on_device, mesh=torus, in_specs=in_specs, out_specs=P(fsdp, SEQ, None), check_vma=False)
```

```python
import jax
import jax.numpy as jnp
from jax import lax
from jax.experimental import pallas as pl
from jax.experimental.pallas import tpu as pltpu
from jax.sharding import Mesh
from jax.sharding import PartitionSpec as P


HEAD_DIM = 128
WIDTH = 3072
BLOCK = 64
PIECE = 288
SHARED = 8 * PIECE
TAIL = (WIDTH - SHARED) // 2

norm_eps = 1e-06
match_eps = 0.05
loss_weight = 4.0


SEQ = ("zl", "x", "core")
ACROSS = [(0, 3), (3, 0), (1, 2), (2, 1)]


VMEM = pl.BlockSpec(memory_space=pltpu.VMEM)


def cost(flops, touched):
    return pl.CostEstimate(flops=flops, bytes_accessed=touched, transcendentals=0)


def limit(mib=24):
    return pltpu.CompilerParams(vmem_limit_bytes=mib * 1024 * 1024)


def ring(step):
    return [(i, (i + step) % 4) for i in range(4)]


def swap():
    return [(0, 1), (1, 0)]


def attention_kernel(x_ref, o_ref):
    bf = jnp.bfloat16
    f32 = jnp.float32
    length = 16 * BLOCK
    scale = HEAD_DIM ** (-0.5)
    to_two = scale * 1.4426950408889634

    def whole(stream, part):
        return x_ref[:, stream, part].reshape(length, HEAD_DIM)

    def dot(a, b):
        return jnp.dot(a, b, preferred_element_type=f32)

    def mix(stream):
        query, key, value = (whole(stream, part) for part in range(3))
        scores = dot(key, query.T)
        highest = jnp.max(scores, axis=0, keepdims=True)
        weights = jnp.exp2((scores - highest) * to_two)
        inverse = 1.0 / jnp.sum(weights, axis=0, keepdims=True)
        return dot(value.T, weights.astype(bf)) * inverse, weights, inverse

    real_out = mix(0)[0]
    fake_out, weights, inverse = mix(1)
    query, key, value = (whole(1, part) for part in range(3))
    differ = fake_out - real_out
    grad_out = (loss_weight * differ * lax.rsqrt(differ * differ + match_eps * match_eps)).astype(bf)
    deltas = jnp.sum(grad_out.astype(f32) * fake_out, axis=0, keepdims=True)
    probs = weights * inverse
    dscores = (probs * (dot(value, grad_out) - deltas)).astype(bf)

    def store(part, grad):
        o_ref[:, part] = grad.reshape(16, BLOCK, HEAD_DIM)

    store(0, (dot(key.T, dscores) * scale).astype(bf).T)
    store(1, (dot(dscores, query) * scale).astype(bf))
    store(2, dot(probs.astype(bf), grad_out.T).astype(bf))


def attention(received):
    return pl.pallas_call(
        attention_kernel,
        out_shape=jax.ShapeDtypeStruct((16, 3, BLOCK, HEAD_DIM), jnp.bfloat16),
        in_specs=[VMEM],
        out_specs=VMEM,
        cost_estimate=cost(11 * 1024 * 1024 * 256, 4 << 20),
        compiler_params=pltpu.CompilerParams(vmem_limit_bytes=36 << 20),
        name="attention",
    )(received)


HBM = pl.BlockSpec(memory_space=pltpu.HBM)
ANY = pl.BlockSpec(memory_space=pl.ANY)
SMEM = pl.BlockSpec(memory_space=pltpu.SMEM)
DMA = pltpu.SemaphoreType.DMA
COLUMNS = 2 * HEAD_DIM


def prepare_kernel(
    where_ref, real_ref, gen_ref, mod_ref, gain_ref, w_ref, sent_ref, tail_ref, oreal_ref, ofake_ref,
    real_buf, gen_buf, mod_buf, gain_buf, sems,
):
    f32, bf = jnp.float32, jnp.bfloat16
    place = pl.multiple_of(((where_ref[0] + 4) % 8) * PIECE, PIECE)
    tail = pl.multiple_of(SHARED + (where_ref[0] % 2) * TAIL, TAIL)
    copies = [
        pltpu.make_async_copy(gen_ref, gen_buf, sems.at[0]),
        pltpu.make_async_copy(real_ref, real_buf, sems.at[1]),
        pltpu.make_async_copy(mod_ref, mod_buf, sems.at[2]),
        pltpu.make_async_copy(gain_ref, gain_buf, sems.at[3]),
        pltpu.make_async_copy(w_ref.at[:, pl.ds(place, PIECE)], sent_ref, sems.at[4]),
        pltpu.make_async_copy(w_ref.at[:, pl.ds(tail, TAIL)], tail_ref, sems.at[5]),
    ]
    for copy in copies:
        copy.start()
    for copy in copies[:4]:
        copy.wait()
    gain = gain_buf[...]
    scale = 1.0 + mod_buf[0:1]
    shift = mod_buf[1:2]
    for r in range(0, BLOCK, 16):
        rows = slice(r, r + 16)
        fake = (gen_buf[rows].astype(f32) * scale + shift).astype(bf).astype(f32)
        for ref, values in ((oreal_ref, real_buf[rows].astype(f32)), (ofake_ref, fake)):
            inverse = lax.rsqrt(jnp.mean(values * values, axis=-1, keepdims=True) + norm_eps)
            ref[rows] = (values * inverse * gain).astype(bf)
    copies[4].wait()
    copies[5].wait()


def prepare(where, real, gen, modulation, gain, weight):
    bf, f32 = jnp.bfloat16, jnp.float32
    rows = jax.ShapeDtypeStruct((BLOCK, WIDTH), bf)
    return pl.pallas_call(
        prepare_kernel,
        out_shape=[jax.ShapeDtypeStruct((3, n, COLUMNS), bf) for n in (PIECE, TAIL)] + [rows, rows],
        in_specs=[SMEM] + [HBM] * 5,
        out_specs=[VMEM] * 4,
        scratch_shapes=[
            pltpu.VMEM((BLOCK, WIDTH), bf),
            pltpu.VMEM((BLOCK, WIDTH), bf),
            pltpu.VMEM((2, WIDTH), f32),
            pltpu.VMEM((1, WIDTH), f32),
            DMA((6,)),
        ],
        cost_estimate=cost(4 << 20, 3 << 20),
        compiler_params=limit(16),
        name="prepare",
    )(where, real, gen, modulation, gain, weight)


NEAR = (2, 3, 2, 3, BLOCK, HEAD_DIM)
SEND = (16, 2, 3, BLOCK, HEAD_DIM)


def load_kernel(w_ref, o_ref, sems):
    copies = [pltpu.make_async_copy(w_ref.at[q], o_ref.at[q], sems.at[q]) for q in range(3)]
    for copy in copies:
        copy.start()
    for copy in copies:
        copy.wait()


def load(weight):
    return pl.pallas_call(
        load_kernel,
        out_shape=jax.ShapeDtypeStruct((3, WIDTH, COLUMNS), jnp.bfloat16),
        in_specs=[HBM],
        out_specs=VMEM,
        scratch_shapes=[DMA((3,))],
        cost_estimate=cost(0, 9 << 20),
        compiler_params=limit(4),
        name="load",
    )(weight)


def near_kernel(*refs):
    row_refs, (w_ref, o_ref, rows_ref) = refs[:6], refs[6:]
    for i, ref in enumerate(row_refs):
        rows_ref[BLOCK * i : BLOCK * (i + 1)] = ref[...]
    for q in range(3):
        out = jnp.dot(rows_ref[...], w_ref[q], preferred_element_type=jnp.float32).astype(jnp.bfloat16)
        for k in range(2):
            for j in range(3):
                for s in range(2):
                    r = (2 * j + s) * BLOCK
                    o_ref[k, j, s, q] = out[r : r + BLOCK, HEAD_DIM * k : HEAD_DIM * (k + 1)]


def project_near(rows, weight):
    return pl.pallas_call(
        near_kernel,
        out_shape=[
            jax.ShapeDtypeStruct(NEAR, jnp.bfloat16),
            jax.ShapeDtypeStruct((6 * BLOCK, WIDTH), jnp.bfloat16),
        ],
        in_specs=[VMEM] * 7,
        out_specs=[VMEM] * 2,
        cost_estimate=cost(2 * 384 * 3072 * 768, 7 << 20),
        compiler_params=limit(8),
        name="project_near",
    )(*rows, weight)


def pack_kernel(a_ref, b_ref, c_ref, o_ref):
    for i, ref in enumerate((a_ref, b_ref, c_ref)):
        o_ref[i] = ref[...]


def pack(pieces):
    return pl.pallas_call(
        pack_kernel,
        out_shape=jax.ShapeDtypeStruct((3, 3, PIECE, COLUMNS), jnp.bfloat16),
        in_specs=[VMEM] * 3,
        out_specs=VMEM,
        cost_estimate=cost(0, 3 << 20),
        compiler_params=limit(4),
        name="pack",
    )(*pieces)


def far_kernel(near_ref, rows_ref, real_ref, fake_ref, w_ref, o_ref, all_ref):
    bf, f32 = jnp.bfloat16, jnp.float32
    all_ref[: 6 * BLOCK] = rows_ref[...]
    all_ref[6 * BLOCK : 7 * BLOCK] = real_ref[...]
    all_ref[7 * BLOCK :] = fake_ref[...]
    for k in range(2):
        for j in range(3):
            o_ref[4 * k + j] = near_ref[k, j]
    for q in range(3):
        out = jnp.dot(all_ref[6 * BLOCK :], w_ref[q], preferred_element_type=f32).astype(bf)
        for k in range(2):
            for s in range(2):
                o_ref[4 * k + 3, s, q] = out[BLOCK * s : BLOCK * (s + 1), HEAD_DIM * k : HEAD_DIM * (k + 1)]


def project_far(near, rows, far_real, far_fake, weight):
    bf = jnp.bfloat16
    return pl.pallas_call(
        far_kernel,
        out_shape=[jax.ShapeDtypeStruct((8, *SEND[1:]), bf), jax.ShapeDtypeStruct((8 * BLOCK, WIDTH), bf)],
        in_specs=[VMEM] * 5,
        out_specs=[VMEM] * 2,
        cost_estimate=cost(2 * 128 * 3072 * 768, 10 << 20),
        compiler_params=limit(8),
        name="project_far",
    )(near, rows, far_real, far_fake, weight)


def rest_kernel(index_ref, half_ref, rows_ref, *refs):
    singles, packed, (o_ref, other_ref) = refs[:7], refs[7], refs[8:]
    bf, f32 = jnp.bfloat16, jnp.float32
    colour, core = index_ref[0] // 2, index_ref[0] % 2

    def shared(c, k):
        return pl.ds(pl.multiple_of((((colour + c) % 4) * 2 + k) * PIECE, PIECE), PIECE)

    def tail(k):
        return pl.ds(pl.multiple_of(SHARED + k * TAIL, TAIL), TAIL)

    partner = 1 - core
    places = [shared(c, core) for c in (0, 3, 1, 2)] + [tail(core), shared(0, partner), tail(partner)]
    o_ref[:8] = half_ref[...]
    for q in range(3):
        for place, piece in zip(places, singles):
            other_ref[q, place] = piece[q]
        for i, c in enumerate((3, 1, 2)):
            other_ref[q, shared(c, partner)] = packed[i, q]
        out = jnp.dot(rows_ref[...], other_ref[q], preferred_element_type=f32).astype(bf)
        for k in range(2):
            for j in range(4):
                for s in range(2):
                    r = (2 * j + s) * BLOCK
                    o_ref[4 * (2 + k) + j, s, q] = out[r : r + BLOCK, HEAD_DIM * k : HEAD_DIM * (k + 1)]


def project_rest(index, half, rows, pieces):
    bf = jnp.bfloat16
    return pl.pallas_call(
        rest_kernel,
        out_shape=[jax.ShapeDtypeStruct(SEND, bf), jax.ShapeDtypeStruct((3, WIDTH, COLUMNS), bf)],
        in_specs=[SMEM] + [VMEM] * 10,
        out_specs=[VMEM] * 2,
        cost_estimate=cost(2 * 512 * 3072 * 768, 14 << 20),
        compiler_params=limit(8),
        name="project_rest",
    )(index, half, rows, *pieces)


CHUNK = 768


HALF_BLOCK = BLOCK // 2


def unproject_rows(first, last, back_ref, own_ref, other_ref, grads_ref, store):
    count = last - first
    for p in range(2):
        for q in range(3):
            for k in range(2):
                d = 4 * (2 * p + k)
                c = ((3 * p + q) * 2 + k) * HEAD_DIM
                grads_ref[:, c : c + HEAD_DIM] = back_ref[d + first : d + last, q].reshape(count * BLOCK, HEAD_DIM)
    for n in range(0, WIDTH, CHUNK):
        total = None
        for p, ref in enumerate((own_ref, other_ref)):
            for q in range(3):
                c = (3 * p + q) * COLUMNS
                term = lax.dot_general(
                    grads_ref[:, c : c + COLUMNS],
                    ref[q, n : n + CHUNK],
                    (((1,), (1,)), ((), ())),
                    preferred_element_type=jnp.float32,
                )
                total = term if total is None else total + term
        store(slice(n, n + CHUNK), total)


def unproject_far_kernel(back_ref, own_ref, other_ref, up_ref, down_ref, grads_ref):
    def store(columns, total):
        up_ref[:, columns] = total[:HALF_BLOCK].astype(jnp.bfloat16)
        down_ref[:, columns] = total[HALF_BLOCK:].astype(jnp.bfloat16)

    unproject_rows(3, 4, back_ref, own_ref, other_ref, grads_ref, store)


def unproject_near_kernel(
    back_ref, own_ref, other_ref, own_out, below_ref, above_ref, up_ref, down_ref, grads_ref
):
    def store(columns, total):
        parts = [total[HALF_BLOCK * i : HALF_BLOCK * (i + 1)] for i in range(6)]
        own_out[:, columns] = total[:BLOCK]
        down_ref[:, columns] = parts[2].astype(jnp.bfloat16)
        below_ref[:, columns] = parts[3]
        above_ref[:, columns] = parts[4]
        up_ref[:, columns] = parts[5].astype(jnp.bfloat16)

    unproject_rows(0, 3, back_ref, own_ref, other_ref, grads_ref, store)


def unproject(kernel, blocks, shapes, back, weight, other):
    return pl.pallas_call(
        kernel,
        out_shape=shapes,
        in_specs=[VMEM] * 3,
        out_specs=[VMEM] * len(shapes),
        scratch_shapes=[pltpu.VMEM((blocks * BLOCK, 12 * HEAD_DIM), jnp.bfloat16)],
        cost_estimate=cost(2 * blocks * BLOCK * 3072 * 1536, 12 << 20),
        compiler_params=limit(16),
    )(back, weight, other)


def unproject_far(back, weight, other):
    half = jax.ShapeDtypeStruct((HALF_BLOCK, WIDTH), jnp.bfloat16)
    return unproject(unproject_far_kernel, 1, [half] * 2, back, weight, other)


def unproject_near(back, weight, other):
    f32 = jnp.float32
    half = (HALF_BLOCK, WIDTH)
    shapes = [jax.ShapeDtypeStruct((BLOCK, WIDTH), f32)] + [jax.ShapeDtypeStruct(half, f32)] * 2
    shapes += [jax.ShapeDtypeStruct(half, jnp.bfloat16)] * 2
    return unproject(unproject_near_kernel, 3, shapes, back, weight, other)


def pass_on_kernel(below_ref, above_ref, down_ref, up_ref, odown_ref, oup_ref):
    odown_ref[...] = (below_ref[...] + down_ref[...].astype(jnp.float32)).astype(jnp.bfloat16)
    oup_ref[...] = (above_ref[...] + up_ref[...].astype(jnp.float32)).astype(jnp.bfloat16)


def pass_on(below, above, from_up, from_down):
    return pl.pallas_call(
        pass_on_kernel,
        out_shape=[jax.ShapeDtypeStruct((HALF_BLOCK, WIDTH), jnp.bfloat16)] * 2,
        in_specs=[VMEM] * 4,
        out_specs=[VMEM] * 2,
        cost_estimate=cost(1 << 18, 2 << 20),
        compiler_params=limit(8),
        name="pass_on",
    )(below, above, from_up, from_down)


def scaled_kernel(gen_ref, mod_ref, o_ref, inverse_ref):
    f32, bf = jnp.float32, jnp.bfloat16
    scale = 1.0 + mod_ref[0:1]
    shift = mod_ref[1:2]
    for r in range(0, BLOCK, 16):
        rows = slice(r, r + 16)
        fake = (gen_ref[rows].astype(f32) * scale + shift).astype(bf).astype(f32)
        inverse = lax.rsqrt(jnp.mean(fake * fake, axis=-1, keepdims=True) + norm_eps)
        o_ref[rows] = fake * inverse
        inverse_ref[rows] = jnp.broadcast_to(inverse, (16, HEAD_DIM))


def scale_tokens(gen, modulation):
    f32 = jnp.float32
    return pl.pallas_call(
        scaled_kernel,
        out_shape=[jax.ShapeDtypeStruct((BLOCK, WIDTH), f32), jax.ShapeDtypeStruct((BLOCK, HEAD_DIM), f32)],
        in_specs=[VMEM] * 2,
        out_specs=[VMEM] * 2,
        cost_estimate=cost(2 << 20, 2 << 20),
        compiler_params=limit(8),
        name="scale_tokens",
    )(gen, modulation)


def finish_kernel(own_ref, a_ref, b_ref, c_ref, d_ref, scaled_ref, inverse_ref, mod_ref, gain_ref, o_ref):
    f32, bf = jnp.float32, jnp.bfloat16
    gain = gain_ref[...]
    scale = 1.0 + mod_ref[0:1]
    for r in range(0, BLOCK, 16):
        rows = slice(r, r + 16)
        scaled = scaled_ref[rows]
        one, two = (a_ref, b_ref) if r < HALF_BLOCK else (c_ref, d_ref)
        part = slice(r % HALF_BLOCK, r % HALF_BLOCK + 16)
        grad = own_ref[rows] + one[part].astype(f32) + two[part].astype(f32)
        grad = grad * gain
        grad = inverse_ref[rows, 0:1] * (grad - scaled * jnp.mean(grad * scaled, axis=-1, keepdims=True))
        o_ref[rows] = (grad * scale).astype(bf)


def finish(own, parts, scaled, inverse, modulation, gain):
    return pl.pallas_call(
        finish_kernel,
        out_shape=jax.ShapeDtypeStruct((BLOCK, WIDTH), jnp.bfloat16),
        in_specs=[VMEM] * 9,
        out_specs=VMEM,
        cost_estimate=cost(4 << 20, 3 << 20),
        compiler_params=limit(8),
        name="finish",
    )(own, *parts, scaled, inverse, modulation, gain)


def on_device(real_tokens, gen_hidden, modulation, norm_gain, weight):
    return step(real_tokens[0], gen_hidden[0], modulation[0], norm_gain[None], weight)[None]


def in_hbm(x):
    return pltpu.with_memory_space_constraint(x, pltpu.HBM)


def step(real_tokens, gen_hidden, modulation, gain, weight):
    colour = (lax.axis_index("x") + 2 * lax.axis_index("zl")) % 4
    core = lax.axis_index("core")

    where = (colour * 2 + core).astype(jnp.int32)[None]
    sent, sent_tail, real, fake = prepare(
        where, in_hbm(real_tokens), in_hbm(gen_hidden), in_hbm(modulation), in_hbm(gain), in_hbm(weight)
    )
    mine = lax.ppermute(sent, ("zl", "zh"), ACROSS)
    tail = lax.ppermute(sent_tail, ("zl", "zh"), ACROSS)
    below_real = lax.ppermute(real, "y", ring(1))
    above_fake = lax.ppermute(fake, "y", ring(-1))
    below_fake = lax.ppermute(fake, "y", ring(1))
    above_real = lax.ppermute(real, "y", ring(-1))
    far_real = lax.ppermute(below_real, "y", ring(1))
    far_fake = lax.ppermute(above_fake, "y", ring(-1))
    left = lax.ppermute(mine, "x", ring(1))
    right = lax.ppermute(mine, "x", ring(-1))
    side = lax.ppermute(mine, "zl", swap())
    partner_mine = lax.ppermute(mine, "core", swap())
    held = load(in_hbm(weight))
    near, near_rows = project_near([real, fake, below_real, below_fake, above_real, above_fake], held)
    partner_tail = lax.ppermute(tail, "core", swap())
    packed = pack([left, right, side])
    packed = lax.ppermute(packed, "core", swap())
    half, rows = project_far(near, near_rows, far_real, far_fake, held)
    pieces = [mine, left, right, side, tail, partner_mine, partner_tail, packed]
    pieces = [pltpu.with_memory_space_constraint(p, pltpu.VMEM) for p in pieces]
    send, other = project_rest(where, half, rows, pieces)
    received = lax.all_to_all(send.reshape(16, 6 * BLOCK, HEAD_DIM), SEQ, split_axis=0, concat_axis=0, tiled=True)
    grads = attention(received.reshape(SEND))
    back = lax.all_to_all(grads.reshape(16, 3 * BLOCK, HEAD_DIM), SEQ, split_axis=0, concat_axis=0, tiled=True)
    back = back.reshape(16, 3, BLOCK, HEAD_DIM)
    far_up, far_down = unproject_far(back, held, other)
    own, below, above, near_up, near_down = unproject_near(back, held, other)
    got_up = lax.ppermute(far_up, "y", ring(1))
    got_down = lax.ppermute(far_down, "y", ring(-1))
    low_near = lax.ppermute(near_down, "y", ring(-1))
    high_near = lax.ppermute(near_up, "y", ring(1))
    sum_down, sum_up = pass_on(below, above, got_down, got_up)
    low_sum = lax.ppermute(sum_up, "y", ring(1))
    high_sum = lax.ppermute(sum_down, "y", ring(-1))
    scaled, inverse = scale_tokens(gen_hidden, modulation)
    return finish(own, (low_sum, low_near, high_near, high_sum), scaled, inverse, modulation, gain)


def solution(mesh):
    torus = Mesh(mesh.devices.reshape(2, 4, 2, 2, 4), ("zl", "x", "core", "zh", "y"))
    fsdp = ("zh", "y")
    in_specs = (
        P(fsdp, SEQ, None),
        P(fsdp, SEQ, None),
        P(fsdp, None, None),
        P(),
        P(None, None, fsdp),
    )
    return jax.shard_map(on_device, mesh=torus, in_specs=in_specs, out_specs=P(fsdp, SEQ, None), check_vma=False)
```

```python
import jax
import jax.numpy as jnp
from jax import lax
from jax.experimental import pallas as pl
from jax.experimental.pallas import tpu as pltpu
from jax.sharding import Mesh
from jax.sharding import PartitionSpec as P


HEAD_DIM = 128
WIDTH = 3072
BLOCK = 64
PIECE = 288
SHARED = 8 * PIECE
TAIL = (WIDTH - SHARED) // 2

norm_eps = 1e-06
match_eps = 0.05
loss_weight = 4.0


SEQ = ("zl", "x", "core")
ACROSS = [(0, 3), (3, 0), (1, 2), (2, 1)]


VMEM = pl.BlockSpec(memory_space=pltpu.VMEM)


def cost(flops, touched):
    return pl.CostEstimate(flops=flops, bytes_accessed=touched, transcendentals=0)


def limit(mib=24):
    return pltpu.CompilerParams(vmem_limit_bytes=mib * 1024 * 1024)


def ring(step):
    return [(i, (i + step) % 4) for i in range(4)]


def swap():
    return [(0, 1), (1, 0)]


def attention_kernel(x_ref, o_ref):
    bf = jnp.bfloat16
    f32 = jnp.float32
    length = 16 * BLOCK
    scale = HEAD_DIM ** (-0.5)
    to_two = scale * 1.4426950408889634

    def whole(stream, part):
        return x_ref[:, stream, part].reshape(length, HEAD_DIM)

    def dot(a, b):
        return jnp.dot(a, b, preferred_element_type=f32)

    def mix(stream):
        query, key, value = (whole(stream, part) for part in range(3))
        scores = dot(key, query.T)
        highest = jnp.max(scores, axis=0, keepdims=True)
        weights = jnp.exp2((scores - highest) * to_two)
        inverse = 1.0 / jnp.sum(weights, axis=0, keepdims=True)
        return dot(value.T, weights.astype(bf)) * inverse, weights, inverse

    real_out = mix(0)[0]
    fake_out, weights, inverse = mix(1)
    query, key, value = (whole(1, part) for part in range(3))
    differ = fake_out - real_out
    grad_out = (loss_weight * differ * lax.rsqrt(differ * differ + match_eps * match_eps)).astype(bf)
    deltas = jnp.sum(grad_out.astype(f32) * fake_out, axis=0, keepdims=True)
    probs = weights * inverse
    dscores = (probs * (dot(value, grad_out) - deltas)).astype(bf)

    def store(part, grad):
        o_ref[:, part] = grad.reshape(16, BLOCK, HEAD_DIM)

    store(0, (dot(key.T, dscores) * scale).astype(bf).T)
    store(1, (dot(dscores, query) * scale).astype(bf))
    store(2, dot(probs.astype(bf), grad_out.T).astype(bf))


def attention(received):
    return pl.pallas_call(
        attention_kernel,
        out_shape=jax.ShapeDtypeStruct((16, 3, BLOCK, HEAD_DIM), jnp.bfloat16),
        in_specs=[VMEM],
        out_specs=VMEM,
        cost_estimate=cost(11 * 1024 * 1024 * 256, 4 << 20),
        compiler_params=pltpu.CompilerParams(vmem_limit_bytes=36 << 20),
        name="attention",
    )(received)


HBM = pl.BlockSpec(memory_space=pltpu.HBM)
ANY = pl.BlockSpec(memory_space=pl.ANY)
SMEM = pl.BlockSpec(memory_space=pltpu.SMEM)
DMA = pltpu.SemaphoreType.DMA
COLUMNS = 2 * HEAD_DIM


def prepare_kernel(
    where_ref, real_ref, gen_ref, mod_ref, gain_ref, w_ref, sent_ref, tail_ref, oreal_ref, ofake_ref,
    real_buf, gen_buf, mod_buf, gain_buf, sems,
):
    f32, bf = jnp.float32, jnp.bfloat16
    place = pl.multiple_of(((where_ref[0] + 4) % 8) * PIECE, PIECE)
    tail = pl.multiple_of(SHARED + (where_ref[0] % 2) * TAIL, TAIL)
    copies = [
        pltpu.make_async_copy(gen_ref, gen_buf, sems.at[0]),
        pltpu.make_async_copy(real_ref, real_buf, sems.at[1]),
        pltpu.make_async_copy(mod_ref, mod_buf, sems.at[2]),
        pltpu.make_async_copy(gain_ref, gain_buf, sems.at[3]),
        pltpu.make_async_copy(w_ref.at[:, pl.ds(place, PIECE)], sent_ref, sems.at[4]),
        pltpu.make_async_copy(w_ref.at[:, pl.ds(tail, TAIL)], tail_ref, sems.at[5]),
    ]
    for copy in copies:
        copy.start()
    for copy in copies[:4]:
        copy.wait()
    gain = gain_buf[...]
    scale = 1.0 + mod_buf[0:1]
    shift = mod_buf[1:2]
    for r in range(0, BLOCK, 16):
        rows = slice(r, r + 16)
        fake = (gen_buf[rows].astype(f32) * scale + shift).astype(bf).astype(f32)
        for ref, values in ((oreal_ref, real_buf[rows].astype(f32)), (ofake_ref, fake)):
            inverse = lax.rsqrt(jnp.mean(values * values, axis=-1, keepdims=True) + norm_eps)
            ref[rows] = (values * inverse * gain).astype(bf)
    copies[4].wait()
    copies[5].wait()


def prepare(where, real, gen, modulation, gain, weight):
    bf, f32 = jnp.bfloat16, jnp.float32
    rows = jax.ShapeDtypeStruct((BLOCK, WIDTH), bf)
    return pl.pallas_call(
        prepare_kernel,
        out_shape=[jax.ShapeDtypeStruct((3, n, COLUMNS), bf) for n in (PIECE, TAIL)] + [rows, rows],
        in_specs=[SMEM] + [HBM] * 5,
        out_specs=[VMEM] * 4,
        scratch_shapes=[
            pltpu.VMEM((BLOCK, WIDTH), bf),
            pltpu.VMEM((BLOCK, WIDTH), bf),
            pltpu.VMEM((2, WIDTH), f32),
            pltpu.VMEM((1, WIDTH), f32),
            DMA((6,)),
        ],
        cost_estimate=cost(4 << 20, 3 << 20),
        compiler_params=limit(16),
        name="prepare",
    )(where, real, gen, modulation, gain, weight)


NEAR = (2, 3, 2, 3, BLOCK, HEAD_DIM)
SEND = (16, 2, 3, BLOCK, HEAD_DIM)


def load_kernel(w_ref, o_ref, sems):
    copies = [pltpu.make_async_copy(w_ref.at[q], o_ref.at[q], sems.at[q]) for q in range(3)]
    for copy in copies:
        copy.start()
    for copy in copies:
        copy.wait()


def load(weight):
    return pl.pallas_call(
        load_kernel,
        out_shape=jax.ShapeDtypeStruct((3, WIDTH, COLUMNS), jnp.bfloat16),
        in_specs=[HBM],
        out_specs=VMEM,
        scratch_shapes=[DMA((3,))],
        cost_estimate=cost(0, 9 << 20),
        compiler_params=limit(4),
        name="load",
    )(weight)


def near_kernel(*refs):
    row_refs, (w_ref, o_ref, rows_ref) = refs[:6], refs[6:]
    for i, ref in enumerate(row_refs):
        rows_ref[BLOCK * i : BLOCK * (i + 1)] = ref[...]
    for q in range(3):
        out = jnp.dot(rows_ref[: 6 * BLOCK], w_ref[q], preferred_element_type=jnp.float32).astype(jnp.bfloat16)
        for k in range(2):
            for j in range(3):
                for s in range(2):
                    r = (2 * j + s) * BLOCK
                    o_ref[k, j, s, q] = out[r : r + BLOCK, HEAD_DIM * k : HEAD_DIM * (k + 1)]


def project_near(rows, weight):
    return pl.pallas_call(
        near_kernel,
        out_shape=[
            jax.ShapeDtypeStruct(NEAR, jnp.bfloat16),
            jax.ShapeDtypeStruct((8 * BLOCK, WIDTH), jnp.bfloat16),
        ],
        in_specs=[VMEM] * 7,
        out_specs=[VMEM] * 2,
        cost_estimate=cost(2 * 384 * 3072 * 768, 7 << 20),
        compiler_params=limit(8),
        name="project_near",
    )(*rows, weight)


def pack_kernel(a_ref, b_ref, c_ref, o_ref):
    for i, ref in enumerate((a_ref, b_ref, c_ref)):
        o_ref[i] = ref[...]


def pack(pieces):
    return pl.pallas_call(
        pack_kernel,
        out_shape=jax.ShapeDtypeStruct((3, 3, PIECE, COLUMNS), jnp.bfloat16),
        in_specs=[VMEM] * 3,
        out_specs=VMEM,
        cost_estimate=cost(0, 3 << 20),
        compiler_params=limit(4),
        name="pack",
    )(*pieces)


def in_vmem(x):
    return pltpu.with_memory_space_constraint(x, pltpu.VMEM)


def shared_rows(where, colour, own):
    half = where % 2 if own else 1 - where % 2
    return pl.ds(pl.multiple_of((((where // 2 + colour) % 4) * 2 + half) * PIECE, PIECE), PIECE)


def tail_rows(where, own):
    half = where % 2 if own else 1 - where % 2
    return pl.ds(pl.multiple_of(SHARED + half * TAIL, TAIL), TAIL)


def join_kernel(where_ref, *refs):
    pieces, o_ref = refs[:7], refs[7]
    where = where_ref[0]
    places = [shared_rows(where, c, True) for c in (0, 3, 1, 2)]
    places += [tail_rows(where, True), shared_rows(where, 0, False), tail_rows(where, False)]
    for place, piece in zip(places, pieces):
        o_ref[:, place] = piece[...]


def join(where, pieces):
    return pl.pallas_call(
        join_kernel,
        out_shape=jax.ShapeDtypeStruct((3, WIDTH, COLUMNS), jnp.bfloat16),
        in_specs=[SMEM] + [VMEM] * 7,
        out_specs=VMEM,
        cost_estimate=cost(0, 7 << 20),
        compiler_params=limit(4),
        name="join",
    )(where, *pieces)


def far_kernel(near_ref, rows_ref, real_ref, fake_ref, w_ref, o_ref, all_ref):
    del rows_ref
    bf, f32 = jnp.bfloat16, jnp.float32
    all_ref[6 * BLOCK : 7 * BLOCK] = real_ref[...]
    all_ref[7 * BLOCK :] = fake_ref[...]
    for k in range(2):
        for j in range(3):
            o_ref[4 * k + j] = near_ref[k, j]
    for q in range(3):
        out = jnp.dot(all_ref[6 * BLOCK :], w_ref[q], preferred_element_type=f32).astype(bf)
        for k in range(2):
            for s in range(2):
                o_ref[4 * k + 3, s, q] = out[BLOCK * s : BLOCK * (s + 1), HEAD_DIM * k : HEAD_DIM * (k + 1)]


def project_far(near, rows, far_real, far_fake, weight):
    bf = jnp.bfloat16
    return pl.pallas_call(
        far_kernel,
        out_shape=[jax.ShapeDtypeStruct((8, *SEND[1:]), bf), jax.ShapeDtypeStruct((8 * BLOCK, WIDTH), bf)],
        in_specs=[VMEM] * 5,
        out_specs=[VMEM] * 2,
        input_output_aliases={1: 1},
        cost_estimate=cost(2 * 128 * 3072 * 768, 10 << 20),
        compiler_params=limit(8),
        name="project_far",
    )(near, in_vmem(rows), far_real, far_fake, weight)


def rest_kernel(where_ref, half_ref, rows_ref, joined_ref, packed_ref, o_ref, other_ref):
    del joined_ref
    bf, f32 = jnp.bfloat16, jnp.float32
    o_ref[:8] = half_ref[...]
    for q in range(3):
        for i, c in enumerate((3, 1, 2)):
            other_ref[q, shared_rows(where_ref[0], c, False)] = packed_ref[i, q]
        out = jnp.dot(rows_ref[...], other_ref[q], preferred_element_type=f32).astype(bf)
        for k in range(2):
            for j in range(4):
                for s in range(2):
                    r = (2 * j + s) * BLOCK
                    o_ref[4 * (2 + k) + j, s, q] = out[r : r + BLOCK, HEAD_DIM * k : HEAD_DIM * (k + 1)]


def project_rest(where, half, rows, joined, packed):
    bf = jnp.bfloat16
    return pl.pallas_call(
        rest_kernel,
        out_shape=[jax.ShapeDtypeStruct(SEND, bf), jax.ShapeDtypeStruct((3, WIDTH, COLUMNS), bf)],
        in_specs=[SMEM] + [VMEM] * 4,
        out_specs=[VMEM] * 2,
        input_output_aliases={3: 1},
        cost_estimate=cost(2 * 512 * 3072 * 768, 14 << 20),
        compiler_params=limit(8),
        name="project_rest",
    )(where, half, rows, in_vmem(joined), in_vmem(packed))


CHUNK = 768


HALF_BLOCK = BLOCK // 2


def unproject_kernel(back_ref, own_ref, other_ref, own_out, below_ref, above_ref, *refs):
    far_up, far_down, near_up, near_down, grads_ref = refs
    bf, f32 = jnp.bfloat16, jnp.float32
    for p in range(2):
        for q in range(3):
            for k in range(2):
                d = 4 * (2 * p + k)
                c = ((3 * p + q) * 2 + k) * HEAD_DIM
                grads_ref[:, c : c + HEAD_DIM] = back_ref[d : d + 4, q].reshape(4 * BLOCK, HEAD_DIM)
    for n in range(0, WIDTH, CHUNK):
        total = None
        for p, ref in enumerate((own_ref, other_ref)):
            for q in range(3):
                c = (3 * p + q) * COLUMNS
                term = lax.dot_general(
                    grads_ref[:, c : c + COLUMNS],
                    ref[q, n : n + CHUNK],
                    (((1,), (1,)), ((), ())),
                    preferred_element_type=f32,
                )
                total = term if total is None else total + term
        columns = slice(n, n + CHUNK)
        parts = [total[HALF_BLOCK * i : HALF_BLOCK * (i + 1)] for i in range(8)]
        own_out[:, columns] = total[:BLOCK]
        near_down[:, columns] = parts[2].astype(bf)
        below_ref[:, columns] = parts[3]
        above_ref[:, columns] = parts[4]
        near_up[:, columns] = parts[5].astype(bf)
        far_up[:, columns] = parts[6].astype(bf)
        far_down[:, columns] = parts[7].astype(bf)


def unproject(back, weight, other):
    f32 = jnp.float32
    half = (HALF_BLOCK, WIDTH)
    return pl.pallas_call(
        unproject_kernel,
        out_shape=[jax.ShapeDtypeStruct((BLOCK, WIDTH), f32)]
        + [jax.ShapeDtypeStruct(half, f32)] * 2
        + [jax.ShapeDtypeStruct(half, jnp.bfloat16)] * 4,
        in_specs=[VMEM] * 3,
        out_specs=[VMEM] * 7,
        scratch_shapes=[pltpu.VMEM((4 * BLOCK, 12 * HEAD_DIM), jnp.bfloat16)],
        cost_estimate=cost(2 * 256 * 3072 * 1536, 12 << 20),
        compiler_params=limit(16),
        name="unproject",
    )(back, weight, other)


def pass_on_kernel(kept_ref, got_ref, o_ref):
    o_ref[...] = (kept_ref[...] + got_ref[...].astype(jnp.float32)).astype(jnp.bfloat16)


def pass_on(kept, got):
    return pl.pallas_call(
        pass_on_kernel,
        out_shape=jax.ShapeDtypeStruct((HALF_BLOCK, WIDTH), jnp.bfloat16),
        in_specs=[VMEM] * 2,
        out_specs=VMEM,
        cost_estimate=cost(1 << 17, 1 << 20),
        compiler_params=limit(8),
        name="pass_on",
    )(kept, got)


def scaled_kernel(gen_ref, mod_ref, o_ref, inverse_ref):
    f32, bf = jnp.float32, jnp.bfloat16
    scale = 1.0 + mod_ref[0:1]
    shift = mod_ref[1:2]
    for r in range(0, BLOCK, 16):
        rows = slice(r, r + 16)
        fake = (gen_ref[rows].astype(f32) * scale + shift).astype(bf).astype(f32)
        inverse = lax.rsqrt(jnp.mean(fake * fake, axis=-1, keepdims=True) + norm_eps)
        o_ref[rows] = fake * inverse
        inverse_ref[rows] = jnp.broadcast_to(inverse, (16, HEAD_DIM))


def scale_tokens(gen, modulation):
    f32 = jnp.float32
    return pl.pallas_call(
        scaled_kernel,
        out_shape=[jax.ShapeDtypeStruct((BLOCK, WIDTH), f32), jax.ShapeDtypeStruct((BLOCK, HEAD_DIM), f32)],
        in_specs=[VMEM] * 2,
        out_specs=[VMEM] * 2,
        cost_estimate=cost(2 << 20, 2 << 20),
        compiler_params=limit(8),
        name="scale_tokens",
    )(gen, modulation)


def finish_kernel(own_ref, a_ref, b_ref, c_ref, d_ref, scaled_ref, inverse_ref, mod_ref, gain_ref, o_ref):
    f32, bf = jnp.float32, jnp.bfloat16
    gain = gain_ref[...]
    scale = 1.0 + mod_ref[0:1]
    for r in range(0, BLOCK, 16):
        rows = slice(r, r + 16)
        scaled = scaled_ref[rows]
        one, two = (a_ref, b_ref) if r < HALF_BLOCK else (c_ref, d_ref)
        part = slice(r % HALF_BLOCK, r % HALF_BLOCK + 16)
        grad = own_ref[rows] + one[part].astype(f32) + two[part].astype(f32)
        grad = grad * gain
        grad = inverse_ref[rows, 0:1] * (grad - scaled * jnp.mean(grad * scaled, axis=-1, keepdims=True))
        o_ref[rows] = (grad * scale).astype(bf)


def finish(own, parts, scaled, inverse, modulation, gain):
    return pl.pallas_call(
        finish_kernel,
        out_shape=jax.ShapeDtypeStruct((BLOCK, WIDTH), jnp.bfloat16),
        in_specs=[VMEM] * 9,
        out_specs=VMEM,
        cost_estimate=cost(4 << 20, 3 << 20),
        compiler_params=limit(8),
        name="finish",
    )(own, *parts, scaled, inverse, modulation, gain)


def on_device(real_tokens, gen_hidden, modulation, norm_gain, weight):
    return step(real_tokens[0], gen_hidden[0], modulation[0], norm_gain[None], weight)[None]


def in_hbm(x):
    return pltpu.with_memory_space_constraint(x, pltpu.HBM)


def step(real_tokens, gen_hidden, modulation, gain, weight):
    colour = (lax.axis_index("x") + 2 * lax.axis_index("zl")) % 4
    core = lax.axis_index("core")

    where = (colour * 2 + core).astype(jnp.int32)[None]
    sent, sent_tail, real, fake = prepare(
        where, in_hbm(real_tokens), in_hbm(gen_hidden), in_hbm(modulation), in_hbm(gain), in_hbm(weight)
    )
    mine = lax.ppermute(sent, ("zl", "zh"), ACROSS)
    tail = lax.ppermute(sent_tail, ("zl", "zh"), ACROSS)
    below_real = lax.ppermute(real, "y", ring(1))
    above_fake = lax.ppermute(fake, "y", ring(-1))
    below_fake = lax.ppermute(fake, "y", ring(1))
    above_real = lax.ppermute(real, "y", ring(-1))
    far_real = lax.ppermute(below_real, "y", ring(1))
    far_fake = lax.ppermute(above_fake, "y", ring(-1))
    left = lax.ppermute(mine, "x", ring(1))
    right = lax.ppermute(mine, "x", ring(-1))
    side = lax.ppermute(mine, "zl", swap())
    partner_mine = lax.ppermute(mine, "core", swap())
    held = load(in_hbm(weight))
    near, near_rows = project_near([real, fake, below_real, below_fake, above_real, above_fake], held)
    partner_tail = lax.ppermute(tail, "core", swap())
    packed = pack([left, right, side])
    packed = lax.ppermute(packed, "core", swap())
    half, rows = project_far(near, near_rows, far_real, far_fake, held)
    joined = join(where, [mine, left, right, side, tail, partner_mine, partner_tail])
    send, other = project_rest(where, half, rows, joined, packed)
    received = lax.all_to_all(send.reshape(16, 6 * BLOCK, HEAD_DIM), SEQ, split_axis=0, concat_axis=0, tiled=True)
    grads = attention(received.reshape(SEND))
    back = lax.all_to_all(grads.reshape(16, 3 * BLOCK, HEAD_DIM), SEQ, split_axis=0, concat_axis=0, tiled=True)
    own, below, above, far_up, far_down, near_up, near_down = unproject(
        back.reshape(16, 3, BLOCK, HEAD_DIM), held, other
    )
    got_up = lax.ppermute(far_up, "y", ring(1))
    got_down = lax.ppermute(far_down, "y", ring(-1))
    low_near = lax.ppermute(near_down, "y", ring(-1))
    high_near = lax.ppermute(near_up, "y", ring(1))
    sum_up = pass_on(above, got_up)
    sum_down = pass_on(below, got_down)
    low_sum = lax.ppermute(sum_up, "y", ring(1))
    high_sum = lax.ppermute(sum_down, "y", ring(-1))
    scaled, inverse = scale_tokens(gen_hidden, modulation)
    return finish(own, (low_sum, low_near, high_near, high_sum), scaled, inverse, modulation, gain)


def solution(mesh):
    torus = Mesh(mesh.devices.reshape(2, 4, 2, 2, 4), ("zl", "x", "core", "zh", "y"))
    fsdp = ("zh", "y")
    in_specs = (
        P(fsdp, SEQ, None),
        P(fsdp, SEQ, None),
        P(fsdp, None, None),
        P(),
        P(None, None, fsdp),
    )
    return jax.shard_map(on_device, mesh=torus, in_specs=in_specs, out_specs=P(fsdp, SEQ, None), check_vma=False)
```

```python
import jax
import jax.numpy as jnp
from jax import lax
from jax.experimental import pallas as pl
from jax.experimental.pallas import tpu as pltpu
from jax.sharding import Mesh
from jax.sharding import PartitionSpec as P


HEAD_DIM = 128
WIDTH = 3072
BLOCK = 64
PIECE = 288
SHARED = 8 * PIECE
TAIL = (WIDTH - SHARED) // 2

norm_eps = 1e-06
match_eps = 0.05
loss_weight = 4.0


SEQ = ("zl", "x", "core")
ACROSS = [(0, 3), (3, 0), (1, 2), (2, 1)]


VMEM = pl.BlockSpec(memory_space=pltpu.VMEM)


def cost(flops, touched):
    return pl.CostEstimate(flops=flops, bytes_accessed=touched, transcendentals=0)


def limit(mib=24):
    return pltpu.CompilerParams(vmem_limit_bytes=mib * 1024 * 1024)


def ring(step):
    return [(i, (i + step) % 4) for i in range(4)]


def plane_ring(plane, step):
    return [(4 * plane + i, 4 * plane + (i + step) % 4) for i in range(4)]


def swap():
    return [(0, 1), (1, 0)]


def attention_kernel(x_ref, o_ref):
    bf = jnp.bfloat16
    f32 = jnp.float32
    length = 16 * BLOCK
    scale = HEAD_DIM ** (-0.5)
    to_two = scale * 1.4426950408889634

    def whole(stream, part):
        return x_ref[:, stream, part].reshape(length, HEAD_DIM)

    def dot(a, b):
        return jnp.dot(a, b, preferred_element_type=f32)

    def mix(stream):
        query, key, value = (whole(stream, part) for part in range(3))
        scores = dot(key, query.T)
        highest = jnp.max(scores, axis=0, keepdims=True)
        weights = jnp.exp2((scores - highest) * to_two)
        inverse = 1.0 / jnp.sum(weights, axis=0, keepdims=True)
        return dot(value.T, weights.astype(bf)) * inverse, weights, inverse

    real_out = mix(0)[0]
    fake_out, weights, inverse = mix(1)
    query, key, value = (whole(1, part) for part in range(3))
    differ = fake_out - real_out
    grad_out = (loss_weight * differ * lax.rsqrt(differ * differ + match_eps * match_eps)).astype(bf)
    deltas = jnp.sum(grad_out.astype(f32) * fake_out, axis=0, keepdims=True)
    probs = weights * inverse
    dscores = (probs * (dot(value, grad_out) - deltas)).astype(bf)

    def store(part, grad):
        o_ref[:, part] = grad.reshape(16, BLOCK, HEAD_DIM)

    store(0, (dot(key.T, dscores) * scale).astype(bf).T)
    store(1, (dot(dscores, query) * scale).astype(bf))
    store(2, dot(probs.astype(bf), grad_out.T).astype(bf))


def attention(received):
    return pl.pallas_call(
        attention_kernel,
        out_shape=jax.ShapeDtypeStruct((16, 3, BLOCK, HEAD_DIM), jnp.bfloat16),
        in_specs=[VMEM],
        out_specs=VMEM,
        cost_estimate=cost(11 * 1024 * 1024 * 256, 4 << 20),
        compiler_params=pltpu.CompilerParams(vmem_limit_bytes=36 << 20),
        name="attention",
    )(received)


HBM = pl.BlockSpec(memory_space=pltpu.HBM)
ANY = pl.BlockSpec(memory_space=pl.ANY)
SMEM = pl.BlockSpec(memory_space=pltpu.SMEM)
DMA = pltpu.SemaphoreType.DMA
COLUMNS = 2 * HEAD_DIM


def prepare_kernel(
    where_ref, real_ref, gen_ref, mod_ref, gain_ref, w_ref, sent_ref, tail_ref, oreal_ref, ofake_ref,
    real_buf, gen_buf, mod_buf, gain_buf, sems,
):
    f32, bf = jnp.float32, jnp.bfloat16
    place = pl.multiple_of(((where_ref[0] + 4) % 8) * PIECE, PIECE)
    tail = pl.multiple_of(SHARED + (where_ref[0] % 2) * TAIL, TAIL)
    copies = [
        pltpu.make_async_copy(gen_ref, gen_buf, sems.at[0]),
        pltpu.make_async_copy(real_ref, real_buf, sems.at[1]),
        pltpu.make_async_copy(mod_ref, mod_buf, sems.at[2]),
        pltpu.make_async_copy(gain_ref, gain_buf, sems.at[3]),
        pltpu.make_async_copy(w_ref.at[:, pl.ds(place, PIECE)], sent_ref, sems.at[4]),
        pltpu.make_async_copy(w_ref.at[:, pl.ds(tail, TAIL)], tail_ref, sems.at[5]),
    ]
    for copy in copies:
        copy.start()
    for copy in copies[:4]:
        copy.wait()
    gain = gain_buf[...]
    scale = 1.0 + mod_buf[0:1]
    shift = mod_buf[1:2]
    for r in range(0, BLOCK, 16):
        rows = slice(r, r + 16)
        fake = (gen_buf[rows].astype(f32) * scale + shift).astype(bf).astype(f32)
        for ref, values in ((oreal_ref, real_buf[rows].astype(f32)), (ofake_ref, fake)):
            inverse = lax.rsqrt(jnp.mean(values * values, axis=-1, keepdims=True) + norm_eps)
            ref[rows] = (values * inverse * gain).astype(bf)
    copies[4].wait()
    copies[5].wait()


def prepare(where, real, gen, modulation, gain, weight):
    bf, f32 = jnp.bfloat16, jnp.float32
    rows = jax.ShapeDtypeStruct((BLOCK, WIDTH), bf)
    return pl.pallas_call(
        prepare_kernel,
        out_shape=[jax.ShapeDtypeStruct((3, n, COLUMNS), bf) for n in (PIECE, TAIL)] + [rows, rows],
        in_specs=[SMEM] + [HBM] * 5,
        out_specs=[VMEM] * 4,
        scratch_shapes=[
            pltpu.VMEM((BLOCK, WIDTH), bf),
            pltpu.VMEM((BLOCK, WIDTH), bf),
            pltpu.VMEM((2, WIDTH), f32),
            pltpu.VMEM((1, WIDTH), f32),
            DMA((6,)),
        ],
        cost_estimate=cost(4 << 20, 3 << 20),
        compiler_params=limit(16),
        name="prepare",
    )(where, real, gen, modulation, gain, weight)


NEAR = (2, 3, 2, 3, BLOCK, HEAD_DIM)
SEND = (16, 2, 3, BLOCK, HEAD_DIM)


def load_kernel(w_ref, o_ref, sems):
    copies = [pltpu.make_async_copy(w_ref.at[q], o_ref.at[q], sems.at[q]) for q in range(3)]
    for copy in copies:
        copy.start()
    for copy in copies:
        copy.wait()


def load(weight):
    return pl.pallas_call(
        load_kernel,
        out_shape=jax.ShapeDtypeStruct((3, WIDTH, COLUMNS), jnp.bfloat16),
        in_specs=[HBM],
        out_specs=VMEM,
        scratch_shapes=[DMA((3,))],
        cost_estimate=cost(0, 9 << 20),
        compiler_params=limit(4),
        name="load",
    )(weight)


def near_kernel(
    real_ref, fake_ref, below_real_0, below_real_1, below_fake, above_real, above_fake_0, above_fake_1, w_ref, o_ref, rows_ref
):
    below_real = below_real_0[...] + below_real_1[...]
    above_fake = above_fake_0[...] + above_fake_1[...]
    for i, rows in enumerate((real_ref[...], fake_ref[...], below_real, below_fake[...], above_real[...], above_fake)):
        rows_ref[BLOCK * i : BLOCK * (i + 1)] = rows
    for q in range(3):
        out = jnp.dot(rows_ref[: 6 * BLOCK], w_ref[q], preferred_element_type=jnp.float32).astype(jnp.bfloat16)
        for k in range(2):
            for j in range(3):
                for s in range(2):
                    r = (2 * j + s) * BLOCK
                    o_ref[k, j, s, q] = out[r : r + BLOCK, HEAD_DIM * k : HEAD_DIM * (k + 1)]


def project_near(rows, weight):
    return pl.pallas_call(
        near_kernel,
        out_shape=[
            jax.ShapeDtypeStruct(NEAR, jnp.bfloat16),
            jax.ShapeDtypeStruct((8 * BLOCK, WIDTH), jnp.bfloat16),
        ],
        in_specs=[VMEM] * 9,
        out_specs=[VMEM] * 2,
        cost_estimate=cost(2 * 384 * 3072 * 768, 7 << 20),
        compiler_params=limit(8),
        name="project_near",
    )(*rows, weight)


def pack_kernel(a_ref, b_ref, c_ref, o_ref):
    for i, ref in enumerate((a_ref, b_ref, c_ref)):
        o_ref[i] = ref[...]


def pack(pieces):
    return pl.pallas_call(
        pack_kernel,
        out_shape=jax.ShapeDtypeStruct((3, 3, PIECE, COLUMNS), jnp.bfloat16),
        in_specs=[VMEM] * 3,
        out_specs=VMEM,
        cost_estimate=cost(0, 3 << 20),
        compiler_params=limit(4),
        name="pack",
    )(*pieces)


def in_vmem(x):
    return pltpu.with_memory_space_constraint(x, pltpu.VMEM)


def shared_rows(where, colour, own):
    half = where % 2 if own else 1 - where % 2
    return pl.ds(pl.multiple_of((((where // 2 + colour) % 4) * 2 + half) * PIECE, PIECE), PIECE)


def tail_rows(where, own):
    half = where % 2 if own else 1 - where % 2
    return pl.ds(pl.multiple_of(SHARED + half * TAIL, TAIL), TAIL)


def join_kernel(where_ref, *refs):
    pieces, o_ref = refs[:7], refs[7]
    where = where_ref[0]
    places = [shared_rows(where, c, True) for c in (0, 3, 1, 2)]
    places += [tail_rows(where, True), shared_rows(where, 0, False), tail_rows(where, False)]
    for place, piece in zip(places, pieces):
        o_ref[:, place] = piece[...]


def join(where, pieces):
    return pl.pallas_call(
        join_kernel,
        out_shape=jax.ShapeDtypeStruct((3, WIDTH, COLUMNS), jnp.bfloat16),
        in_specs=[SMEM] + [VMEM] * 7,
        out_specs=VMEM,
        cost_estimate=cost(0, 7 << 20),
        compiler_params=limit(4),
        name="join",
    )(where, *pieces)


def far_kernel(near_ref, rows_ref, real_0, real_1, fake_0, fake_1, w_ref, o_ref, all_ref):
    del rows_ref
    bf, f32 = jnp.bfloat16, jnp.float32
    all_ref[6 * BLOCK : 7 * BLOCK] = real_0[...] + real_1[...]
    all_ref[7 * BLOCK :] = fake_0[...] + fake_1[...]
    for k in range(2):
        for j in range(3):
            o_ref[4 * k + j] = near_ref[k, j]
    for q in range(3):
        out = jnp.dot(all_ref[6 * BLOCK :], w_ref[q], preferred_element_type=f32).astype(bf)
        for k in range(2):
            for s in range(2):
                o_ref[4 * k + 3, s, q] = out[BLOCK * s : BLOCK * (s + 1), HEAD_DIM * k : HEAD_DIM * (k + 1)]


def project_far(near, rows, far_real, far_fake, weight):
    bf = jnp.bfloat16
    return pl.pallas_call(
        far_kernel,
        out_shape=[jax.ShapeDtypeStruct((8, *SEND[1:]), bf), jax.ShapeDtypeStruct((8 * BLOCK, WIDTH), bf)],
        in_specs=[VMEM] * 7,
        out_specs=[VMEM] * 2,
        input_output_aliases={1: 1},
        cost_estimate=cost(2 * 128 * 3072 * 768, 10 << 20),
        compiler_params=limit(8),
        name="project_far",
    )(near, in_vmem(rows), *far_real, *far_fake, weight)


def rest_kernel(where_ref, half_ref, rows_ref, joined_ref, packed_ref, o_ref, other_ref):
    del joined_ref
    bf, f32 = jnp.bfloat16, jnp.float32
    o_ref[:8] = half_ref[...]
    for q in range(3):
        for i, c in enumerate((3, 1, 2)):
            other_ref[q, shared_rows(where_ref[0], c, False)] = packed_ref[i, q]
        out = jnp.dot(rows_ref[...], other_ref[q], preferred_element_type=f32).astype(bf)
        for k in range(2):
            for j in range(4):
                for s in range(2):
                    r = (2 * j + s) * BLOCK
                    o_ref[4 * (2 + k) + j, s, q] = out[r : r + BLOCK, HEAD_DIM * k : HEAD_DIM * (k + 1)]


def project_rest(where, half, rows, joined, packed):
    bf = jnp.bfloat16
    return pl.pallas_call(
        rest_kernel,
        out_shape=[jax.ShapeDtypeStruct(SEND, bf), jax.ShapeDtypeStruct((3, WIDTH, COLUMNS), bf)],
        in_specs=[SMEM] + [VMEM] * 4,
        out_specs=[VMEM] * 2,
        input_output_aliases={3: 1},
        cost_estimate=cost(2 * 512 * 3072 * 768, 14 << 20),
        compiler_params=limit(8),
        name="project_rest",
    )(where, half, rows, in_vmem(joined), in_vmem(packed))


CHUNK = 768


HALF_BLOCK = BLOCK // 2


def unproject_kernel(back_ref, own_ref, other_ref, own_out, below_ref, above_ref, *refs):
    far_up, far_down, near_up, near_down, grads_ref = refs
    bf, f32 = jnp.bfloat16, jnp.float32
    for p in range(2):
        for q in range(3):
            for k in range(2):
                d = 4 * (2 * p + k)
                c = ((3 * p + q) * 2 + k) * HEAD_DIM
                grads_ref[:, c : c + HEAD_DIM] = back_ref[d : d + 4, q].reshape(4 * BLOCK, HEAD_DIM)
    for n in range(0, WIDTH, CHUNK):
        total = None
        for p, ref in enumerate((own_ref, other_ref)):
            for q in range(3):
                c = (3 * p + q) * COLUMNS
                term = lax.dot_general(
                    grads_ref[:, c : c + COLUMNS],
                    ref[q, n : n + CHUNK],
                    (((1,), (1,)), ((), ())),
                    preferred_element_type=f32,
                )
                total = term if total is None else total + term
        columns = slice(n, n + CHUNK)
        parts = [total[HALF_BLOCK * i : HALF_BLOCK * (i + 1)] for i in range(8)]
        own_out[:, columns] = total[:BLOCK]
        near_down[:, columns] = parts[2].astype(bf)
        below_ref[:, columns] = parts[3]
        above_ref[:, columns] = parts[4]
        near_up[:, columns] = parts[5].astype(bf)
        far_up[:, columns] = parts[6].astype(bf)
        far_down[:, columns] = parts[7].astype(bf)


def unproject(back, weight, other):
    f32 = jnp.float32
    half = (HALF_BLOCK, WIDTH)
    return pl.pallas_call(
        unproject_kernel,
        out_shape=[jax.ShapeDtypeStruct((BLOCK, WIDTH), f32)]
        + [jax.ShapeDtypeStruct(half, f32)] * 2
        + [jax.ShapeDtypeStruct(half, jnp.bfloat16)] * 4,
        in_specs=[VMEM] * 3,
        out_specs=[VMEM] * 7,
        scratch_shapes=[pltpu.VMEM((4 * BLOCK, 12 * HEAD_DIM), jnp.bfloat16)],
        cost_estimate=cost(2 * 256 * 3072 * 1536, 12 << 20),
        compiler_params=limit(16),
        name="unproject",
    )(back, weight, other)


def pass_on_kernel(kept_ref, got_ref, o_ref):
    o_ref[...] = (kept_ref[...] + got_ref[...].astype(jnp.float32)).astype(jnp.bfloat16)


def pass_on(kept, got):
    return pl.pallas_call(
        pass_on_kernel,
        out_shape=jax.ShapeDtypeStruct((HALF_BLOCK, WIDTH), jnp.bfloat16),
        in_specs=[VMEM] * 2,
        out_specs=VMEM,
        cost_estimate=cost(1 << 17, 1 << 20),
        compiler_params=limit(8),
        name="pass_on",
    )(kept, got)


def scaled_kernel(gen_ref, mod_ref, o_ref, inverse_ref):
    f32, bf = jnp.float32, jnp.bfloat16
    scale = 1.0 + mod_ref[0:1]
    shift = mod_ref[1:2]
    for r in range(0, BLOCK, 16):
        rows = slice(r, r + 16)
        fake = (gen_ref[rows].astype(f32) * scale + shift).astype(bf).astype(f32)
        inverse = lax.rsqrt(jnp.mean(fake * fake, axis=-1, keepdims=True) + norm_eps)
        o_ref[rows] = fake * inverse
        inverse_ref[rows] = jnp.broadcast_to(inverse, (16, HEAD_DIM))


def scale_tokens(gen, modulation):
    f32 = jnp.float32
    return pl.pallas_call(
        scaled_kernel,
        out_shape=[jax.ShapeDtypeStruct((BLOCK, WIDTH), f32), jax.ShapeDtypeStruct((BLOCK, HEAD_DIM), f32)],
        in_specs=[VMEM] * 2,
        out_specs=[VMEM] * 2,
        cost_estimate=cost(2 << 20, 2 << 20),
        compiler_params=limit(8),
        name="scale_tokens",
    )(gen, modulation)


def finish_kernel(own_ref, a_ref, b_ref, c_ref, d_ref, scaled_ref, inverse_ref, mod_ref, gain_ref, o_ref):
    f32, bf = jnp.float32, jnp.bfloat16
    gain = gain_ref[...]
    scale = 1.0 + mod_ref[0:1]
    for r in range(0, BLOCK, 16):
        rows = slice(r, r + 16)
        scaled = scaled_ref[rows]
        one, two = (a_ref, b_ref) if r < HALF_BLOCK else (c_ref, d_ref)
        part = slice(r % HALF_BLOCK, r % HALF_BLOCK + 16)
        grad = own_ref[rows] + one[part].astype(f32) + two[part].astype(f32)
        grad = grad * gain
        grad = inverse_ref[rows, 0:1] * (grad - scaled * jnp.mean(grad * scaled, axis=-1, keepdims=True))
        o_ref[rows] = (grad * scale).astype(bf)


def finish(own, parts, scaled, inverse, modulation, gain):
    return pl.pallas_call(
        finish_kernel,
        out_shape=jax.ShapeDtypeStruct((BLOCK, WIDTH), jnp.bfloat16),
        in_specs=[VMEM] * 9,
        out_specs=VMEM,
        cost_estimate=cost(4 << 20, 3 << 20),
        compiler_params=limit(8),
        name="finish",
    )(own, *parts, scaled, inverse, modulation, gain)


def on_device(real_tokens, gen_hidden, modulation, norm_gain, weight):
    return step(real_tokens[0], gen_hidden[0], modulation[0], norm_gain[None], weight)[None]


def in_hbm(x):
    return pltpu.with_memory_space_constraint(x, pltpu.HBM)


def step(real_tokens, gen_hidden, modulation, gain, weight):
    colour = (lax.axis_index("x") + 2 * lax.axis_index("zl")) % 4
    core = lax.axis_index("core")

    where = (colour * 2 + core).astype(jnp.int32)[None]
    sent, sent_tail, real, fake = prepare(
        where, in_hbm(real_tokens), in_hbm(gen_hidden), in_hbm(modulation), in_hbm(gain), in_hbm(weight)
    )
    mine = lax.ppermute(sent, ("zl", "zh"), ACROSS)
    tail = lax.ppermute(sent_tail, ("zl", "zh"), ACROSS)
    both = ("zh", "y")
    below_real = [lax.ppermute(real, both, plane_ring(p, 1)) for p in range(2)]
    above_fake = [lax.ppermute(fake, both, plane_ring(p, -1)) for p in range(2)]
    below_fake = lax.ppermute(fake, "y", ring(1))
    above_real = lax.ppermute(real, "y", ring(-1))
    far_real = [lax.ppermute(below_real[p], both, plane_ring(p, 1)) for p in range(2)]
    far_fake = [lax.ppermute(above_fake[p], both, plane_ring(p, -1)) for p in range(2)]
    left = lax.ppermute(mine, "x", ring(1))
    right = lax.ppermute(mine, "x", ring(-1))
    side = lax.ppermute(mine, "zl", swap())
    partner_mine = lax.ppermute(mine, "core", swap())
    held = load(in_hbm(weight))
    near, near_rows = project_near([real, fake, *below_real, below_fake, above_real, *above_fake], held)
    partner_tail = lax.ppermute(tail, "core", swap())
    packed = pack([left, right, side])
    packed = lax.ppermute(packed, "core", swap())
    half, rows = project_far(near, near_rows, far_real, far_fake, held)
    joined = join(where, [mine, left, right, side, tail, partner_mine, partner_tail])
    send, other = project_rest(where, half, rows, joined, packed)
    received = lax.all_to_all(send.reshape(16, 6 * BLOCK, HEAD_DIM), SEQ, split_axis=0, concat_axis=0, tiled=True)
    grads = attention(received.reshape(SEND))
    back = lax.all_to_all(grads.reshape(16, 3 * BLOCK, HEAD_DIM), SEQ, split_axis=0, concat_axis=0, tiled=True)
    own, below, above, far_up, far_down, near_up, near_down = unproject(
        back.reshape(16, 3, BLOCK, HEAD_DIM), held, other
    )
    got_up = lax.ppermute(far_up, "y", ring(1))
    got_down = lax.ppermute(far_down, "y", ring(-1))
    low_near = lax.ppermute(near_down, "y", ring(-1))
    high_near = lax.ppermute(near_up, "y", ring(1))
    sum_up = pass_on(above, got_up)
    sum_down = pass_on(below, got_down)
    low_sum = lax.ppermute(sum_up, "y", ring(1))
    high_sum = lax.ppermute(sum_down, "y", ring(-1))
    scaled, inverse = scale_tokens(gen_hidden, modulation)
    return finish(own, (low_sum, low_near, high_near, high_sum), scaled, inverse, modulation, gain)


def solution(mesh):
    torus = Mesh(mesh.devices.reshape(2, 4, 2, 2, 4), ("zl", "x", "core", "zh", "y"))
    fsdp = ("zh", "y")
    in_specs = (
        P(fsdp, SEQ, None),
        P(fsdp, SEQ, None),
        P(fsdp, None, None),
        P(),
        P(None, None, fsdp),
    )
    return jax.shard_map(on_device, mesh=torus, in_specs=in_specs, out_specs=P(fsdp, SEQ, None), check_vma=False)
```

```python
import jax
import jax.numpy as jnp
from jax import lax
from jax.experimental import pallas as pl
from jax.experimental.pallas import tpu as pltpu
from jax.sharding import Mesh
from jax.sharding import PartitionSpec as P


HEAD_DIM = 128
WIDTH = 3072
BLOCK = 64
PIECE = 288
SHARED = 8 * PIECE
TAIL = (WIDTH - SHARED) // 2

norm_eps = 1e-06
match_eps = 0.05
loss_weight = 4.0


SEQ = ("zl", "x", "core")
ACROSS = [(0, 3), (3, 0), (1, 2), (2, 1)]


VMEM = pl.BlockSpec(memory_space=pltpu.VMEM)


def cost(flops, touched):
    return pl.CostEstimate(flops=flops, bytes_accessed=touched, transcendentals=0)


def limit(mib=24):
    return pltpu.CompilerParams(vmem_limit_bytes=mib * 1024 * 1024)


def ring(step):
    return [(i, (i + step) % 4) for i in range(4)]


def swap():
    return [(0, 1), (1, 0)]


def attention_kernel(x_ref, o_ref):
    bf = jnp.bfloat16
    f32 = jnp.float32
    length = 16 * BLOCK
    scale = HEAD_DIM ** (-0.5)
    to_two = scale * 1.4426950408889634

    def whole(stream, part):
        return x_ref[:, stream, part].reshape(length, HEAD_DIM)

    def dot(a, b):
        return jnp.dot(a, b, preferred_element_type=f32)

    def mix(stream):
        query, key, value = (whole(stream, part) for part in range(3))
        scores = dot(key, query.T)
        highest = jnp.max(scores, axis=0, keepdims=True)
        weights = jnp.exp2((scores - highest) * to_two)
        inverse = 1.0 / jnp.sum(weights, axis=0, keepdims=True)
        return dot(value.T, weights.astype(bf)) * inverse, weights, inverse

    real_out = mix(0)[0]
    fake_out, weights, inverse = mix(1)
    query, key, value = (whole(1, part) for part in range(3))
    differ = fake_out - real_out
    grad_out = (loss_weight * differ * lax.rsqrt(differ * differ + match_eps * match_eps)).astype(bf)
    deltas = jnp.sum(grad_out.astype(f32) * fake_out, axis=0, keepdims=True)
    probs = weights * inverse
    dscores = (probs * (dot(value, grad_out) - deltas)).astype(bf)

    def store(part, grad):
        o_ref[:, part] = grad.reshape(16, BLOCK, HEAD_DIM)

    store(0, (dot(key.T, dscores) * scale).astype(bf).T)
    store(1, (dot(dscores, query) * scale).astype(bf))
    store(2, dot(probs.astype(bf), grad_out.T).astype(bf))


def attention(received):
    return pl.pallas_call(
        attention_kernel,
        out_shape=jax.ShapeDtypeStruct((16, 3, BLOCK, HEAD_DIM), jnp.bfloat16),
        in_specs=[VMEM],
        out_specs=VMEM,
        cost_estimate=cost(11 * 1024 * 1024 * 256, 4 << 20),
        compiler_params=pltpu.CompilerParams(vmem_limit_bytes=36 << 20),
        name="attention",
    )(received)


HBM = pl.BlockSpec(memory_space=pltpu.HBM)
ANY = pl.BlockSpec(memory_space=pl.ANY)
SMEM = pl.BlockSpec(memory_space=pltpu.SMEM)
DMA = pltpu.SemaphoreType.DMA
COLUMNS = 2 * HEAD_DIM


def prepare_kernel(
    where_ref, real_ref, gen_ref, mod_ref, gain_ref, w_ref, sent_ref, tail_ref, oreal_ref, ofake_ref,
    real_buf, gen_buf, mod_buf, gain_buf, sems,
):
    f32, bf = jnp.float32, jnp.bfloat16
    place = pl.multiple_of(((where_ref[0] + 4) % 8) * PIECE, PIECE)
    tail = pl.multiple_of(SHARED + (where_ref[0] % 2) * TAIL, TAIL)
    copies = [
        pltpu.make_async_copy(gen_ref, gen_buf, sems.at[0]),
        pltpu.make_async_copy(real_ref, real_buf, sems.at[1]),
        pltpu.make_async_copy(mod_ref, mod_buf, sems.at[2]),
        pltpu.make_async_copy(gain_ref, gain_buf, sems.at[3]),
        pltpu.make_async_copy(w_ref.at[:, pl.ds(place, PIECE)], sent_ref, sems.at[4]),
        pltpu.make_async_copy(w_ref.at[:, pl.ds(tail, TAIL)], tail_ref, sems.at[5]),
    ]
    for copy in copies:
        copy.start()
    for copy in copies[:4]:
        copy.wait()
    gain = gain_buf[...]
    scale = 1.0 + mod_buf[0:1]
    shift = mod_buf[1:2]
    for r in range(0, BLOCK, 16):
        rows = slice(r, r + 16)
        fake = (gen_buf[rows].astype(f32) * scale + shift).astype(bf).astype(f32)
        for ref, values in ((oreal_ref, real_buf[rows].astype(f32)), (ofake_ref, fake)):
            inverse = lax.rsqrt(jnp.mean(values * values, axis=-1, keepdims=True) + norm_eps)
            ref[rows] = (values * inverse * gain).astype(bf)
    copies[4].wait()
    copies[5].wait()


def prepare(where, real, gen, modulation, gain, weight):
    bf, f32 = jnp.bfloat16, jnp.float32
    rows = jax.ShapeDtypeStruct((BLOCK, WIDTH), bf)
    return pl.pallas_call(
        prepare_kernel,
        out_shape=[jax.ShapeDtypeStruct((3, n, COLUMNS), bf) for n in (PIECE, TAIL)] + [rows, rows],
        in_specs=[SMEM] + [HBM] * 5,
        out_specs=[VMEM] * 4,
        scratch_shapes=[
            pltpu.VMEM((BLOCK, WIDTH), bf),
            pltpu.VMEM((BLOCK, WIDTH), bf),
            pltpu.VMEM((2, WIDTH), f32),
            pltpu.VMEM((1, WIDTH), f32),
            DMA((6,)),
        ],
        cost_estimate=cost(4 << 20, 3 << 20),
        compiler_params=limit(16),
        name="prepare",
    )(where, real, gen, modulation, gain, weight)


NEAR = (2, 3, 2, 3, BLOCK, HEAD_DIM)
SEND = (16, 2, 3, BLOCK, HEAD_DIM)


def load_kernel(w_ref, o_ref, sems):
    copies = [pltpu.make_async_copy(w_ref.at[q], o_ref.at[q], sems.at[q]) for q in range(3)]
    for copy in copies:
        copy.start()
    for copy in copies:
        copy.wait()


def load(weight):
    return pl.pallas_call(
        load_kernel,
        out_shape=jax.ShapeDtypeStruct((3, WIDTH, COLUMNS), jnp.bfloat16),
        in_specs=[HBM],
        out_specs=VMEM,
        scratch_shapes=[DMA((3,))],
        cost_estimate=cost(0, 9 << 20),
        compiler_params=limit(4),
        name="load",
    )(weight)


def near_kernel(*refs):
    row_refs, (w_ref, o_ref, rows_ref) = refs[:6], refs[6:]
    for i, ref in enumerate(row_refs):
        rows_ref[BLOCK * i : BLOCK * (i + 1)] = ref[...]
    for q in range(3):
        out = jnp.dot(rows_ref[: 6 * BLOCK], w_ref[q], preferred_element_type=jnp.float32).astype(jnp.bfloat16)
        for k in range(2):
            for j in range(3):
                for s in range(2):
                    r = (2 * j + s) * BLOCK
                    o_ref[k, j, s, q] = out[r : r + BLOCK, HEAD_DIM * k : HEAD_DIM * (k + 1)]


def project_near(rows, weight):
    return pl.pallas_call(
        near_kernel,
        out_shape=[
            jax.ShapeDtypeStruct(NEAR, jnp.bfloat16),
            jax.ShapeDtypeStruct((8 * BLOCK, WIDTH), jnp.bfloat16),
        ],
        in_specs=[VMEM] * 7,
        out_specs=[VMEM] * 2,
        cost_estimate=cost(2 * 384 * 3072 * 768, 7 << 20),
        compiler_params=limit(8),
        name="project_near",
    )(*rows, weight)


def pack_kernel(a_ref, b_ref, o_ref):
    o_ref[0] = a_ref[...]
    o_ref[1] = b_ref[...]


def pack(pieces):
    return pl.pallas_call(
        pack_kernel,
        out_shape=jax.ShapeDtypeStruct((2, 3, PIECE, COLUMNS), jnp.bfloat16),
        in_specs=[VMEM] * 2,
        out_specs=VMEM,
        cost_estimate=cost(0, 3 << 20),
        compiler_params=limit(4),
        name="pack",
    )(*pieces)


def in_vmem(x):
    return pltpu.with_memory_space_constraint(x, pltpu.VMEM)


def shared_rows(where, colour, own):
    half = where % 2 if own else 1 - where % 2
    return pl.ds(pl.multiple_of((((where // 2 + colour) % 4) * 2 + half) * PIECE, PIECE), PIECE)


def tail_rows(where, own):
    half = where % 2 if own else 1 - where % 2
    return pl.ds(pl.multiple_of(SHARED + half * TAIL, TAIL), TAIL)


def join_kernel(where_ref, *refs):
    pieces, o_ref = refs[:7], refs[7]
    where = where_ref[0]
    places = [shared_rows(where, c, True) for c in (0, 3, 1, 2)]
    places += [tail_rows(where, True), shared_rows(where, 0, False), tail_rows(where, False)]
    for place, piece in zip(places, pieces):
        o_ref[:, place] = piece[...]


def join(where, pieces):
    return pl.pallas_call(
        join_kernel,
        out_shape=jax.ShapeDtypeStruct((3, WIDTH, COLUMNS), jnp.bfloat16),
        in_specs=[SMEM] + [VMEM] * 7,
        out_specs=VMEM,
        cost_estimate=cost(0, 7 << 20),
        compiler_params=limit(4),
        name="join",
    )(where, *pieces)


def far_kernel(near_ref, rows_ref, real_ref, fake_ref, w_ref, o_ref, all_ref):
    del rows_ref
    bf, f32 = jnp.bfloat16, jnp.float32
    all_ref[6 * BLOCK : 7 * BLOCK] = real_ref[...]
    all_ref[7 * BLOCK :] = fake_ref[...]
    for k in range(2):
        for j in range(3):
            o_ref[4 * k + j] = near_ref[k, j]
    for q in range(3):
        out = jnp.dot(all_ref[6 * BLOCK :], w_ref[q], preferred_element_type=f32).astype(bf)
        for k in range(2):
            for s in range(2):
                o_ref[4 * k + 3, s, q] = out[BLOCK * s : BLOCK * (s + 1), HEAD_DIM * k : HEAD_DIM * (k + 1)]


def project_far(near, rows, far_real, far_fake, weight):
    bf = jnp.bfloat16
    return pl.pallas_call(
        far_kernel,
        out_shape=[jax.ShapeDtypeStruct((8, *SEND[1:]), bf), jax.ShapeDtypeStruct((8 * BLOCK, WIDTH), bf)],
        in_specs=[VMEM] * 5,
        out_specs=[VMEM] * 2,
        input_output_aliases={1: 1},
        cost_estimate=cost(2 * 128 * 3072 * 768, 10 << 20),
        compiler_params=limit(8),
        name="project_far",
    )(near, in_vmem(rows), far_real, far_fake, weight)


def rest_kernel(where_ref, half_ref, rows_ref, joined_ref, packed_ref, side_ref, o_ref, other_ref):
    del joined_ref
    bf, f32 = jnp.bfloat16, jnp.float32
    o_ref[:8] = half_ref[...]
    for q in range(3):
        for i, c in enumerate((3, 1)):
            other_ref[q, shared_rows(where_ref[0], c, False)] = packed_ref[i, q]
        other_ref[q, shared_rows(where_ref[0], 2, False)] = side_ref[q]
        out = jnp.dot(rows_ref[...], other_ref[q], preferred_element_type=f32).astype(bf)
        for k in range(2):
            for j in range(4):
                for s in range(2):
                    r = (2 * j + s) * BLOCK
                    o_ref[4 * (2 + k) + j, s, q] = out[r : r + BLOCK, HEAD_DIM * k : HEAD_DIM * (k + 1)]


def project_rest(where, half, rows, joined, packed, side):
    bf = jnp.bfloat16
    return pl.pallas_call(
        rest_kernel,
        out_shape=[jax.ShapeDtypeStruct(SEND, bf), jax.ShapeDtypeStruct((3, WIDTH, COLUMNS), bf)],
        in_specs=[SMEM] + [VMEM] * 5,
        out_specs=[VMEM] * 2,
        input_output_aliases={3: 1},
        cost_estimate=cost(2 * 512 * 3072 * 768, 14 << 20),
        compiler_params=limit(8),
        name="project_rest",
    )(where, half, rows, in_vmem(joined), in_vmem(packed), in_vmem(side))


CHUNK = 768


HALF_BLOCK = BLOCK // 2


def unproject_kernel(back_ref, own_ref, other_ref, own_out, below_ref, above_ref, *refs):
    far_up, far_down, near_up, near_down, grads_ref = refs
    bf, f32 = jnp.bfloat16, jnp.float32
    for p in range(2):
        for q in range(3):
            for k in range(2):
                d = 4 * (2 * p + k)
                c = ((3 * p + q) * 2 + k) * HEAD_DIM
                grads_ref[:, c : c + HEAD_DIM] = back_ref[d : d + 4, q].reshape(4 * BLOCK, HEAD_DIM)
    for n in range(0, WIDTH, CHUNK):
        total = None
        for p, ref in enumerate((own_ref, other_ref)):
            for q in range(3):
                c = (3 * p + q) * COLUMNS
                term = lax.dot_general(
                    grads_ref[:, c : c + COLUMNS],
                    ref[q, n : n + CHUNK],
                    (((1,), (1,)), ((), ())),
                    preferred_element_type=f32,
                )
                total = term if total is None else total + term
        columns = slice(n, n + CHUNK)
        parts = [total[HALF_BLOCK * i : HALF_BLOCK * (i + 1)] for i in range(8)]
        own_out[:, columns] = total[:BLOCK]
        near_down[:, columns] = parts[2].astype(bf)
        below_ref[:, columns] = parts[3]
        above_ref[:, columns] = parts[4]
        near_up[:, columns] = parts[5].astype(bf)
        far_up[:, columns] = parts[6].astype(bf)
        far_down[:, columns] = parts[7].astype(bf)


def unproject(back, weight, other):
    f32 = jnp.float32
    half = (HALF_BLOCK, WIDTH)
    return pl.pallas_call(
        unproject_kernel,
        out_shape=[jax.ShapeDtypeStruct((BLOCK, WIDTH), f32)]
        + [jax.ShapeDtypeStruct(half, f32)] * 2
        + [jax.ShapeDtypeStruct(half, jnp.bfloat16)] * 4,
        in_specs=[VMEM] * 3,
        out_specs=[VMEM] * 7,
        scratch_shapes=[pltpu.VMEM((4 * BLOCK, 12 * HEAD_DIM), jnp.bfloat16)],
        cost_estimate=cost(2 * 256 * 3072 * 1536, 12 << 20),
        compiler_params=limit(16),
        name="unproject",
    )(back, weight, other)


def pass_on_kernel(kept_ref, got_ref, o_ref):
    o_ref[...] = (kept_ref[...] + got_ref[...].astype(jnp.float32)).astype(jnp.bfloat16)


def pass_on(kept, got):
    return pl.pallas_call(
        pass_on_kernel,
        out_shape=jax.ShapeDtypeStruct((HALF_BLOCK, WIDTH), jnp.bfloat16),
        in_specs=[VMEM] * 2,
        out_specs=VMEM,
        cost_estimate=cost(1 << 17, 1 << 20),
        compiler_params=limit(8),
        name="pass_on",
    )(kept, got)


def scaled_kernel(gen_ref, mod_ref, o_ref, inverse_ref):
    f32, bf = jnp.float32, jnp.bfloat16
    scale = 1.0 + mod_ref[0:1]
    shift = mod_ref[1:2]
    for r in range(0, BLOCK, 16):
        rows = slice(r, r + 16)
        fake = (gen_ref[rows].astype(f32) * scale + shift).astype(bf).astype(f32)
        inverse = lax.rsqrt(jnp.mean(fake * fake, axis=-1, keepdims=True) + norm_eps)
        o_ref[rows] = fake * inverse
        inverse_ref[rows] = jnp.broadcast_to(inverse, (16, HEAD_DIM))


def scale_tokens(gen, modulation):
    f32 = jnp.float32
    return pl.pallas_call(
        scaled_kernel,
        out_shape=[jax.ShapeDtypeStruct((BLOCK, WIDTH), f32), jax.ShapeDtypeStruct((BLOCK, HEAD_DIM), f32)],
        in_specs=[VMEM] * 2,
        out_specs=[VMEM] * 2,
        cost_estimate=cost(2 << 20, 2 << 20),
        compiler_params=limit(8),
        name="scale_tokens",
    )(gen, modulation)


def finish_kernel(own_ref, a_ref, b_ref, c_ref, d_ref, scaled_ref, inverse_ref, mod_ref, gain_ref, o_ref):
    f32, bf = jnp.float32, jnp.bfloat16
    gain = gain_ref[...]
    scale = 1.0 + mod_ref[0:1]
    for r in range(0, BLOCK, 16):
        rows = slice(r, r + 16)
        scaled = scaled_ref[rows]
        one, two = (a_ref, b_ref) if r < HALF_BLOCK else (c_ref, d_ref)
        part = slice(r % HALF_BLOCK, r % HALF_BLOCK + 16)
        grad = own_ref[rows] + one[part].astype(f32) + two[part].astype(f32)
        grad = grad * gain
        grad = inverse_ref[rows, 0:1] * (grad - scaled * jnp.mean(grad * scaled, axis=-1, keepdims=True))
        o_ref[rows] = (grad * scale).astype(bf)


def finish(own, parts, scaled, inverse, modulation, gain):
    return pl.pallas_call(
        finish_kernel,
        out_shape=jax.ShapeDtypeStruct((BLOCK, WIDTH), jnp.bfloat16),
        in_specs=[VMEM] * 9,
        out_specs=VMEM,
        cost_estimate=cost(4 << 20, 3 << 20),
        compiler_params=limit(8),
        name="finish",
    )(own, *parts, scaled, inverse, modulation, gain)


def on_device(real_tokens, gen_hidden, modulation, norm_gain, weight):
    return step(real_tokens[0], gen_hidden[0], modulation[0], norm_gain[None], weight)[None]


def in_hbm(x):
    return pltpu.with_memory_space_constraint(x, pltpu.HBM)


def step(real_tokens, gen_hidden, modulation, gain, weight):
    colour = (lax.axis_index("x") + 2 * lax.axis_index("zl")) % 4
    core = lax.axis_index("core")

    where = (colour * 2 + core).astype(jnp.int32)[None]
    sent, sent_tail, real, fake = prepare(
        where, in_hbm(real_tokens), in_hbm(gen_hidden), in_hbm(modulation), in_hbm(gain), in_hbm(weight)
    )
    mine = lax.ppermute(sent, ("zl", "zh"), ACROSS)
    tail = lax.ppermute(sent_tail, ("zl", "zh"), ACROSS)
    below_real = lax.ppermute(real, "y", ring(1))
    above_fake = lax.ppermute(fake, "y", ring(-1))
    below_fake = lax.ppermute(fake, "y", ring(1))
    above_real = lax.ppermute(real, "y", ring(-1))
    far_real = lax.ppermute(below_real, "y", ring(1))
    far_fake = lax.ppermute(above_fake, "y", ring(-1))
    left = lax.ppermute(mine, "x", ring(1))
    right = lax.ppermute(mine, "x", ring(-1))
    side = lax.ppermute(mine, "zl", swap())
    partner_mine = lax.ppermute(mine, "core", swap())
    held = load(in_hbm(weight))
    near, near_rows = project_near([real, fake, below_real, below_fake, above_real, above_fake], held)
    partner_tail = lax.ppermute(tail, "core", swap())
    packed = pack([left, right])
    packed = lax.ppermute(packed, "core", swap())
    partner_side = lax.ppermute(side, "core", swap())
    half, rows = project_far(near, near_rows, far_real, far_fake, held)
    joined = join(where, [mine, left, right, side, tail, partner_mine, partner_tail])
    send, other = project_rest(where, half, rows, joined, packed, partner_side)
    received = lax.all_to_all(send.reshape(16, 6 * BLOCK, HEAD_DIM), SEQ, split_axis=0, concat_axis=0, tiled=True)
    grads = attention(received.reshape(SEND))
    back = lax.all_to_all(grads.reshape(16, 3 * BLOCK, HEAD_DIM), SEQ, split_axis=0, concat_axis=0, tiled=True)
    own, below, above, far_up, far_down, near_up, near_down = unproject(
        back.reshape(16, 3, BLOCK, HEAD_DIM), held, other
    )
    got_up = lax.ppermute(far_up, "y", ring(1))
    got_down = lax.ppermute(far_down, "y", ring(-1))
    low_near = lax.ppermute(near_down, "y", ring(-1))
    high_near = lax.ppermute(near_up, "y", ring(1))
    sum_up = pass_on(above, got_up)
    sum_down = pass_on(below, got_down)
    low_sum = lax.ppermute(sum_up, "y", ring(1))
    high_sum = lax.ppermute(sum_down, "y", ring(-1))
    scaled, inverse = scale_tokens(gen_hidden, modulation)
    return finish(own, (low_sum, low_near, high_near, high_sum), scaled, inverse, modulation, gain)


def solution(mesh):
    torus = Mesh(mesh.devices.reshape(2, 4, 2, 2, 4), ("zl", "x", "core", "zh", "y"))
    fsdp = ("zh", "y")
    in_specs = (
        P(fsdp, SEQ, None),
        P(fsdp, SEQ, None),
        P(fsdp, None, None),
        P(),
        P(None, None, fsdp),
    )
    return jax.shard_map(on_device, mesh=torus, in_specs=in_specs, out_specs=P(fsdp, SEQ, None), check_vma=False)
```
